512 devices in a mesh: section: 8 (over y_hi, x), ctx: 64 (over y_lo, z, core).
Axes of the slice: x: 4, y: 8 (y_hi: 2, y_lo: 4; y = y_hi * 4 + y_lo), z: 8, core: 2. Of those that a mesh axis runs over, the one named last changes fastest.
Arguments:
- inputs: bfloat16 [8192, 2048], P('ctx', 'section'), may hold values from -8 to 8
- out_grads: bfloat16 [8192, 2048], P('ctx', 'section'), may hold values from -6 to 6
- conv_weight: float32 [3, 4, 2048], P(None, None, 'section'), may hold values from -3 to 3
- log_decay: float32 [8192, 2048], P('ctx', 'section'), may hold values from -1 to 0
- beta: float32 [8192, 16], P('ctx', 'section'), may hold values from 0 to 1
Outputs:
- stream_out: bfloat16 [8192, 2048], P('ctx', 'section')
- input_grad: bfloat16 [8192, 2048], P('ctx', 'section')
The draws below stay inside these ranges and needn't reach their ends.
All inputs are finite; a program needn't handle non-finite values.
Results may differ from the reference program's by a relative error of at most 0.001.
Values sent between devices are 32-bit elements; how exact they have to be, the bound alone decides.
A program may use at most 128 MiB of HBM per device.

```python
import math
import jax
import jax.numpy as jnp
from jax import lax

HEADS = 16
HEAD_DIM = 128
KERNEL = 4
TOK_DEV = 128
CHANNELS = 2048
TOKENS = 8192


def head_kinds(key):
    base = jax.random.fold_in(key, 11)
    share = 0.5
    return jax.random.uniform(base, (HEADS,)) < share


def draw_inputs(key, part):
    keys_all = jax.random.split(jax.random.fold_in(key, 41), 1)
    position = jnp.arange(CHANNELS).astype(jnp.float32) / CHANNELS
    rise = jnp.exp(0.5 * math.log(4.0) * position)
    values = jax.random.normal(keys_all[0], (TOKENS, CHANNELS), jnp.float32) * rise[None, :]
    return jnp.clip(values, -8.0, 8.0).astype(jnp.bfloat16)


def draw_log_decay(key, part):
    slow_factor = head_kinds(key)
    keys_all = jax.random.split(jax.random.fold_in(key, 23), 6)
    shape_rate = (1, HEADS, HEAD_DIM)
    slow_rate = math.log(10.0) / TOKENS * jnp.exp(jax.random.uniform(keys_all[0], shape_rate, jnp.float32, math.log(0.02), math.log(0.3)))
    fast_rate = jnp.exp(jax.random.uniform(keys_all[1], shape_rate, jnp.float32, math.log(1.0 / 50.0), math.log(1.0 / 20.0)))
    learning_rate = jnp.where(slow_factor[None, :, None], slow_rate, fast_rate)
    random_noise = jax.random.uniform(keys_all[2], (TOKENS, HEADS, HEAD_DIM), jnp.float32, 0.5, 1.5)
    block_count = TOKENS // TOK_DEV
    block_scale = jnp.exp(jax.random.uniform(keys_all[3], (block_count, 1, HEADS, 1), jnp.float32, math.log(0.5), math.log(2.0)))
    random_noise = (random_noise.reshape(block_count, TOK_DEV, HEADS, HEAD_DIM) * block_scale).reshape(TOKENS, HEADS, HEAD_DIM)
    spots = jax.random.randint(keys_all[4], (4,), 0, TOKENS)
    match_flag = jnp.any(jnp.arange(TOKENS)[:, None] == spots[None, :], axis=-1)
    stack_depth = jax.random.uniform(keys_all[5], (TOKENS, HEADS, 1), jnp.float32, 0.2, 0.5)
    spike_factor = jnp.where(match_flag[:, None, None] & slow_factor[None, :, None], jnp.log(1.0 - stack_depth), 0.0)
    final_result = -learning_rate * random_noise + spike_factor
    return final_result.reshape(TOKENS, HEADS * HEAD_DIM).astype(jnp.float32)


def draw_beta(key, part):
    slow_factor = head_kinds(key)
    keys_all = jax.random.split(jax.random.fold_in(key, 31), 2)
    limit = min(0.9, HEAD_DIM * math.log(10.0) / TOKENS)
    slow_beta = jax.random.uniform(keys_all[0], (TOKENS, HEADS), jnp.float32, 0.2, 1.0) * limit
    fast_beta = jax.random.uniform(keys_all[1], (TOKENS, HEADS), jnp.float32, 0.2, 0.9)
    return jnp.where(slow_factor[None, :], slow_beta, fast_beta).astype(jnp.float32)


def steps_of(rng, shape, cuts, smallest, high):
    gain = 1.0
    for axis_at, shards_of in cuts:
        draws = jax.random.uniform(jax.random.fold_in(jax.random.fold_in(rng, 6), axis_at), (shards_of,), jnp.float32, smallest / len(cuts), high / len(cuts))
        gain = gain * jnp.repeat(jnp.exp(draws), shape[axis_at] // shards_of).reshape((-1,) + (1,) * (len(shape) - 1 - axis_at))
    return gain


def bell_draw(own_key, shape, deviation, bound, pieces=(), kind=jnp.bfloat16):
    drawn = jax.random.normal(own_key, shape, jnp.float32) * deviation
    if len(pieces) > 0:
        drawn = steps_of(own_key, shape, pieces, -0.22, 0.18) * drawn
    return jnp.clip(drawn, min=-bound, max=bound).astype(kind)


def setup_inputs(seed: int = 0) -> dict:
    seeds = jax.random.split(jax.random.key(seed), 6)
    return {
        "inputs": draw_inputs(jax.random.fold_in(seeds[5], 71), 0),
        "out_grads": bell_draw(seeds[1], (TOKENS, CHANNELS), 1.0, 6.0, ((0, 64), (1, 8))),
        "conv_weight": bell_draw(seeds[2], (3, KERNEL, CHANNELS), KERNEL ** -0.5, 3.0, ((2, 8),), jnp.float32),
        "log_decay": draw_log_decay(jax.random.fold_in(seeds[5], 71), 0),
        "beta": draw_beta(jax.random.fold_in(seeds[5], 71), 0),
    }


epsilon = 1e-06
norm_eps = 1e-05
highest = lax.Precision.HIGHEST

def unit_rows(mixed):
    act = jax.nn.silu(mixed).reshape(mixed.shape[0], -1, HEAD_DIM)
    return act / jnp.sqrt(lax.optimization_barrier(jnp.sum(act * act, axis=-1, keepdims=True)) + epsilon)

def features(padded, kern):
    taps_count = kern.shape[1]
    length = padded.shape[0] - taps_count + 1
    mixes = [sum((kern[j, i] * padded[i:i + length] for i in range(taps_count))) for j in range(3)]
    queries = unit_rows(mixes[0])
    keys = unit_rows(mixes[1])
    values = jax.nn.silu(mixes[2]).reshape(length, -1, HEAD_DIM)
    return (queries, keys, values)

def solve_block(keys, values, cumulative, rates):
    length = keys.shape[0]
    middle = cumulative[length // 2]
    key_fwd = keys * jnp.exp(cumulative - middle)
    key_back = keys * jnp.exp(middle - cumulative)
    products = jnp.einsum('thc,shc->hts', key_fwd, key_back, precision=highest)
    strict_mask = jnp.tril(jnp.ones((length, length), jnp.float32), -1)
    rate_col = jnp.swapaxes(rates, 0, 1)[:, :, None]
    system = jnp.eye(length, dtype=jnp.float32) + rate_col * products * strict_mask
    rhs_keys = rate_col * jnp.swapaxes(keys * jnp.exp(cumulative), 0, 1)
    rhs_values = rate_col * jnp.swapaxes(values, 0, 1)
    solved = lax.linalg.triangular_solve(system, jnp.concatenate([rhs_keys, rhs_values], axis=-1), left_side=True, lower=True, unit_diagonal=True)
    return (solved[..., :HEAD_DIM], solved[..., HEAD_DIM:])

def transition(keys, cumulative, w_rows, u_rows):
    final_decay = cumulative[-1]
    key_end = keys * jnp.exp(final_decay - cumulative)
    retained = jnp.exp(final_decay)[:, :, None] * jnp.eye(HEAD_DIM, dtype=jnp.float32)
    transit = retained - jnp.einsum('thd,hte->hde', key_end, w_rows, precision=highest)
    inject = jnp.einsum('thd,hte->hde', key_end, u_rows, precision=highest)
    return (transit, inject)

def block_out(queries, keys, cumulative, w_rows, u_rows, start):
    length = queries.shape[0]
    middle = cumulative[length // 2]
    query_fwd = queries * jnp.exp(cumulative - middle)
    key_back = keys * jnp.exp(middle - cumulative)
    full_mask = jnp.tril(jnp.ones((length, length), jnp.float32))
    scores = jnp.einsum('thc,shc->hts', query_fwd, key_back, precision=highest) * full_mask
    fresh = u_rows - jnp.einsum('htd,hde->hte', w_rows, start, precision=highest)
    output = jnp.einsum('thd,hde->the', queries * jnp.exp(cumulative), start, precision=highest)
    output = output + jnp.einsum('hts,hse->the', scores, fresh, precision=highest)
    return output.reshape(length, -1)

def layer(stream_in, kern, decay, rates):
    stream = stream_in.astype(jnp.float32)
    scale = 1.0 / jnp.sqrt(lax.optimization_barrier(jnp.mean(stream * stream, axis=1, keepdims=True)) + norm_eps)
    normed = stream * scale
    padded = jnp.concatenate([jnp.zeros((KERNEL - 1, stream.shape[1]), jnp.float32), normed], axis=0)
    queries, keys, values = features(padded, kern)
    blocks = TOKENS // TOK_DEV
    parts = (queries.reshape(blocks, TOK_DEV, HEADS, HEAD_DIM), keys.reshape(blocks, TOK_DEV, HEADS, HEAD_DIM), values.reshape(blocks, TOK_DEV, HEADS, HEAD_DIM), decay.reshape(blocks, TOK_DEV, HEADS, HEAD_DIM), rates.reshape(blocks, TOK_DEV, HEADS))

    def advance(state, piece):
        query_b, key_b, value_b, decay_b, rate_b = piece
        cumulative = jnp.cumsum(decay_b, axis=0)
        w_rows, u_rows = solve_block(key_b, value_b, cumulative, rate_b)
        transit, inject = transition(key_b, cumulative, w_rows, u_rows)
        output = block_out(query_b, key_b, cumulative, w_rows, u_rows, state)
        following = jnp.einsum('hde,hef->hdf', transit, state, precision=highest) + inject
        return (following, output)
    initial = jnp.zeros((HEADS, HEAD_DIM, HEAD_DIM), jnp.float32)
    _, outputs = lax.scan(advance, initial, parts)
    return (stream + outputs.reshape(TOKENS, -1)).astype(jnp.bfloat16)

def reference(inputs, out_grads, conv_weight, log_decay, beta):
    stream_out, pull = jax.vjp(lambda a: layer(a, conv_weight, log_decay, beta), inputs)
    input_grad = pull(out_grads)[0].astype(jnp.bfloat16)
    return (stream_out, input_grad)
```

```python
import functools

import jax
import jax.numpy as jnp
from jax import lax
from jax.experimental import pallas as pl
from jax.experimental.pallas import tpu as pltpu
from jax.sharding import PartitionSpec as P

MESH = pl.DeviceIdType.MESH
D = 128
F32 = jnp.float32
BF16 = jnp.bfloat16


def split2(a):
    high = a.astype(BF16)
    low = (a - high.astype(F32)).astype(BF16)
    return high, low


def raw_dot(a, b, ca, cb):
    return lax.dot_general(a, b, (((ca,), (cb,)), ((), ())), preferred_element_type=F32)


def mm(a, b, ca=1, cb=0):
    ah, al = split2(a)
    bh, bl = split2(b)
    return raw_dot(ah, bh, ca, cb) + (raw_dot(ah, bl, ca, cb) + raw_dot(al, bh, ca, cb))


def mm_nt(a, b):
    return mm(a, b, 1, 1)


def mm_tn(a, b):
    return mm(a, b, 0, 0)


def iota2(shape, axis):
    return lax.broadcasted_iota(jnp.int32, shape, axis)


def row_sums(values):
    high, low = split2(values)
    ones = jnp.ones((8, values.shape[1]), BF16)
    return raw_dot(ones, high, 1, 1) + raw_dot(ones, low, 1, 1)


def as_columns(tile):
    return jnp.transpose(jnp.broadcast_to(tile[0:1], (D, D)))


def unit_lower_inverse(strict_parts):
    r, c = iota2((D, D), 0), iota2((D, D), 1)
    eye = jnp.where(r == c, 1.0, 0.0).astype(F32)
    inverse = None
    for k in range(7):
        mask = ((r >> (k + 1)) == (c >> (k + 1))) & (((r >> k) & 1) == 1) & (((c >> k) & 1) == 0)
        off = [jnp.where(mask, a, 0.0) for a in strict_parts]
        if k == 0:
            inverse = [eye - o for o in off]
        else:
            half = [mm(m, o) for m, o in zip(inverse, off)]
            inverse = [m - mm(h, m) for h, m in zip(half, inverse)]
    return inverse


def kernel(geom, x_ref, do_ref, g_ref, beta_ref, w_ref, out_ref, dx_ref, *scratch):
    sections, n_y, n_z, width_all = geom
    (
        SB, XB, R, R2, TB, NP, RIM, RIMB, SC,
        QK, DS, EX, FB, WQ, UO, ZK, MAPS, TS, VS, VR, YB, SO, ST, DM, OB, OR, GB, GR,
        row_s, row_r, row2_s, row2_r, one_s, one_r, ring_s, ring_r, vec_s, vec_r, back_s, back_r,
    ) = scratch
    n_ctx = n_y * n_z * 2
    cols = D // n_z
    sec = lax.axis_index("section")
    ctx = lax.axis_index("ctx")
    core = lax.rem(ctx, 2)
    chip = ctx // 2
    y = chip // n_z
    z = lax.rem(chip, n_z)
    partner = ctx + 1 - 2 * core
    after = lax.rem(ctx + 2, n_ctx)
    before = lax.rem(ctx + n_ctx - 2, n_ctx)

    def at_z(zz):
        return y * (2 * n_z) + zz * 2 + core

    def at_y(yy):
        return yy * (2 * n_z) + z * 2 + core

    def copy_to(src, dst, ss, rs, to_sec, to_ctx):
        return pltpu.make_async_remote_copy(
            src_ref=src, dst_ref=dst, send_sem=ss, recv_sem=rs,
            device_id=(to_sec, to_ctx), device_id_type=MESH,
        )

    peers = [(ds, dc) for ds in range(sections) for dc in range(2) if ds or dc]

    barrier = pltpu.get_barrier_semaphore()

    def greet(to_sec, to_ctx):
        pl.semaphore_signal(barrier, inc=1, device_id=(to_sec, to_ctx), device_id_type=MESH)

    for ds, dc in peers:
        greet(lax.rem(sec + ds, sections), partner if dc else ctx)
    for dz in range(1, n_z):
        greet(sec, at_z(lax.rem(z + dz, n_z)))
    for dy in range(1, n_y):
        greet(sec, at_y(lax.rem(y + dy, n_y)))
    greet(sec, after)
    greet(sec, before)
    greeted = len(peers) + n_z - 1 + n_y - 1 + 2

    first = core == 0

    def halves(ref):
        whole = ref[...].astype(F32)
        low, high = whole[:, :D], whole[:, D:]
        return jnp.where(first, low, high), jnp.where(first, high, low), whole

    x_own, x_oth, x_all = halves(x_ref)
    d_own, d_oth, _ = halves(do_ref)
    g_own, g_oth, _ = halves(g_ref)
    b0 = jnp.broadcast_to(beta_ref[:, 0:1], (D, D))
    b1 = jnp.broadcast_to(beta_ref[:, 1:2], (D, D))
    SB[0] = x_oth
    SB[1] = d_oth
    SB[2] = g_oth
    SB[3] = jnp.where(first, b1, b0)
    XB[core, 0] = x_own
    XB[core, 1] = d_own
    XB[core, 2] = g_own
    XB[core, 3] = jnp.where(first, b0, b1)
    R[0] = row_sums(x_all * x_all)
    pl.semaphore_wait(barrier, greeted)

    row_copies = []
    for ds, dc in peers:
        back = ((sections - ds) % sections) * 2 + dc
        copy = copy_to(R.at[0], R.at[back], row_s.at[ds * 2 + dc], row_r.at[back],
                       lax.rem(sec + ds, sections), partner if dc else ctx)
        copy.start()
        row_copies.append(copy)
    swap = copy_to(SB, XB.at[core], one_s.at[0], one_r.at[0], sec, partner)
    swap.start()

    def rows_wait(buf, ss, rs):
        for ds, dc in peers:
            slot = ds * 2 + dc
            copy_to(buf.at[slot], buf.at[slot], ss.at[slot], rs.at[slot], sec, ctx).wait_recv()

    rows_wait(R, row_s, row_r)
    same = R[0]
    other = R[1]
    for ds in range(1, sections):
        same = same + R[2 * ds]
        other = other + R[2 * ds + 1]
    scale_same = 1.0 / jnp.sqrt(same / width_all + 1e-5)
    scale_other = 1.0 / jnp.sqrt(other / width_all + 1e-5)
    SC[core] = as_columns(scale_same)
    SC[1 - core] = as_columns(scale_other)
    copy_to(SB, XB.at[1 - core], one_s.at[0], one_r.at[0], sec, partner).wait_recv()

    for b in range(2):
        NP[8 + D * b : 8 + D * (b + 1), :] = XB[b, 0] * SC[b]
    rim = copy_to(NP.at[pl.ds(2 * D, 8)], RIM, one_s.at[1], one_r.at[1], sec, after)
    rim.start()

    r, c = iota2((D, D), 0), iota2((D, D), 1)
    incl = r >= c
    strict = r > c
    lower = jnp.where(incl, 1.0, 0.0).astype(BF16)
    fins = []
    for b in range(2):
        g = XB[b, 2]
        gh = g.astype(BF16)
        rest = g - gh.astype(F32)
        gm = rest.astype(BF16)
        gl = (rest - gm.astype(F32)).astype(BF16)
        cum = raw_dot(lower, gh, 1, 0) + (raw_dot(lower, gm, 1, 0) + raw_dot(lower, gl, 1, 0))
        mid = cum[D // 2 : D // 2 + 1]
        fin = cum[D - 1 : D]
        EX[b, 0] = jnp.exp(cum - mid)
        EX[b, 1] = jnp.exp(mid - cum)
        EX[b, 2] = jnp.exp(cum)
        EX[b, 3] = jnp.exp(fin - cum)
        fins.append(fin)

    copy_to(NP.at[pl.ds(2 * D, 8)], RIM, one_s.at[1], one_r.at[1], sec, before).wait_recv()
    NP[0:8, :] = jnp.where(chip == 0, 0.0, RIM[...])

    def tap(j, i):
        both = w_ref[j, i : i + 1, :]
        return jnp.where(first, both[:, :D], both[:, D:])

    taps = [[tap(j, i) for i in range(4)] for j in range(3)]
    shifted = [NP[5 + i : 5 + i + 2 * D, :] for i in range(4)]
    for j in range(3):
        mix = taps[j][0] * shifted[0]
        for i in range(1, 4):
            mix = mix + taps[j][i] * shifted[i]
        gate = 1.0 / (1.0 + jnp.exp(-mix))
        act = mix * gate
        slope = gate * (1.0 + mix * (1.0 - gate))
        if j < 2:
            norm = 1.0 / jnp.sqrt(jnp.sum(act * act, axis=1, keepdims=True) + 1e-6)
            QK[j] = act * norm
            DS[j] = slope * norm
        else:
            QK[j] = act
            DS[j] = slope

    blk = [slice(D * b, D * (b + 1)) for b in range(2)]
    systems, scores = [], []
    for b in range(2):
        q, k = QK[0, blk[b], :], QK[1, blk[b], :]
        kf, kb, qf = k * EX[b, 0], k * EX[b, 1], q * EX[b, 0]
        FB[b, 0:D, :] = kf
        FB[b, D : 2 * D, :] = qf
        FB[b, 2 * D : 3 * D, :] = kb
        both = mm_nt(jnp.concatenate([kf, qf], axis=0), kb)
        systems.append(jnp.where(strict, XB[b, 3] * both[:D], 0.0))
        scores.append(jnp.where(incl, both[D:], 0.0))
    inverses = unit_lower_inverse(systems)
    for b in range(2):
        q, k, v = QK[0, blk[b], :], QK[1, blk[b], :], QK[2, blk[b], :]
        beta, d_out, inv, sc = XB[b, 3], XB[b, 1], inverses[b], scores[b]
        ke, qc = k * EX[b, 3], q * EX[b, 2]
        wu = mm(inv, jnp.concatenate([beta * k * EX[b, 2], beta * v], axis=1))
        w, u = wu[:, :D], wu[:, D:]
        swu = mm(sc, wu)
        qeff = qc - swu[:, :D]
        WQ[b, 0:D, :] = w
        WQ[b, D : 2 * D, :] = qeff
        UO[b, 0] = u
        UO[b, 1] = swu[:, D:]
        MAPS[b, 0] = jnp.where(r == c, jnp.exp(fins[b]), 0.0) - mm_tn(ke, w)
        MAPS[b, 1] = mm_tn(u, ke)
        MAPS[b, 2] = mm_tn(d_out, qeff)
        h = mm_tn(sc, d_out)
        zk = mm_tn(inv, jnp.concatenate([h, ke], axis=1))
        ZK[b, 0] = zk[:, :D]
        ZK[b, 1] = zk[:, D:]

    t0, t1 = MAPS[0, 0], MAPS[1, 0]
    t_pair = mm(t1, t0)
    i_pair = mm_nt(MAPS[0, 1], t1) + MAPS[1, 1]
    s_pair = MAPS[0, 2] + mm(MAPS[1, 2], t0)
    TS[z] = t_pair
    for zz in range(n_z):
        VS[zz, 0:cols, :] = i_pair[zz * cols : (zz + 1) * cols]
        VS[zz, cols : 2 * cols, :] = s_pair[zz * cols : (zz + 1) * cols]
    VR[z] = VS[z]

    up_hops, down_hops = n_z // 2, n_z - 1 - n_z // 2

    def ring_copy(direction, hop):
        source = lax.rem(z + n_z - (hop - 1) if direction == 0 else z + hop - 1, n_z)
        target = lax.rem(z + 1 if direction == 0 else z + n_z - 1, n_z)
        slot = direction * up_hops + hop - 1
        return copy_to(TS.at[source], TS.at[source], ring_s.at[slot], ring_r.at[slot], sec, at_z(target))

    def ring_recv(direction, hop):
        source = lax.rem(z + n_z - hop if direction == 0 else z + hop, n_z)
        slot = direction * up_hops + hop - 1
        copy_to(TS.at[source], TS.at[source], ring_s.at[slot], ring_r.at[slot], sec, ctx).wait_recv()

    sent = []

    def go(copy):
        copy.start()
        sent.append(copy)

    go(ring_copy(0, 1))
    if down_hops:
        go(ring_copy(1, 1))
    for dz in range(1, n_z):
        to = lax.rem(z + dz, n_z)
        go(copy_to(VS.at[to], VR.at[z], vec_s.at[dz], vec_r.at[n_z - dz], sec, at_z(to)))
    for hop in range(1, up_hops + 1):
        ring_recv(0, hop)
        if hop < up_hops:
            go(ring_copy(0, hop + 1))
        if hop <= down_hops:
            ring_recv(1, hop)
            if hop < down_hops:
                go(ring_copy(1, hop + 1))
    for dz in range(1, n_z):
        src = lax.rem(z + dz, n_z)
        copy_to(VS.at[src], VR.at[src], vec_s.at[dz], vec_r.at[dz], sec, ctx).wait_recv()

    stack = jnp.concatenate([VR[0, 0:cols, :], jnp.transpose(TS[0])], axis=0)
    down = VR[n_z - 1, cols : 2 * cols, :]
    zero_map = jnp.zeros((D, D), F32)
    for step in range(1, n_z):
        zu, zd = step, n_z - 1 - step
        stack = mm_nt(stack, TS[zu]) + jnp.concatenate([VR[zu, 0:cols, :], zero_map], axis=0)
        down = mm(down, TS[zd]) + VR[zd, cols : 2 * cols, :]
    up, total = stack[:cols], stack[cols:]

    YB[0] = jnp.zeros((cols, D), F32)
    YB[1] = jnp.zeros((cols, D), F32)
    YB[2] = up
    YB[3] = down
    YB[4:4 + n_z, :, :] = total.reshape(n_z, cols, D)
    up_y = lax.rem(y + 1, n_y)
    down_y = lax.rem(y + n_y - 1, n_y)
    chain_up = copy_to(YB.at[2], SO.at[0, 0], one_s.at[2], one_r.at[2], sec, at_y(up_y))
    chain_down = copy_to(YB.at[3], SO.at[0, 1], one_s.at[3], one_r.at[3], sec, at_y(down_y))

    @pl.when(y > 0)
    def _():
        chain_up.wait_recv()
        arrived = SO[0, 0]
        YB[0] = arrived
        YB[2] = YB[2] + mm(arrived, YB[4:4 + n_z, :, :].reshape(D, D))

    @pl.when(y < n_y - 1)
    def _():
        chain_up.start()

    @pl.when(y < n_y - 1)
    def _():
        chain_down.wait_recv()
        arrived = SO[0, 1]
        YB[1] = arrived
        YB[3] = YB[3] + mm_nt(arrived, YB[4:4 + n_z, :, :].reshape(D, D))

    @pl.when(y > 0)
    def _():
        chain_down.start()

    up, down = YB[0], YB[1]

    def back_copy(zz, kind, to):
        slot = zz * 2 + kind
        return copy_to(SO.at[1 + zz, kind], ST.at[kind, pl.ds(pl.multiple_of(z * cols, cols), cols)],
                       back_s.at[slot], back_r.at[z * 2 + kind], sec, at_z(to))

    for step in range(n_z):
        zu, zd = step, n_z - 1 - step
        SO[1 + zu, 0] = up
        SO[1 + zd, 1] = down
        for zz, kind in ((zu, 0), (zd, 1)):
            @pl.when(z != zz)
            def _():
                back_copy(zz, kind, zz).start()

            @pl.when(z == zz)
            def _():
                ST[kind, zz * cols : (zz + 1) * cols, :] = SO[1 + zz, kind]
        if step < n_z - 1:
            up = mm_nt(up, TS[zu]) + VR[zu, 0:cols, :]
            down = mm(down, TS[zd]) + VR[zd, cols : 2 * cols, :]
    for dz in range(1, n_z):
        src = lax.rem(z + dz, n_z)
        for kind in range(2):
            copy_to(SO.at[1, kind], ST.at[kind, pl.ds(pl.multiple_of(src * cols, cols), cols)],
                    back_s.at[0], back_r.at[src * 2 + kind], sec, ctx).wait_recv()

    starts = [ST[0], None]
    ends = [None, ST[1]]
    starts[1] = mm_nt(starts[0], t0) + MAPS[0, 1]
    ends[0] = mm(ends[1], t1) + MAPS[1, 2]
    DM[:, 0:8, :] = jnp.zeros((3, 8, D), F32)
    DM[:, 8 + 2 * D :, :] = jnp.zeros((3, 8, D), F32)
    for b in range(2):
        q, k = QK[0, blk[b], :], QK[1, blk[b], :]
        beta, d_out = XB[b, 3], XB[b, 1]
        wq = mm_nt(WQ[b], starts[b])
        fresh = UO[b, 0] - wq[:D]
        OB[b] = UO[b, 1] + wq[D:]
        zeta = ZK[b, 0] + mm_nt(ZK[b, 1], ends[b])
        pair = mm_nt(jnp.concatenate([d_out, zeta], axis=0), fresh)
        d_sc = jnp.where(incl, pair[:D], 0.0)
        d_p = beta * jnp.where(strict, -pair[D:], 0.0)
        dz_s = mm(jnp.concatenate([d_out, zeta], axis=0), starts[b])
        f_g = mm(fresh, ends[b])
        by_kb = mm(jnp.concatenate([d_sc, d_p], axis=0), FB[b, 2 * D : 3 * D, :])
        d_kb = mm_tn(jnp.concatenate([d_p, d_sc], axis=0), FB[b, 0 : 2 * D, :])
        dq = EX[b, 2] * dz_s[:D] + EX[b, 0] * by_kb[:D]
        dk = EX[b, 3] * f_g - beta * EX[b, 2] * dz_s[D:] + EX[b, 0] * by_kb[D:] + EX[b, 1] * d_kb
        for j, (unit, grad) in enumerate(((q, dq), (k, dk))):
            along = jnp.sum(unit * grad, axis=1, keepdims=True)
            DM[j, 8 + D * b : 8 + D * (b + 1), :] = (grad - unit * along) * DS[j, blk[b], :]
        DM[2, 8 + D * b : 8 + D * (b + 1), :] = beta * zeta * DS[2, blk[b], :]
    out_swap = copy_to(OB.at[1 - core], OR, one_s.at[4], one_r.at[4], sec, partner)
    out_swap.start()

    d_norm = jnp.zeros((2 * D + 8, D), F32)
    for j in range(3):
        for i in range(4):
            d_norm = d_norm + taps[j][i] * DM[j, 3 - i : 3 - i + 2 * D + 8, :]
    RIMB[0] = d_norm[:8]
    rim_back = copy_to(RIMB.at[0], RIMB.at[1], one_s.at[5], one_r.at[5], sec, before)
    rim_back.start()
    GB[0] = d_norm[8 : 8 + D]
    GB[1] = d_norm[8 + D :]
    copy_to(RIMB.at[0], RIMB.at[1], one_s.at[5], one_r.at[5], sec, after).wait_recv()
    GB[1, D - 8 : D, :] = GB[1, D - 8 : D, :] + jnp.where(chip == n_ctx // 2 - 1, 0.0, RIMB[1])
    for b in range(2):
        TB[b] = row_sums(GB[b] * XB[b, 0])
    for ds, dc in peers:
        back = ((sections - ds) % sections) * 2 + dc
        copy = copy_to(TB.at[1 - core if dc else core], R2.at[back], row2_s.at[ds * 2 + dc], row2_r.at[back],
                       lax.rem(sec + ds, sections), partner if dc else ctx)
        go(copy)
    grad_swap = copy_to(GB.at[1 - core], GR, one_s.at[6], one_r.at[6], sec, partner)
    grad_swap.start()
    rows_wait(R2, row2_s, row2_r)
    inner = TB[core]
    for slot in range(1, 2 * sections):
        inner = inner + R2[slot]
    scale = SC[core]
    coef = as_columns(scale_same * scale_same * scale_same * inner / width_all)
    out_swap.wait_recv()
    grad_swap.wait_recv()

    def joined(own, oth):
        return jnp.concatenate([jnp.where(first, own, oth), jnp.where(first, oth, own)], axis=1)

    out_ref[...] = (x_ref[...].astype(F32) + joined(OB[core], OR[...])).astype(BF16)
    wide_scale = jnp.concatenate([scale, scale], axis=1)
    wide_coef = jnp.concatenate([coef, coef], axis=1)
    dx_ref[...] = (
        do_ref[...].astype(F32) + joined(GB[core], GR[...]) * wide_scale - x_ref[...].astype(F32) * wide_coef
    ).astype(BF16)

    for copy in row_copies + sent + [swap, rim, out_swap, rim_back, grad_swap]:
        copy.wait_send()

    @pl.when(y < n_y - 1)
    def _():
        chain_up.wait_send()

    @pl.when(y > 0)
    def _():
        chain_down.wait_send()

    for zz in range(n_z):
        @pl.when(z != zz)
        def _():
            for kind in range(2):
                back_copy(zz, kind, zz).wait_send()


def solution(mesh):
    sections, n_ctx = mesh.shape["section"], mesh.shape["ctx"]
    n_y, n_z = (4, 8) if n_ctx == 64 else (2, n_ctx // 4)
    cols = D // n_z
    dma = pltpu.SemaphoreType.DMA

    def shards(inputs, out_grads, conv_weight, log_decay, beta):
        width_all = float(inputs.shape[1] * sections)
        v = lambda *s: pltpu.VMEM(s, F32)
        scratch = [
            v(4, D, D), v(2, 4, D, D), v(2 * sections, 8, D), v(2 * sections, 8, D), v(2, 8, D),
            v(2 * D + 8, D), v(8, D), v(2, 8, D), v(2, D, D),
            v(3, 2 * D, D), v(3, 2 * D, D), v(2, 4, D, D), v(2, 3 * D, D), v(2, 2 * D, D), v(2, 2, D, D),
            v(2, 2, D, D), v(2, 3, D, D), v(n_z, D, D), v(n_z, 2 * cols, D), v(n_z, 2 * cols, D),
            v(4 + n_z, cols, D), v(1 + n_z, 2, cols, D), v(2, D, D), v(3, 2 * D + 16, D),
            v(2, D, D), v(D, D), v(2, D, D), v(D, D),
            dma((2 * sections,)), dma((2 * sections,)), dma((2 * sections,)), dma((2 * sections,)),
            dma((8,)), dma((8,)), dma((n_z,)), dma((n_z,)), dma((n_z,)), dma((n_z,)),
            dma((2 * n_z,)), dma((2 * n_z,)),
        ]
        vm = pl.BlockSpec(memory_space=pltpu.VMEM)
        return pl.pallas_call(
            functools.partial(kernel, (sections, n_y, n_z, width_all)),
            out_shape=(jax.ShapeDtypeStruct(inputs.shape, BF16), jax.ShapeDtypeStruct(inputs.shape, BF16)),
            in_specs=[vm] * 5,
            out_specs=(vm, vm),
            scratch_shapes=scratch,
            compiler_params=pltpu.CompilerParams(
                collective_id=0, has_side_effects=True, vmem_limit_bytes=40 * 2**20
            ),
        )(inputs, out_grads, log_decay, beta, conv_weight)

    spec = P("ctx", "section")
    return jax.shard_map(
        shards, mesh=mesh, in_specs=(spec, spec, P(None, None, "section"), spec, spec),
        out_specs=(spec, spec), check_vma=False,
    )
```

```python
import functools

import jax
import jax.numpy as jnp
from jax import lax
from jax.experimental import pallas as pl
from jax.experimental.pallas import tpu as pltpu
from jax.sharding import PartitionSpec as P

MESH = pl.DeviceIdType.MESH
D = 128
F32 = jnp.float32
BF16 = jnp.bfloat16


def split2(a):
    high = a.astype(BF16)
    low = (a - high.astype(F32)).astype(BF16)
    return high, low


def raw_dot(a, b, ca, cb):
    return lax.dot_general(a, b, (((ca,), (cb,)), ((), ())), preferred_element_type=F32)


def mm(a, b, ca=1, cb=0):
    ah, al = split2(a)
    bh, bl = split2(b)
    return raw_dot(ah, bh, ca, cb) + (raw_dot(ah, bl, ca, cb) + raw_dot(al, bh, ca, cb))


def mm_nt(a, b):
    return mm(a, b, 1, 1)


def mm_tn(a, b):
    return mm(a, b, 0, 0)


def iota2(shape, axis):
    return lax.broadcasted_iota(jnp.int32, shape, axis)


def row_sums(values):
    high, low = split2(values)
    ones = jnp.ones((8, values.shape[1]), BF16)
    return raw_dot(ones, high, 1, 1) + raw_dot(ones, low, 1, 1)


def as_columns(tile):
    return jnp.transpose(jnp.broadcast_to(tile[0:1], (D, D)))


def unit_lower_inverse(strict_parts):
    r, c = iota2((D, D), 0), iota2((D, D), 1)
    eye = jnp.where(r == c, 1.0, 0.0).astype(F32)
    inverse = None
    for k in range(7):
        mask = ((r >> (k + 1)) == (c >> (k + 1))) & (((r >> k) & 1) == 1) & (((c >> k) & 1) == 0)
        off = [jnp.where(mask, a, 0.0) for a in strict_parts]
        if k == 0:
            inverse = [eye - o for o in off]
        else:
            half = [mm(m, o) for m, o in zip(inverse, off)]
            inverse = [m - mm(h, m) for h, m in zip(half, inverse)]
    return inverse


def kernel(geom, x_hbm, do_hbm, g_hbm, beta_hbm, w_hbm, out_ref, dx_ref, *scratch):
    sections, n_y, n_z, width_all = geom
    (
        x_ref, do_ref, g_ref, beta_ref, w_ref,
        SB, XB, R, R2, TB, NP, RIM, RIMR, SC, GRIM, RIM2, RT,
        QK, DS, EX, FB, WQ, UO, ZK, MAPS, TS, VS, VR, UP, DN, XS, XF, XY, PY, SG, SGF, DM, OB, OR, GB, GR,
        in_s, row_s, row_r, rim_s, rim_r, row2_s, row2_r, rim2_s, rim2_r, one_s, one_r,
        ring_s, ring_r, vec_s, vec_r, xf_s, xf_r, sg_s, sg_r, ya_s, ya_r, yb_s, yb_r,
    ) = scratch
    n_ctx = n_y * n_z * 2
    n_chip = n_y * n_z
    cols = D // n_z
    half = n_z // 2
    sec = lax.axis_index("section")
    ctx = lax.axis_index("ctx")
    core = lax.rem(ctx, 2)
    chip = ctx // 2
    y = chip // n_z
    z = lax.rem(chip, n_z)
    partner = ctx + 1 - 2 * core
    first = core == 0
    has_before = chip > 0
    has_after = chip < n_chip - 1
    feeds = jnp.logical_and(core == 1, has_after)
    after_chip = 2 * lax.rem(chip + 1, n_chip)
    before_tail = 2 * lax.rem(chip + n_chip - 1, n_chip) + 1

    def at_z(zz):
        return y * (2 * n_z) + zz * 2 + core

    def at_y(yy):
        return yy * (2 * n_z) + z * 2 + core

    def side(ds):
        return lax.rem(sec + ds, sections)

    def copy_to(src, dst, ss, rs, to_sec, to_ctx):
        return pltpu.make_async_remote_copy(
            src_ref=src, dst_ref=dst, send_sem=ss, recv_sem=rs,
            device_id=(to_sec, to_ctx), device_id_type=MESH,
        )

    def arrives(dst, rs):
        copy_to(dst, dst, one_s.at[0], rs, sec, partner).wait_recv()

    sent = []

    def go(*args):
        copy = copy_to(*args)
        copy.start()
        sent.append(copy)

    peers = [(ds, dc) for ds in range(sections) for dc in range(2) if ds or dc]

    loads = [
        pltpu.make_async_copy(src, dst, in_s.at[n])
        for n, (src, dst) in enumerate(
            ((x_hbm, x_ref), (do_hbm, do_ref), (g_hbm, g_ref), (beta_hbm, beta_ref), (w_hbm, w_ref))
        )
    ]
    for load in loads:
        load.start()

    barrier = pltpu.get_barrier_semaphore()

    def greet(to_sec, to_ctx):
        pl.semaphore_signal(barrier, inc=1, device_id=(to_sec, to_ctx), device_id_type=MESH)

    for ds, dc in peers:
        greet(side(ds), partner if dc else ctx)
    for dz in range(1, n_z):
        greet(sec, at_z(lax.rem(z + dz, n_z)))
    for dy in range(1, n_y):
        greet(sec, at_y(lax.rem(y + dy, n_y)))

    @pl.when(has_before)
    def _():
        for ds in range(sections):
            greet(side(ds), before_tail)

    @pl.when(feeds)
    def _():
        for ds in range(sections):
            for dc in range(2):
                greet(side(ds), after_chip + dc)

    greeted = (
        len(peers) + n_z - 1 + n_y - 1
        + sections * has_before.astype(jnp.int32) + 2 * sections * feeds.astype(jnp.int32)
    )

    for load in loads:
        load.wait()

    def halves(ref):
        whole = ref[...].astype(F32)
        low, high = whole[:, :D], whole[:, D:]
        return jnp.where(first, low, high), jnp.where(first, high, low), whole

    x_own, x_oth, x_all = halves(x_ref)
    R[0] = row_sums(x_all * x_all)
    d_own, d_oth, _ = halves(do_ref)
    g_own, g_oth, _ = halves(g_ref)
    b0, b1 = as_columns(beta_ref[0:1, :]), as_columns(beta_ref[1:2, :])
    SB[0] = x_oth
    SB[1] = d_oth
    SB[2] = g_oth
    SB[3] = jnp.where(first, b1, b0)
    XB[core, 0] = x_own
    XB[core, 1] = d_own
    XB[core, 2] = g_own
    XB[core, 3] = jnp.where(first, b0, b1)
    RT[0] = x_all[D - 8 :, :D]
    RT[1] = x_all[D - 8 :, D:]
    pl.semaphore_wait(barrier, greeted)

    for ds, dc in reversed(peers):
        back = ((sections - ds) % sections) * 2 + dc
        go(R.at[0], R.at[back], row_s.at[ds * 2 + dc], row_r.at[back], side(ds), partner if dc else ctx)
    go(SB, XB.at[core], one_s.at[0], one_r.at[0], sec, partner)

    def rim_copies():
        made = []
        for dc in range(2):
            made.append(copy_to(RT.at[dc], RIMR, rim_s.at[2 * sections + dc], rim_r.at[sections], sec, after_chip + dc))
            for ds in range(sections):
                made.append(copy_to(R.at[0], RIM.at[(sections - ds) % sections], rim_s.at[2 * ds + dc],
                                    rim_r.at[(sections - ds) % sections], side(ds), after_chip + dc))
        return made

    @pl.when(feeds)
    def _():
        for copy in rim_copies():
            copy.start()

    arrives(XB.at[1 - core], one_r.at[0])
    r, c = iota2((D, D), 0), iota2((D, D), 1)
    incl = r >= c
    strict = r > c
    lower = jnp.where(incl, 1.0, 0.0).astype(BF16)
    fins = []
    for b in range(2):
        g = XB[b, 2]
        gh = g.astype(BF16)
        rest = g - gh.astype(F32)
        gm = rest.astype(BF16)
        gl = (rest - gm.astype(F32)).astype(BF16)
        cum = raw_dot(lower, gh, 1, 0) + (raw_dot(lower, gm, 1, 0) + raw_dot(lower, gl, 1, 0))
        mid = cum[D // 2 : D // 2 + 1]
        fin = cum[D - 1 : D]
        EX[b, 0] = jnp.exp(cum - mid)
        EX[b, 1] = jnp.exp(mid - cum)
        EX[b, 2] = jnp.exp(cum)
        EX[b, 3] = jnp.exp(fin - cum)
        fins.append(fin)

    for ds, dc in peers:
        slot = ds * 2 + dc
        arrives(R.at[slot], row_r.at[slot])
    same = R[0]
    other = R[1]
    for ds in range(1, sections):
        same = same + R[2 * ds]
        other = other + R[2 * ds + 1]

    def scale_of(total):
        return 1.0 / jnp.sqrt(total / width_all + 1e-5)

    scale_same = scale_of(same)
    SC[core] = as_columns(scale_same)
    SC[1 - core] = as_columns(scale_of(other))
    for b in range(2):
        NP[8 + D * b : 8 + D * (b + 1), :] = XB[b, 0] * SC[b]

    @pl.when(has_before)
    def _():
        for ds in range(sections):
            arrives(RIM.at[ds], rim_r.at[ds])
        arrives(RIMR, rim_r.at[sections])
        rim_total = RIM[0]
        for ds in range(1, sections):
            rim_total = rim_total + RIM[ds]
        NP[0:8, :] = RIMR[...] * as_columns(scale_of(rim_total))[D - 8 :]

    @pl.when(jnp.logical_not(has_before))
    def _():
        NP[0:8, :] = jnp.zeros((8, D), F32)
        RIMR[...] = jnp.zeros((8, D), F32)

    def tap(j, i):
        both = w_ref[j, i : i + 1, :]
        return jnp.where(first, both[:, :D], both[:, D:])

    taps = [[tap(j, i) for i in range(4)] for j in range(3)]
    shifted = [NP[5 + i : 5 + i + 2 * D, :] for i in range(4)]
    for j in range(3):
        mix = taps[j][0] * shifted[0]
        for i in range(1, 4):
            mix = mix + taps[j][i] * shifted[i]
        gate = 1.0 / (1.0 + jnp.exp(-mix))
        act = mix * gate
        slope = gate * (1.0 + mix * (1.0 - gate))
        if j < 2:
            norm = 1.0 / jnp.sqrt(jnp.sum(act * act, axis=1, keepdims=True) + 1e-6)
            QK[j] = act * norm
            DS[j] = slope * norm
        else:
            QK[j] = act
            DS[j] = slope

    blk = [slice(D * b, D * (b + 1)) for b in range(2)]
    systems, scores = [], []
    for b in range(2):
        q, k = QK[0, blk[b], :], QK[1, blk[b], :]
        kf, kb, qf = k * EX[b, 0], k * EX[b, 1], q * EX[b, 0]
        FB[b, 0:D, :] = kf
        FB[b, D : 2 * D, :] = qf
        FB[b, 2 * D : 3 * D, :] = kb
        both = mm_nt(jnp.concatenate([kf, qf], axis=0), kb)
        systems.append(jnp.where(strict, XB[b, 3] * both[:D], 0.0))
        scores.append(jnp.where(incl, both[D:], 0.0))
    inverses = unit_lower_inverse(systems)
    wus, kes = [], []
    for b in range(2):
        k, v, beta = QK[1, blk[b], :], QK[2, blk[b], :], XB[b, 3]
        ke = k * EX[b, 3]
        wu = mm(inverses[b], jnp.concatenate([beta * k * EX[b, 2], beta * v], axis=1))
        MAPS[b, 0] = jnp.where(r == c, jnp.exp(fins[b]), 0.0) - mm_tn(ke, wu[:, :D])
        wus.append(wu)
        kes.append(ke)
    t0, t1 = MAPS[0, 0], MAPS[1, 0]
    TS[z] = mm(t1, t0)

    direct = [dz for dz in range(1, n_z) if dz != half or n_z == 2]
    for dz in sorted(direct, key=lambda dz: (min(dz, n_z - dz) > 1, -min(dz, n_z - dz))):
        go(TS.at[z], TS.at[z], ring_s.at[dz], ring_r.at[n_z - dz], sec, at_z(lax.rem(z + dz, n_z)))

    for b in range(2):
        q, d_out, sc = QK[0, blk[b], :], XB[b, 1], scores[b]
        w, u = wus[b][:, :D], wus[b][:, D:]
        swu = mm(sc, wus[b])
        qeff = q * EX[b, 2] - swu[:, :D]
        WQ[b, 0:D, :] = w
        WQ[b, D : 2 * D, :] = qeff
        UO[b, 0] = u
        UO[b, 1] = swu[:, D:]
        MAPS[b, 1] = mm_tn(u, kes[b])
        MAPS[b, 2] = mm_tn(d_out, qeff)
    i_pair = mm_nt(MAPS[0, 1], t1) + MAPS[1, 1]
    s_pair = MAPS[0, 2] + mm(MAPS[1, 2], t0)
    for zz in range(n_z):
        VS[zz, 0:cols, :] = i_pair[zz * cols : (zz + 1) * cols]
        VS[zz, cols : 2 * cols, :] = s_pair[zz * cols : (zz + 1) * cols]
    VR[z] = VS[z]
    for dz in range(1, n_z):
        to = lax.rem(z + dz, n_z)
        go(VS.at[to], VR.at[z], vec_s.at[dz], vec_r.at[n_z - dz], sec, at_z(to))
    if n_z > 2:
        low, high = pl.ds(0, D // 2), pl.ds(D // 2, D // 2)
        left, right = lax.rem(z + n_z - 1, n_z), lax.rem(z + 1, n_z)
        arrives(TS.at[left], ring_r.at[n_z - 1])
        go(TS.at[left, low], TS.at[left, low], ring_s.at[0], ring_r.at[0], sec, at_z(lax.rem(z + half - 1, n_z)))
        arrives(TS.at[right], ring_r.at[1])
        go(TS.at[right, high], TS.at[right, high], ring_s.at[half], ring_r.at[half], sec,
           at_z(lax.rem(z + n_z - half + 1, n_z)))

    for b in range(2):
        h = mm_tn(scores[b], XB[b, 1])
        zk = mm_tn(inverses[b], jnp.concatenate([h, kes[b]], axis=1))
        ZK[b, 0] = zk[:, :D]
        ZK[b, 1] = zk[:, D:]
    for dz in direct:
        if n_z == 2 or dz not in (1, n_z - 1):
            arrives(TS.at[lax.rem(z + dz, n_z)], ring_r.at[dz])
    for dz in range(1, n_z):
        arrives(VR.at[lax.rem(z + dz, n_z)], vec_r.at[dz])
    if n_z > 2:
        far = lax.rem(z + half, n_z)
        arrives(TS.at[far, low], ring_r.at[0])
        arrives(TS.at[far, high], ring_r.at[half])

    eye = jnp.where(r == c, 1.0, 0.0).astype(F32)
    zero_map = jnp.zeros((D, D), F32)
    UP[0] = jnp.concatenate([jnp.zeros((cols, D), F32), eye], axis=0)
    DN[n_z - 1] = jnp.concatenate([jnp.zeros((cols, D), F32), eye], axis=0)
    up = jnp.concatenate([VR[0, 0:cols, :], jnp.transpose(TS[0])], axis=0)
    down = jnp.concatenate([VR[n_z - 1, cols : 2 * cols, :], TS[n_z - 1]], axis=0)
    for step in range(1, n_z):
        zu, zd = step, n_z - 1 - step
        UP[zu] = up
        DN[zd] = down
        up = mm_nt(up, TS[zu]) + jnp.concatenate([VR[zu, 0:cols, :], zero_map], axis=0)
        down = mm(down, TS[zd]) + jnp.concatenate([VR[zd, cols : 2 * cols, :], zero_map], axis=0)
    XY[y, 0] = up[:cols]
    XY[y, 1] = down[:cols]
    for dy in range(1, n_y):
        go(XY.at[y], XY.at[y], ya_s.at[dy], ya_r.at[n_y - dy], sec, at_y(lax.rem(y + dy, n_y)))

    def map_copy(yy, dy):
        slot = PY.at[yy - 1]
        return copy_to(slot, slot, yb_s.at[dy], yb_r.at[yy], sec, at_y(lax.rem(y + dy, n_y)))

    for yy in range(1, n_y - 1):
        @pl.when(y == yy)
        def _():
            PY[yy - 1] = up[cols:]
            for dy in range(1, n_y):
                map_copy(yy, dy).start()

    for zz in range(n_z):
        XS[zz, 0] = UP[zz, 0:cols, :]
        XS[zz, 1] = DN[zz, 0:cols, :]
    mine = pl.ds(pl.multiple_of(z * cols, cols), cols)
    XF[:, mine, :] = XS[z]
    for dz in range(1, n_z):
        to = lax.rem(z + dz, n_z)
        go(XS.at[to], XF.at[:, mine], xf_s.at[dz], xf_r.at[n_z - dz], sec, at_z(to))

    for dy in range(1, n_y):
        arrives(XY.at[lax.rem(y + dy, n_y)], ya_r.at[dy])
    for yy in range(1, n_y - 1):
        @pl.when(y != yy)
        def _():
            arrives(PY.at[yy - 1], yb_r.at[yy])
    enter = jnp.where(y > 0, XY[0, 0], 0.0)
    leave = jnp.where(y < n_y - 1, XY[n_y - 1, 1], 0.0)
    for step in range(1, n_y - 1):
        yu, yd = step, n_y - 1 - step
        enter = jnp.where(y > yu, mm(enter, PY[yu - 1]) + XY[yu, 0], enter)
        leave = jnp.where(y < yd, mm_nt(leave, PY[yd - 1]) + XY[yd, 1], leave)
    SG[0] = enter
    SG[1] = leave
    SGF[:, mine, :] = SG[...]
    for dz in range(1, n_z):
        go(SG, SGF.at[:, mine], sg_s.at[dz], sg_r.at[n_z - dz], sec, at_z(lax.rem(z + dz, n_z)))
    for dz in range(1, n_z):
        theirs = pl.ds(pl.multiple_of(lax.rem(z + dz, n_z) * cols, cols), cols)
        arrives(XF.at[:, theirs], xf_r.at[dz])
        arrives(SGF.at[:, theirs], sg_r.at[dz])

    starts = [XF[0] + mm(SGF[0], UP[z, cols:, :]), None]
    ends = [None, XF[1] + mm(SGF[1], DN[z, cols:, :])]
    starts[1] = mm_nt(starts[0], t0) + MAPS[0, 1]
    ends[0] = mm(ends[1], t1) + MAPS[1, 2]
    DM[:, 0:8, :] = jnp.zeros((3, 8, D), F32)
    DM[:, 8 + 2 * D :, :] = jnp.zeros((3, 8, D), F32)
    for b in range(2):
        q, k = QK[0, blk[b], :], QK[1, blk[b], :]
        beta, d_out = XB[b, 3], XB[b, 1]
        wq = mm_nt(WQ[b], starts[b])
        fresh = UO[b, 0] - wq[:D]
        OB[b] = UO[b, 1] + wq[D:]
        zeta = ZK[b, 0] + mm_nt(ZK[b, 1], ends[b])
        pair = mm_nt(jnp.concatenate([d_out, zeta], axis=0), fresh)
        d_sc = jnp.where(incl, pair[:D], 0.0)
        d_p = beta * jnp.where(strict, -pair[D:], 0.0)
        dz_s = mm(jnp.concatenate([d_out, zeta], axis=0), starts[b])
        f_g = mm(fresh, ends[b])
        by_kb = mm(jnp.concatenate([d_sc, d_p], axis=0), FB[b, 2 * D : 3 * D, :])
        d_kb = mm_tn(jnp.concatenate([d_p, d_sc], axis=0), FB[b, 0 : 2 * D, :])
        dq = EX[b, 2] * dz_s[:D] + EX[b, 0] * by_kb[:D]
        dk = EX[b, 3] * f_g - beta * EX[b, 2] * dz_s[D:] + EX[b, 0] * by_kb[D:] + EX[b, 1] * d_kb
        for j, (unit, grad) in enumerate(((q, dq), (k, dk))):
            along = jnp.sum(unit * grad, axis=1, keepdims=True)
            DM[j, 8 + D * b : 8 + D * (b + 1), :] = (grad - unit * along) * DS[j, blk[b], :]
        DM[2, 8 + D * b : 8 + D * (b + 1), :] = beta * zeta * DS[2, blk[b], :]
    go(OB.at[1 - core], OR, one_s.at[1], one_r.at[1], sec, partner)

    d_norm = jnp.zeros((2 * D + 8, D), F32)
    for j in range(3):
        for i in range(4):
            d_norm = d_norm + taps[j][i] * DM[j, 3 - i : 3 - i + 2 * D + 8, :]
    GB[0] = d_norm[8 : 8 + D]
    GB[1] = d_norm[8 + D :]
    GRIM[2] = d_norm[:8]
    TB[2] = row_sums(jnp.concatenate([jnp.zeros((D - 8, D), F32), d_norm[:8] * RIMR[...]], axis=0))
    TB[0] = row_sums(d_norm[8 : 8 + D] * XB[0, 0])
    TB[1] = row_sums(d_norm[8 + D :] * XB[1, 0])

    for ds, dc in reversed(peers):
        back = ((sections - ds) % sections) * 2 + dc
        go(TB.at[1 - core if dc else core], R2.at[back], row2_s.at[ds * 2 + dc], row2_r.at[back],
           side(ds), partner if dc else ctx)

    def rim_back_copies():
        made = [copy_to(GRIM.at[2], GRIM.at[core], rim2_s.at[sections], rim2_r.at[2 * sections + core], sec, before_tail)]
        for ds in range(sections):
            slot = 2 * ((sections - ds) % sections) + core
            made.append(copy_to(TB.at[2], RIM2.at[slot], rim2_s.at[ds], rim2_r.at[slot], side(ds), before_tail))
        return made

    @pl.when(has_before)
    def _():
        for copy in rim_back_copies():
            copy.start()

    go(GB.at[1 - core], GR, one_s.at[2], one_r.at[2], sec, partner)

    @pl.when(feeds)
    def _():
        for slot in range(2 * sections):
            arrives(RIM2.at[slot], rim2_r.at[slot])
        for n in range(2):
            arrives(GRIM.at[n], rim2_r.at[2 * sections + n])

    @pl.when(jnp.logical_not(feeds))
    def _():
        RIM2[...] = jnp.zeros((2 * sections, 8, D), F32)
        GRIM[0] = jnp.zeros((8, D), F32)
        GRIM[1] = jnp.zeros((8, D), F32)

    for ds, dc in peers:
        slot = ds * 2 + dc
        arrives(R2.at[slot], row2_r.at[slot])
    inner = TB[core] + RIM2[0]
    for slot in range(1, 2 * sections):
        inner = inner + R2[slot] + RIM2[slot]
    scale = SC[core]
    coef = as_columns(scale_same * scale_same * scale_same * inner / width_all)
    arrives(OR, one_r.at[1])
    arrives(GR, one_r.at[2])

    def joined(own, oth):
        return jnp.concatenate([jnp.where(first, own, oth), jnp.where(first, oth, own)], axis=1)

    out_ref[...] = (x_ref[...].astype(F32) + joined(OB[core], OR[...])).astype(BF16)
    late = jnp.concatenate([GRIM[0], GRIM[1]], axis=1)
    grads = joined(GB[core], GR[...])
    grads = jnp.concatenate([grads[: D - 8], grads[D - 8 :] + late], axis=0)
    wide_scale = jnp.concatenate([scale, scale], axis=1)
    wide_coef = jnp.concatenate([coef, coef], axis=1)
    dx_ref[...] = (
        do_ref[...].astype(F32) + grads * wide_scale - x_ref[...].astype(F32) * wide_coef
    ).astype(BF16)

    for copy in sent:
        copy.wait_send()

    @pl.when(feeds)
    def _():
        for copy in rim_copies():
            copy.wait_send()

    @pl.when(has_before)
    def _():
        for copy in rim_back_copies():
            copy.wait_send()

    for yy in range(1, n_y - 1):
        @pl.when(y == yy)
        def _():
            for dy in range(1, n_y):
                map_copy(yy, dy).wait_send()


def solution(mesh):
    sections, n_ctx = mesh.shape["section"], mesh.shape["ctx"]
    n_y, n_z = (4, 8) if n_ctx == 64 else (2, n_ctx // 4)
    cols = D // n_z
    dma = lambda n: pltpu.SemaphoreType.DMA((n,))

    def shards(inputs, out_grads, conv_weight, log_decay, beta):
        width_all = float(inputs.shape[1] * sections)
        v = lambda *s: pltpu.VMEM(s, F32)
        scratch = [
            pltpu.VMEM((D, 2 * D), BF16), pltpu.VMEM((D, 2 * D), BF16), v(D, 2 * D), v(2, D), v(3, 4, 2 * D),
            v(4, D, D), v(2, 4, D, D), v(2 * sections, 8, D), v(2 * sections, 8, D), v(3, 8, D),
            v(2 * D + 8, D), v(sections, 8, D), v(8, D), v(2, D, D), v(3, 8, D), v(2 * sections, 8, D), v(2, 8, D),
            v(3, 2 * D, D), v(3, 2 * D, D), v(2, 4, D, D), v(2, 3 * D, D), v(2, 2 * D, D), v(2, 2, D, D),
            v(2, 2, D, D), v(2, 3, D, D), v(n_z, D, D), v(n_z, 2 * cols, D), v(n_z, 2 * cols, D),
            v(n_z, cols + D, D), v(n_z, cols + D, D), v(n_z, 2, cols, D), v(2, D, D), v(n_y, 2, cols, D),
            v(max(n_y - 2, 1), D, D), v(2, cols, D), v(2, D, D), v(3, 2 * D + 16, D),
            v(2, D, D), v(D, D), v(2, D, D), v(D, D),
            dma(5), dma(2 * sections), dma(2 * sections), dma(2 * sections + 2), dma(sections + 1),
            dma(2 * sections), dma(2 * sections), dma(sections + 1), dma(2 * sections + 2), dma(3), dma(3),
            dma(n_z), dma(n_z), dma(n_z), dma(n_z), dma(n_z), dma(n_z), dma(n_z), dma(n_z),
            dma(n_y), dma(n_y), dma(n_y), dma(n_y),
        ]
        vm = pl.BlockSpec(memory_space=pltpu.VMEM)
        hbm = pl.BlockSpec(memory_space=pltpu.MemorySpace.HBM)
        return pl.pallas_call(
            functools.partial(kernel, (sections, n_y, n_z, width_all)),
            out_shape=(jax.ShapeDtypeStruct(inputs.shape, BF16), jax.ShapeDtypeStruct(inputs.shape, BF16)),
            in_specs=[hbm] * 5,
            out_specs=(vm, vm),
            scratch_shapes=scratch,
            compiler_params=pltpu.CompilerParams(
                collective_id=0, has_side_effects=True, vmem_limit_bytes=64 * 2**20 - 2**18
            ),
        )(inputs, out_grads, log_decay, beta.T, conv_weight)

    spec = P("ctx", "section")
    return jax.shard_map(
        shards, mesh=mesh, in_specs=(spec, spec, P(None, None, "section"), spec, spec),
        out_specs=(spec, spec), check_vma=False,
    )
```

```python
import functools

import jax
import jax.numpy as jnp
from jax import lax
from jax.experimental import pallas as pl
from jax.experimental.pallas import tpu as pltpu
from jax.sharding import PartitionSpec as P

MESH = pl.DeviceIdType.MESH
D = 128
F32 = jnp.float32
BF16 = jnp.bfloat16


def split2(a):
    high = a.astype(BF16)
    low = (a - high.astype(F32)).astype(BF16)
    return high, low


def raw_dot(a, b, ca, cb):
    return lax.dot_general(a, b, (((ca,), (cb,)), ((), ())), preferred_element_type=F32)


def mm(a, b, ca=1, cb=0):
    ah, al = split2(a)
    bh, bl = split2(b)
    aa = jnp.concatenate([ah, al], axis=ca)
    bb = jnp.concatenate([jnp.concatenate([bh, bh], axis=cb), jnp.concatenate([bl, bl], axis=cb)], axis=1 - cb)
    wide = raw_dot(aa, bb, ca, cb)
    n = b.shape[1 - cb]
    return wide[:, :n] + wide[:, n:]


def mm_nt(a, b):
    return mm(a, b, 1, 1)


def mm_tn(a, b):
    return mm(a, b, 0, 0)


def iota2(shape, axis):
    return lax.broadcasted_iota(jnp.int32, shape, axis)


def row_sums(values):
    high, low = split2(values)
    ones = jnp.ones((8, values.shape[1]), BF16)
    return raw_dot(ones, high, 1, 1) + raw_dot(ones, low, 1, 1)


def as_columns(tile):
    return jnp.transpose(jnp.broadcast_to(tile[0:1], (D, D)))


def unit_lower_inverse(strict_parts):
    r, c = iota2((D, D), 0), iota2((D, D), 1)
    eye = jnp.where(r == c, 1.0, 0.0).astype(F32)
    inverse = None
    for k in range(7):
        mask = ((r >> (k + 1)) == (c >> (k + 1))) & (((r >> k) & 1) == 1) & (((c >> k) & 1) == 0)
        off = [jnp.where(mask, a, 0.0) for a in strict_parts]
        if k == 0:
            inverse = [eye - o for o in off]
        else:
            half = [mm(m, o) for m, o in zip(inverse, off)]
            inverse = [m - mm(h, m) for h, m in zip(half, inverse)]
    return inverse


def kernel(geom, x_hbm, do_hbm, g_hbm, beta_hbm, w_hbm, out_ref, dx_ref, *scratch):
    sections, n_y, n_z, width_all = geom
    (
        x_ref, do_ref, g_ref, beta_ref, w_ref,
        SB, XB, R, R2, TB, NP, RIM, RIMR, SC, GRIM, RIM2, RT,
        QK, DS, EX, FB, WQ, UO, ZK, MAPS, TS, VS, VR, UP, DN, XY, PY, SS, ST, DM, OB, OR, GB, GR,
        in_s, row_s, row_r, rim_s, rim_r, row2_s, row2_r, rim2_s, rim2_r, one_s, one_r,
        ring_s, ring_r, vec_s, vec_r, sg_s, sg_r, ya_s, ya_r, yb_s, yb_r,
    ) = scratch
    n_ctx = n_y * n_z * 2
    n_chip = n_y * n_z
    roots = n_z // 2
    cols = D // roots
    sec = lax.axis_index("section")
    ctx = lax.axis_index("ctx")
    core = lax.rem(ctx, 2)
    chip = ctx // 2
    y = chip // n_z
    z = lax.rem(chip, n_z)
    partner = ctx + 1 - 2 * core
    first = core == 0
    rank = z // 2
    is_root = lax.rem(z, 2) == core
    has_before = chip > 0
    has_after = chip < n_chip - 1
    feeds = jnp.logical_and(core == 1, has_after)
    after_chip = 2 * lax.rem(chip + 1, n_chip)
    before_tail = 2 * lax.rem(chip + n_chip - 1, n_chip) + 1

    def at_z(zz):
        return y * (2 * n_z) + zz * 2 + core

    def at_y(yy):
        return yy * (2 * n_z) + z * 2 + core

    def side(ds):
        return lax.rem(sec + ds, sections)

    def copy_to(src, dst, ss, rs, to_sec, to_ctx):
        return pltpu.make_async_remote_copy(
            src_ref=src, dst_ref=dst, send_sem=ss, recv_sem=rs,
            device_id=(to_sec, to_ctx), device_id_type=MESH,
        )

    def arrives(dst, rs):
        copy_to(dst, dst, one_s.at[0], rs, sec, partner).wait_recv()

    sent = []

    def go(*args):
        copy = copy_to(*args)
        copy.start()
        sent.append(copy)

    peers = [(ds, dc) for ds in range(sections) for dc in range(2) if ds or dc]
    peers.sort(key=lambda p: abs(p[0] - sections // 2))

    loads = [
        pltpu.make_async_copy(src, dst, in_s.at[n])
        for n, (src, dst) in enumerate(
            ((x_hbm, x_ref), (do_hbm, do_ref), (g_hbm, g_ref), (beta_hbm, beta_ref), (w_hbm, w_ref))
        )
    ]
    for load in loads:
        load.start()

    barrier = pltpu.get_barrier_semaphore()

    def greet(to_sec, to_ctx):
        pl.semaphore_signal(barrier, inc=1, device_id=(to_sec, to_ctx), device_id_type=MESH)

    for ds, dc in peers:
        greet(side(ds), partner if dc else ctx)
    for dz in range(1, n_z):
        greet(sec, at_z(lax.rem(z + dz, n_z)))
    for dy in range(1, n_y):
        greet(sec, at_y(lax.rem(y + dy, n_y)))

    @pl.when(has_before)
    def _():
        for ds in range(sections):
            greet(side(ds), before_tail)

    @pl.when(feeds)
    def _():
        for ds in range(sections):
            for dc in range(2):
                greet(side(ds), after_chip + dc)

    greeted = (
        len(peers) + n_z - 1 + n_y - 1
        + sections * has_before.astype(jnp.int32) + 2 * sections * feeds.astype(jnp.int32)
    )

    for load in loads:
        load.wait()

    def halves(ref):
        whole = ref[...].astype(F32)
        low, high = whole[:, :D], whole[:, D:]
        return jnp.where(first, low, high), jnp.where(first, high, low), whole

    x_own, x_oth, x_all = halves(x_ref)
    R[0] = row_sums(x_all * x_all)
    d_own, d_oth, _ = halves(do_ref)
    g_own, g_oth, _ = halves(g_ref)
    b0, b1 = as_columns(beta_ref[0:1, :]), as_columns(beta_ref[1:2, :])
    SB[0] = x_oth
    SB[1] = d_oth
    SB[2] = g_oth
    SB[3] = jnp.where(first, b1, b0)
    XB[core, 0] = x_own
    XB[core, 1] = d_own
    XB[core, 2] = g_own
    XB[core, 3] = jnp.where(first, b0, b1)
    RT[0] = x_all[D - 8 :, :D]
    RT[1] = x_all[D - 8 :, D:]
    pl.semaphore_wait(barrier, greeted)

    for ds, dc in peers:
        back = ((sections - ds) % sections) * 2 + dc
        go(R.at[0], R.at[back], row_s.at[ds * 2 + dc], row_r.at[back], side(ds), partner if dc else ctx)
    go(SB, XB.at[core], one_s.at[0], one_r.at[0], sec, partner)

    def rim_copies():
        made = []
        for dc in range(2):
            made.append(copy_to(RT.at[dc], RIMR, rim_s.at[2 * sections + dc], rim_r.at[sections], sec, after_chip + dc))
            for ds in range(sections):
                made.append(copy_to(R.at[0], RIM.at[(sections - ds) % sections], rim_s.at[2 * ds + dc],
                                    rim_r.at[(sections - ds) % sections], side(ds), after_chip + dc))
        return made

    @pl.when(feeds)
    def _():
        for copy in rim_copies():
            copy.start()

    arrives(XB.at[1 - core], one_r.at[0])
    r, c = iota2((D, D), 0), iota2((D, D), 1)
    incl = r >= c
    strict = r > c
    lower = jnp.where(incl, 1.0, 0.0).astype(BF16)
    fins = []
    for b in range(2):
        g = XB[b, 2]
        gh = g.astype(BF16)
        rest = g - gh.astype(F32)
        gm = rest.astype(BF16)
        gl = (rest - gm.astype(F32)).astype(BF16)
        cum = raw_dot(lower, gh, 1, 0) + (raw_dot(lower, gm, 1, 0) + raw_dot(lower, gl, 1, 0))
        mid = cum[D // 2 : D // 2 + 1]
        fin = cum[D - 1 : D]
        EX[b, 0] = jnp.exp(cum - mid)
        EX[b, 1] = jnp.exp(mid - cum)
        EX[b, 2] = jnp.exp(cum)
        EX[b, 3] = jnp.exp(fin - cum)
        fins.append(fin)

    for ds, dc in peers:
        slot = ds * 2 + dc
        arrives(R.at[slot], row_r.at[slot])
    same = R[0]
    other = R[1]
    for ds in range(1, sections):
        same = same + R[2 * ds]
        other = other + R[2 * ds + 1]

    def scale_of(total):
        return 1.0 / jnp.sqrt(total / width_all + 1e-5)

    scale_same = scale_of(same)
    SC[core] = as_columns(scale_same)
    SC[1 - core] = as_columns(scale_of(other))
    for b in range(2):
        NP[8 + D * b : 8 + D * (b + 1), :] = XB[b, 0] * SC[b]

    @pl.when(has_before)
    def _():
        for ds in range(sections):
            arrives(RIM.at[ds], rim_r.at[ds])
        arrives(RIMR, rim_r.at[sections])
        rim_total = RIM[0]
        for ds in range(1, sections):
            rim_total = rim_total + RIM[ds]
        NP[0:8, :] = RIMR[...] * as_columns(scale_of(rim_total))[D - 8 :]

    @pl.when(jnp.logical_not(has_before))
    def _():
        NP[0:8, :] = jnp.zeros((8, D), F32)
        RIMR[...] = jnp.zeros((8, D), F32)

    def tap(j, i):
        both = w_ref[j, i : i + 1, :]
        return jnp.where(first, both[:, :D], both[:, D:])

    taps = [[tap(j, i) for i in range(4)] for j in range(3)]
    shifted = [NP[5 + i : 5 + i + 2 * D, :] for i in range(4)]
    for j in range(3):
        mix = taps[j][0] * shifted[0]
        for i in range(1, 4):
            mix = mix + taps[j][i] * shifted[i]
        gate = 1.0 / (1.0 + jnp.exp(-mix))
        act = mix * gate
        slope = gate * (1.0 + mix * (1.0 - gate))
        if j < 2:
            norm = 1.0 / jnp.sqrt(jnp.sum(act * act, axis=1, keepdims=True) + 1e-6)
            QK[j] = act * norm
            DS[j] = slope * norm
        else:
            QK[j] = act
            DS[j] = slope

    blk = [slice(D * b, D * (b + 1)) for b in range(2)]
    systems, scores = [], []
    for b in range(2):
        q, k = QK[0, blk[b], :], QK[1, blk[b], :]
        kf, kb, qf = k * EX[b, 0], k * EX[b, 1], q * EX[b, 0]
        FB[b, 0:D, :] = kf
        FB[b, D : 2 * D, :] = qf
        FB[b, 2 * D : 3 * D, :] = kb
        both = mm_nt(jnp.concatenate([kf, qf], axis=0), kb)
        systems.append(jnp.where(strict, XB[b, 3] * both[:D], 0.0))
        scores.append(jnp.where(incl, both[D:], 0.0))
    inverses = unit_lower_inverse(systems)
    wus, kes = [], []
    for b in range(2):
        k, v, beta = QK[1, blk[b], :], QK[2, blk[b], :], XB[b, 3]
        ke = k * EX[b, 3]
        wu = mm(inverses[b], jnp.concatenate([beta * k * EX[b, 2], beta * v], axis=1))
        MAPS[b, 0] = jnp.where(r == c, jnp.exp(fins[b]), 0.0) - mm_tn(ke, wu[:, :D])
        wus.append(wu)
        kes.append(ke)
    t0, t1 = MAPS[0, 0], MAPS[1, 0]
    TS[z] = mm(t1, t0)

    def root_at(j):
        return at_z(2 * j + core)

    def map_send(dj):
        j = lax.rem(rank + dj, roots)
        return copy_to(TS.at[z], TS.at[z], ring_s.at[dj], ring_r.at[z], sec, root_at(j))

    def part_send(dj):
        j = lax.rem(rank + dj, roots)
        return copy_to(VS.at[j], VR.at[z], vec_s.at[dj], vec_r.at[z], sec, root_at(j))

    def all_roots(send, act):
        for dj in range(1, roots):
            act(send(dj))

        @pl.when(jnp.logical_not(is_root))
        def _():
            act(send(0))

    all_roots(map_send, lambda copy: copy.start())

    for b in range(2):
        q, d_out, sc = QK[0, blk[b], :], XB[b, 1], scores[b]
        w, u = wus[b][:, :D], wus[b][:, D:]
        swu = mm(sc, wus[b])
        qeff = q * EX[b, 2] - swu[:, :D]
        WQ[b, 0:D, :] = w
        WQ[b, D : 2 * D, :] = qeff
        UO[b, 0] = u
        UO[b, 1] = swu[:, D:]
        MAPS[b, 1] = mm_tn(u, kes[b])
        MAPS[b, 2] = mm_tn(d_out, qeff)
    i_pair = mm_nt(MAPS[0, 1], t1) + MAPS[1, 1]
    s_pair = MAPS[0, 2] + mm(MAPS[1, 2], t0)
    for j in range(roots):
        VS[j, 0] = i_pair[j * cols : (j + 1) * cols]
        VS[j, 1] = s_pair[j * cols : (j + 1) * cols]
    all_roots(part_send, lambda copy: copy.start())

    for b in range(2):
        h = mm_tn(scores[b], XB[b, 1])
        zk = mm_tn(inverses[b], jnp.concatenate([h, kes[b]], axis=1))
        ZK[b, 0] = zk[:, :D]
        ZK[b, 1] = zk[:, D:]
    DM[:, 0:8, :] = jnp.zeros((3, 8, D), F32)
    DM[:, 8 + 2 * D :, :] = jnp.zeros((3, 8, D), F32)
    eye = jnp.where(r == c, 1.0, 0.0).astype(F32)
    mine = pl.ds(pl.multiple_of(rank * cols, cols), cols)

    def ends_send(dy):
        return copy_to(XY.at[y], XY.at[y], ya_s.at[dy], ya_r.at[n_y - dy], sec, at_y(lax.rem(y + dy, n_y)))

    def total_send(yy, dy):
        slot = PY.at[yy - 1]
        return copy_to(slot, slot, yb_s.at[dy], yb_r.at[yy], sec, at_y(lax.rem(y + dy, n_y)))

    def slice_send(dz):
        to = lax.rem(z + dz, n_z)
        return copy_to(SS.at[to], ST.at[:, mine], sg_s.at[dz], sg_r.at[rank], sec, at_z(to))

    @pl.when(is_root)
    def _():
        VR[z] = VS[rank]
        for dz in range(1, n_z):
            zz = lax.rem(z + dz, n_z)
            arrives(TS.at[zz], ring_r.at[zz])
            arrives(VR.at[zz], vec_r.at[zz])
        none = jnp.zeros((D, D), F32)
        up = jnp.concatenate([VR[0, 0], jnp.transpose(TS[0])], axis=0)
        down = jnp.concatenate([VR[n_z - 1, 1], TS[n_z - 1]], axis=0)
        for step in range(1, n_z):
            zu, zd = step, n_z - 1 - step
            UP[zu] = up
            DN[zd] = down
            up = mm_nt(up, TS[zu]) + jnp.concatenate([VR[zu, 0], none], axis=0)
            down = mm(down, TS[zd]) + jnp.concatenate([VR[zd, 1], none], axis=0)
        XY[y, 0] = up[:cols]
        XY[y, 1] = down[:cols]
        for dy in range(1, n_y):
            ends_send(dy).start()
        for yy in range(1, n_y - 1):
            @pl.when(y == yy)
            def _():
                PY[yy - 1] = up[cols:]
                for dy in range(1, n_y):
                    total_send(yy, dy).start()

        for dy in range(1, n_y):
            arrives(XY.at[lax.rem(y + dy, n_y)], ya_r.at[dy])
        for yy in range(1, n_y - 1):
            @pl.when(y != yy)
            def _():
                arrives(PY.at[yy - 1], yb_r.at[yy])
        enter = jnp.where(y > 0, XY[0, 0], 0.0)
        leave = jnp.where(y < n_y - 1, XY[n_y - 1, 1], 0.0)
        for step in range(1, n_y - 1):
            yu, yd = step, n_y - 1 - step
            enter = jnp.where(y > yu, mm(enter, PY[yu - 1]) + XY[yu, 0], enter)
            leave = jnp.where(y < yd, mm_nt(leave, PY[yd - 1]) + XY[yd, 1], leave)

        for zz in range(n_z):
            SS[zz, 0] = enter if zz == 0 else UP[zz, :cols, :] + mm(enter, UP[zz, cols:, :])
            SS[zz, 1] = leave if zz == n_z - 1 else DN[zz, :cols, :] + mm(leave, DN[zz, cols:, :])
        ST[:, mine, :] = SS[z]
        for dz in range(1, n_z):
            slice_send(dz).start()

    for dj in range(roots):
        j = lax.rem(rank + dj, roots)
        theirs = ST.at[:, pl.ds(pl.multiple_of(j * cols, cols), cols)]
        if dj:
            arrives(theirs, sg_r.at[j])
        else:
            @pl.when(jnp.logical_not(is_root))
            def _():
                arrives(theirs, sg_r.at[j])

    starts = [ST[0], None]
    ends = [None, ST[1]]
    starts[1] = mm_nt(starts[0], t0) + MAPS[0, 1]
    ends[0] = mm(ends[1], t1) + MAPS[1, 2]
    for b in range(2):
        q, k = QK[0, blk[b], :], QK[1, blk[b], :]
        beta, d_out = XB[b, 3], XB[b, 1]
        wq = mm_nt(WQ[b], starts[b])
        fresh = UO[b, 0] - wq[:D]
        OB[b] = UO[b, 1] + wq[D:]
        zeta = ZK[b, 0] + mm_nt(ZK[b, 1], ends[b])
        pair = mm_nt(jnp.concatenate([d_out, zeta], axis=0), fresh)
        d_sc = jnp.where(incl, pair[:D], 0.0)
        d_p = beta * jnp.where(strict, -pair[D:], 0.0)
        dz_s = mm(jnp.concatenate([d_out, zeta], axis=0), starts[b])
        f_g = mm(fresh, ends[b])
        by_kb = mm(jnp.concatenate([d_sc, d_p], axis=0), FB[b, 2 * D : 3 * D, :])
        d_kb = mm_tn(jnp.concatenate([d_p, d_sc], axis=0), FB[b, 0 : 2 * D, :])
        dq = EX[b, 2] * dz_s[:D] + EX[b, 0] * by_kb[:D]
        dk = EX[b, 3] * f_g - beta * EX[b, 2] * dz_s[D:] + EX[b, 0] * by_kb[D:] + EX[b, 1] * d_kb
        for j, (unit, grad) in enumerate(((q, dq), (k, dk))):
            along = jnp.sum(unit * grad, axis=1, keepdims=True)
            DM[j, 8 + D * b : 8 + D * (b + 1), :] = (grad - unit * along) * DS[j, blk[b], :]
        DM[2, 8 + D * b : 8 + D * (b + 1), :] = beta * zeta * DS[2, blk[b], :]
    go(OB.at[1 - core], OR, one_s.at[1], one_r.at[1], sec, partner)

    d_norm = jnp.zeros((2 * D + 8, D), F32)
    for j in range(3):
        for i in range(4):
            d_norm = d_norm + taps[j][i] * DM[j, 3 - i : 3 - i + 2 * D + 8, :]
    GB[0] = d_norm[8 : 8 + D]
    GB[1] = d_norm[8 + D :]
    GRIM[2] = d_norm[:8]
    TB[2] = row_sums(jnp.concatenate([jnp.zeros((D - 8, D), F32), d_norm[:8] * RIMR[...]], axis=0))
    TB[0] = row_sums(d_norm[8 : 8 + D] * XB[0, 0])
    TB[1] = row_sums(d_norm[8 + D :] * XB[1, 0])

    for ds, dc in peers:
        back = ((sections - ds) % sections) * 2 + dc
        go(TB.at[1 - core if dc else core], R2.at[back], row2_s.at[ds * 2 + dc], row2_r.at[back],
           side(ds), partner if dc else ctx)

    def rim_back_copies():
        made = [copy_to(GRIM.at[2], GRIM.at[core], rim2_s.at[sections], rim2_r.at[2 * sections + core], sec, before_tail)]
        for ds in range(sections):
            slot = 2 * ((sections - ds) % sections) + core
            made.append(copy_to(TB.at[2], RIM2.at[slot], rim2_s.at[ds], rim2_r.at[slot], side(ds), before_tail))
        return made

    @pl.when(has_before)
    def _():
        for copy in rim_back_copies():
            copy.start()

    go(GB.at[1 - core], GR, one_s.at[2], one_r.at[2], sec, partner)

    @pl.when(feeds)
    def _():
        for slot in range(2 * sections):
            arrives(RIM2.at[slot], rim2_r.at[slot])
        for n in range(2):
            arrives(GRIM.at[n], rim2_r.at[2 * sections + n])

    @pl.when(jnp.logical_not(feeds))
    def _():
        RIM2[...] = jnp.zeros((2 * sections, 8, D), F32)
        GRIM[0] = jnp.zeros((8, D), F32)
        GRIM[1] = jnp.zeros((8, D), F32)

    for ds, dc in peers:
        slot = ds * 2 + dc
        arrives(R2.at[slot], row2_r.at[slot])
    inner = TB[core] + RIM2[0]
    for slot in range(1, 2 * sections):
        inner = inner + R2[slot] + RIM2[slot]
    scale = SC[core]
    coef = as_columns(scale_same * scale_same * scale_same * inner / width_all)
    arrives(OR, one_r.at[1])
    arrives(GR, one_r.at[2])

    def joined(own, oth):
        return jnp.concatenate([jnp.where(first, own, oth), jnp.where(first, oth, own)], axis=1)

    out_ref[...] = (x_ref[...].astype(F32) + joined(OB[core], OR[...])).astype(BF16)
    late = jnp.concatenate([GRIM[0], GRIM[1]], axis=1)
    grads = joined(GB[core], GR[...])
    grads = jnp.concatenate([grads[: D - 8], grads[D - 8 :] + late], axis=0)
    wide_scale = jnp.concatenate([scale, scale], axis=1)
    wide_coef = jnp.concatenate([coef, coef], axis=1)
    dx_ref[...] = (
        do_ref[...].astype(F32) + grads * wide_scale - x_ref[...].astype(F32) * wide_coef
    ).astype(BF16)

    for copy in sent:
        copy.wait_send()

    @pl.when(feeds)
    def _():
        for copy in rim_copies():
            copy.wait_send()

    @pl.when(has_before)
    def _():
        for copy in rim_back_copies():
            copy.wait_send()

    all_roots(map_send, lambda copy: copy.wait_send())
    all_roots(part_send, lambda copy: copy.wait_send())

    @pl.when(is_root)
    def _():
        for dy in range(1, n_y):
            ends_send(dy).wait_send()
        for dz in range(1, n_z):
            slice_send(dz).wait_send()
        for yy in range(1, n_y - 1):
            @pl.when(y == yy)
            def _():
                for dy in range(1, n_y):
                    total_send(yy, dy).wait_send()


def solution(mesh):
    sections, n_ctx = mesh.shape["section"], mesh.shape["ctx"]
    n_y, n_z = (4, 8) if n_ctx == 64 else (2, n_ctx // 4)
    roots = n_z // 2
    cols = D // roots
    dma = lambda n: pltpu.SemaphoreType.DMA((n,))

    def shards(inputs, out_grads, conv_weight, log_decay, beta):
        width_all = float(inputs.shape[1] * sections)
        v = lambda *s: pltpu.VMEM(s, F32)
        scratch = [
            pltpu.VMEM((D, 2 * D), BF16), pltpu.VMEM((D, 2 * D), BF16), v(D, 2 * D), v(2, D), v(3, 4, 2 * D),
            v(4, D, D), v(2, 4, D, D), v(2 * sections, 8, D), v(2 * sections, 8, D), v(3, 8, D),
            v(2 * D + 8, D), v(sections, 8, D), v(8, D), v(2, D, D), v(3, 8, D), v(2 * sections, 8, D), v(2, 8, D),
            v(3, 2 * D, D), v(3, 2 * D, D), v(2, 4, D, D), v(2, 3 * D, D), v(2, 2 * D, D), v(2, 2, D, D),
            v(2, 2, D, D), v(2, 3, D, D), v(n_z, D, D), v(roots, 2, cols, D), v(n_z, 2, cols, D),
            v(n_z, cols + D, D), v(n_z, cols + D, D), v(n_y, 2, cols, D),
            v(max(n_y - 2, 1), D, D), v(n_z, 2, cols, D), v(2, D, D), v(3, 2 * D + 16, D),
            v(2, D, D), v(D, D), v(2, D, D), v(D, D),
            dma(5), dma(2 * sections), dma(2 * sections), dma(2 * sections + 2), dma(sections + 1),
            dma(2 * sections), dma(2 * sections), dma(sections + 1), dma(2 * sections + 2), dma(3), dma(3),
            dma(roots), dma(n_z), dma(roots), dma(n_z), dma(n_z), dma(roots),
            dma(n_y), dma(n_y), dma(n_y), dma(n_y),
        ]
        vm = pl.BlockSpec(memory_space=pltpu.VMEM)
        hbm = pl.BlockSpec(memory_space=pltpu.MemorySpace.HBM)
        return pl.pallas_call(
            functools.partial(kernel, (sections, n_y, n_z, width_all)),
            out_shape=(jax.ShapeDtypeStruct(inputs.shape, BF16), jax.ShapeDtypeStruct(inputs.shape, BF16)),
            in_specs=[hbm] * 5,
            out_specs=(vm, vm),
            scratch_shapes=scratch,
            compiler_params=pltpu.CompilerParams(
                collective_id=0, has_side_effects=True, vmem_limit_bytes=64 * 2**20 - 2**18
            ),
        )(inputs, out_grads, log_decay, beta.T, conv_weight)

    spec = P("ctx", "section")
    return jax.shard_map(
        shards, mesh=mesh, in_specs=(spec, spec, P(None, None, "section"), spec, spec),
        out_specs=(spec, spec), check_vma=False,
    )
```

```python
import functools

import jax
import jax.numpy as jnp
from jax import lax
from jax.experimental import pallas as pl
from jax.experimental.pallas import tpu as pltpu
from jax.sharding import PartitionSpec as P

MESH = pl.DeviceIdType.MESH
D = 128
F32 = jnp.float32
BF16 = jnp.bfloat16


def split2(a):
    high = a.astype(BF16)
    low = (a - high.astype(F32)).astype(BF16)
    return high, low


def raw_dot(a, b, ca, cb):
    return lax.dot_general(a, b, (((ca,), (cb,)), ((), ())), preferred_element_type=F32)


def mm(a, b, ca=1, cb=0):
    ah, al = split2(a)
    bh, bl = split2(b)
    aa = jnp.concatenate([ah, al], axis=ca)
    bb = jnp.concatenate([jnp.concatenate([bh, bh], axis=cb), jnp.concatenate([bl, bl], axis=cb)], axis=1 - cb)
    wide = raw_dot(aa, bb, ca, cb)
    n = b.shape[1 - cb]
    return wide[:, :n] + wide[:, n:]


def mm_nt(a, b):
    return mm(a, b, 1, 1)


def mm_tn(a, b):
    return mm(a, b, 0, 0)


def iota2(shape, axis):
    return lax.broadcasted_iota(jnp.int32, shape, axis)


def row_sums(values):
    high, low = split2(values)
    ones = jnp.ones((8, values.shape[1]), BF16)
    return raw_dot(ones, high, 1, 1) + raw_dot(ones, low, 1, 1)


def as_columns(tile):
    return jnp.transpose(jnp.broadcast_to(tile[0:1], (D, D)))


def unit_lower_inverse(strict_parts):
    r, c = iota2((D, D), 0), iota2((D, D), 1)
    eye = jnp.where(r == c, 1.0, 0.0).astype(F32)
    inverse = None
    for k in range(7):
        mask = ((r >> (k + 1)) == (c >> (k + 1))) & (((r >> k) & 1) == 1) & (((c >> k) & 1) == 0)
        off = [jnp.where(mask, a, 0.0) for a in strict_parts]
        if k == 0:
            inverse = [eye - o for o in off]
        else:
            half = [mm(m, o) for m, o in zip(inverse, off)]
            inverse = [m - mm(h, m) for h, m in zip(half, inverse)]
    return inverse


def kernel(geom, x_hbm, do_hbm, g_hbm, beta_hbm, w_hbm, out_ref, dx_ref, *scratch):
    sections, n_y, n_z, width_all = geom
    (
        x_ref, do_ref, g_ref, beta_ref, w_ref,
        SB, XB, R, R2, TB, NP, RIM, RIMR, SC, GRIM, RIM2, RT,
        QK, DS, EX, FB, WQ, UO, ZK, MAPS, TS, VS, VR, UP, DN, XY, PY, SS, ST, DM, OB, OR, GB, GR, FIN, RT2,
        in_s, row_s, row_r, rim_s, rim_r, row2_s, row2_r, rim2_s, rim2_r, one_s, one_r,
        ring_s, ring_r, vec_s, vec_r, sg_s, sg_r, ya_s, ya_r, yb_s, yb_r,
    ) = scratch
    n_ctx = n_y * n_z * 2
    n_chip = n_y * n_z
    roots = n_z // 2
    cols = D // roots
    sec = lax.axis_index("section")
    ctx = lax.axis_index("ctx")
    core = lax.rem(ctx, 2)
    chip = ctx // 2
    y = chip // n_z
    z = lax.rem(chip, n_z)
    partner = ctx + 1 - 2 * core
    first = core == 0
    rank = z // 2
    is_root = lax.rem(z, 2) == core
    has_before = chip > 0
    has_after = chip < n_chip - 1
    feeds = jnp.logical_and(core == 1, has_after)
    after_chip = 2 * lax.rem(chip + 1, n_chip)
    before_tail = 2 * lax.rem(chip + n_chip - 1, n_chip) + 1

    def at_z(zz):
        return y * (2 * n_z) + zz * 2 + core

    def at_y(yy):
        return yy * (2 * n_z) + z * 2 + core

    def side(ds):
        return lax.rem(sec + ds, sections)

    def copy_to(src, dst, ss, rs, to_sec, to_ctx):
        return pltpu.make_async_remote_copy(
            src_ref=src, dst_ref=dst, send_sem=ss, recv_sem=rs,
            device_id=(to_sec, to_ctx), device_id_type=MESH,
        )

    def arrives(dst, rs):
        copy_to(dst, dst, one_s.at[0], rs, sec, partner).wait_recv()

    sent = []

    def go(*args):
        copy = copy_to(*args)
        copy.start()
        sent.append(copy)

    peers = [(ds, dc) for ds in range(sections) for dc in range(2) if ds or dc]
    peers.sort(key=lambda p: abs(p[0] - sections // 2))

    loads = [
        pltpu.make_async_copy(src, dst, in_s.at[n])
        for n, (src, dst) in enumerate(
            ((x_hbm, x_ref), (do_hbm, do_ref), (g_hbm, g_ref), (beta_hbm, beta_ref), (w_hbm, w_ref))
        )
    ]
    for load in loads:
        load.start()

    barrier = pltpu.get_barrier_semaphore()

    def greet(to_sec, to_ctx):
        pl.semaphore_signal(barrier, inc=1, device_id=(to_sec, to_ctx), device_id_type=MESH)

    @pl.when(has_before)
    def _():
        for ds in range(sections):
            greet(side(ds), before_tail)

    @pl.when(feeds)
    def _():
        for ds in range(sections):
            for dc in range(2):
                greet(side(ds), after_chip + dc)

    for ds, dc in peers:
        greet(side(ds), partner if dc else ctx)
    for dz in range(1, n_z):
        greet(sec, at_z(lax.rem(z + dz, n_z)))
    for dy in range(1, n_y):
        greet(sec, at_y(lax.rem(y + dy, n_y)))

    greeted = (
        len(peers) + n_z - 1 + n_y - 1
        + sections * has_before.astype(jnp.int32) + 2 * sections * feeds.astype(jnp.int32)
    )

    for load in loads:
        load.wait()

    def halves(ref):
        whole = ref[...].astype(F32)
        low, high = whole[:, :D], whole[:, D:]
        return jnp.where(first, low, high), jnp.where(first, high, low), whole

    x_own, x_oth, x_all = halves(x_ref)
    R[0] = row_sums(x_all * x_all)
    d_own, d_oth, _ = halves(do_ref)
    g_own, g_oth, _ = halves(g_ref)
    b0, b1 = as_columns(beta_ref[0:1, :]), as_columns(beta_ref[1:2, :])
    SB[0] = x_oth
    SB[1] = d_oth
    SB[2] = g_oth
    SB[3] = jnp.where(first, b1, b0)
    XB[core, 0] = x_own
    XB[core, 1] = d_own
    XB[core, 2] = g_own
    XB[core, 3] = jnp.where(first, b0, b1)
    RT[0] = x_all[D - 8 :, :D]
    RT[1] = x_all[D - 8 :, D:]
    pl.semaphore_wait(barrier, greeted)

    for ds, dc in peers:
        back = ((sections - ds) % sections) * 2 + dc
        go(R.at[0], R.at[back], row_s.at[ds * 2 + dc], row_r.at[back], side(ds), partner if dc else ctx)
    go(SB, XB.at[core], one_s.at[0], one_r.at[0], sec, partner)

    def rim_copies():
        made = []
        for dc in range(2):
            made.append(copy_to(RT.at[dc], RIMR, rim_s.at[2 * sections + dc], rim_r.at[sections], sec, after_chip + dc))
            for ds in range(sections):
                made.append(copy_to(R.at[0], RIM.at[(sections - ds) % sections], rim_s.at[2 * ds + dc],
                                    rim_r.at[(sections - ds) % sections], side(ds), after_chip + dc))
        return made

    @pl.when(feeds)
    def _():
        for copy in rim_copies():
            copy.start()

    arrives(XB.at[1 - core], one_r.at[0])
    r, c = iota2((D, D), 0), iota2((D, D), 1)
    incl = r >= c
    strict = r > c
    lower = jnp.where(incl, 1.0, 0.0).astype(BF16)
    fins = []
    for b in range(2):
        g = XB[b, 2]
        gh = g.astype(BF16)
        rest = g - gh.astype(F32)
        gm = rest.astype(BF16)
        gl = (rest - gm.astype(F32)).astype(BF16)
        cum = raw_dot(lower, gh, 1, 0) + (raw_dot(lower, gm, 1, 0) + raw_dot(lower, gl, 1, 0))
        mid = cum[D // 2 : D // 2 + 1]
        fin = cum[D - 1 : D]
        EX[b, 0] = jnp.exp(cum - mid)
        EX[b, 1] = jnp.exp(mid - cum)
        EX[b, 2] = jnp.exp(cum)
        EX[b, 3] = jnp.exp(fin - cum)
        fins.append(fin)

    for ds, dc in peers:
        slot = ds * 2 + dc
        arrives(R.at[slot], row_r.at[slot])
    same = R[0]
    other = R[1]
    for ds in range(1, sections):
        same = same + R[2 * ds]
        other = other + R[2 * ds + 1]

    def scale_of(total):
        return 1.0 / jnp.sqrt(total / width_all + 1e-5)

    scale_same = scale_of(same)
    SC[core] = as_columns(scale_same)
    SC[1 - core] = as_columns(scale_of(other))
    for b in range(2):
        NP[8 + D * b : 8 + D * (b + 1), :] = XB[b, 0] * SC[b]

    @pl.when(has_before)
    def _():
        for ds in range(sections):
            arrives(RIM.at[ds], rim_r.at[ds])
        arrives(RIMR, rim_r.at[sections])
        rim_total = RIM[0]
        for ds in range(1, sections):
            rim_total = rim_total + RIM[ds]
        NP[0:8, :] = RIMR[...] * as_columns(scale_of(rim_total))[D - 8 :]

    @pl.when(jnp.logical_not(has_before))
    def _():
        NP[0:8, :] = jnp.zeros((8, D), F32)
        RIMR[...] = jnp.zeros((8, D), F32)

    def tap(j, i):
        both = w_ref[j, i : i + 1, :]
        return jnp.where(first, both[:, :D], both[:, D:])

    taps = [[tap(j, i) for i in range(4)] for j in range(3)]
    shifted = [NP[5 + i : 5 + i + 2 * D, :] for i in range(4)]
    for j in range(3):
        mix = taps[j][0] * shifted[0]
        for i in range(1, 4):
            mix = mix + taps[j][i] * shifted[i]
        gate = 1.0 / (1.0 + jnp.exp(-mix))
        act = mix * gate
        slope = gate * (1.0 + mix * (1.0 - gate))
        if j < 2:
            norm = 1.0 / jnp.sqrt(jnp.sum(act * act, axis=1, keepdims=True) + 1e-6)
            QK[j] = act * norm
            DS[j] = slope * norm
        else:
            QK[j] = act
            DS[j] = slope

    blk = [slice(D * b, D * (b + 1)) for b in range(2)]
    systems, scores = [], []
    for b in range(2):
        q, k = QK[0, blk[b], :], QK[1, blk[b], :]
        kf, kb, qf = k * EX[b, 0], k * EX[b, 1], q * EX[b, 0]
        FB[b, 0:D, :] = kf
        FB[b, D : 2 * D, :] = qf
        FB[b, 2 * D : 3 * D, :] = kb
        both = mm_nt(jnp.concatenate([kf, qf], axis=0), kb)
        systems.append(jnp.where(strict, XB[b, 3] * both[:D], 0.0))
        scores.append(jnp.where(incl, both[D:], 0.0))
    inverses = unit_lower_inverse(systems)
    wus, kes = [], []
    for b in range(2):
        k, v, beta = QK[1, blk[b], :], QK[2, blk[b], :], XB[b, 3]
        ke = k * EX[b, 3]
        wu = mm(inverses[b], jnp.concatenate([beta * k * EX[b, 2], beta * v], axis=1))
        MAPS[b, 0] = jnp.where(r == c, jnp.exp(fins[b]), 0.0) - mm_tn(ke, wu[:, :D])
        wus.append(wu)
        kes.append(ke)
    t0, t1 = MAPS[0, 0], MAPS[1, 0]
    TS[z] = mm(t1, t0)

    def root_at(j):
        return at_z(2 * j + core)

    def map_send(dj):
        j = lax.rem(rank + dj, roots)
        return copy_to(TS.at[z], TS.at[z], ring_s.at[dj], ring_r.at[z], sec, root_at(j))

    def part_send(dj):
        j = lax.rem(rank + dj, roots)
        return copy_to(VS.at[j], VR.at[z], vec_s.at[dj], vec_r.at[z], sec, root_at(j))

    def all_roots(send, act):
        for dj in sorted(range(1, roots), key=lambda dj: abs(2 * dj - roots)):
            act(send(dj))

        @pl.when(jnp.logical_not(is_root))
        def _():
            act(send(0))

    all_roots(map_send, lambda copy: copy.start())

    for b in range(2):
        q, d_out, sc = QK[0, blk[b], :], XB[b, 1], scores[b]
        w, u = wus[b][:, :D], wus[b][:, D:]
        swu = mm(sc, wus[b])
        qeff = q * EX[b, 2] - swu[:, :D]
        WQ[b, 0:D, :] = w
        WQ[b, D : 2 * D, :] = qeff
        UO[b, 0] = u
        UO[b, 1] = swu[:, D:]
        MAPS[b, 1] = mm_tn(u, kes[b])
        MAPS[b, 2] = mm_tn(d_out, qeff)
    i_pair = mm_nt(MAPS[0, 1], t1) + MAPS[1, 1]
    s_pair = MAPS[0, 2] + mm(MAPS[1, 2], t0)
    for j in range(roots):
        VS[j, 0] = i_pair[j * cols : (j + 1) * cols]
        VS[j, 1] = s_pair[j * cols : (j + 1) * cols]
    all_roots(part_send, lambda copy: copy.start())

    for b in range(2):
        h = mm_tn(scores[b], XB[b, 1])
        zk = mm_tn(inverses[b], jnp.concatenate([h, kes[b]], axis=1))
        ZK[b, 0] = zk[:, :D]
        ZK[b, 1] = zk[:, D:]
    DM[:, 0:8, :] = jnp.zeros((3, 8, D), F32)
    DM[:, 8 + 2 * D :, :] = jnp.zeros((3, 8, D), F32)
    eye = jnp.where(r == c, 1.0, 0.0).astype(F32)
    mine = pl.ds(pl.multiple_of(rank * cols, cols), cols)

    def ends_send(dy):
        return copy_to(XY.at[y], XY.at[y], ya_s.at[dy], ya_r.at[n_y - dy], sec, at_y(lax.rem(y + dy, n_y)))

    def total_send(yy, dy):
        slot = PY.at[yy - 1]
        return copy_to(slot, slot, yb_s.at[dy], yb_r.at[yy], sec, at_y(lax.rem(y + dy, n_y)))

    def slice_send(dz):
        to = lax.rem(z + dz, n_z)
        return copy_to(SS.at[to], ST.at[:, mine], sg_s.at[dz], sg_r.at[rank], sec, at_z(to))

    @pl.when(is_root)
    def _():
        VR[z] = VS[rank]
        for dz in range(1, n_z):
            zz = lax.rem(z + dz, n_z)
            arrives(TS.at[zz], ring_r.at[zz])
            arrives(VR.at[zz], vec_r.at[zz])
        none = jnp.zeros((D, D), F32)
        UP[0] = jnp.concatenate([jnp.zeros((cols, D), F32), eye], axis=0)
        DN[n_z - 1] = UP[0]
        up = jnp.concatenate([VR[0, 0], jnp.transpose(TS[0])], axis=0)
        down = jnp.concatenate([VR[n_z - 1, 1], TS[n_z - 1]], axis=0)
        for step in range(1, n_z):
            zu, zd = step, n_z - 1 - step
            UP[zu] = up
            DN[zd] = down
            up = mm_nt(up, TS[zu]) + jnp.concatenate([VR[zu, 0], none], axis=0)
            down = mm(down, TS[zd]) + jnp.concatenate([VR[zd, 1], none], axis=0)
        for yy in range(1, n_y - 1):
            @pl.when(y == yy)
            def _():
                PY[yy - 1] = up[cols:]
                for dy in sorted(range(1, n_y), key=lambda dy: abs(2 * dy - n_y)):
                    total_send(yy, dy).start()
        XY[y, 0] = up[:cols]
        XY[y, 1] = down[:cols]
        for dy in sorted(range(1, n_y), key=lambda dy: abs(2 * dy - n_y)):
            ends_send(dy).start()

        for dy in range(1, n_y):
            arrives(XY.at[lax.rem(y + dy, n_y)], ya_r.at[dy])
        for yy in range(1, n_y - 1):
            @pl.when(y != yy)
            def _():
                arrives(PY.at[yy - 1], yb_r.at[yy])
        enter = jnp.where(y > 0, XY[0, 0], 0.0)
        leave = jnp.where(y < n_y - 1, XY[n_y - 1, 1], 0.0)
        for step in range(1, n_y - 1):
            yu, yd = step, n_y - 1 - step
            enter = jnp.where(y > yu, mm(enter, PY[yu - 1]) + XY[yu, 0], enter)
            leave = jnp.where(y < yd, mm_nt(leave, PY[yd - 1]) + XY[yd, 1], leave)

        for dz in sorted(range(n_z), key=lambda dz: (dz == 0, abs(2 * dz - n_z))):
            zz = lax.rem(z + dz, n_z)
            SS[zz, 0] = UP[zz, :cols, :] + mm(enter, UP[zz, cols:, :])
            SS[zz, 1] = DN[zz, :cols, :] + mm(leave, DN[zz, cols:, :])
            if dz:
                slice_send(dz).start()
        ST[:, mine, :] = SS[z]

    for dj in range(roots):
        j = lax.rem(rank + dj, roots)
        theirs = ST.at[:, pl.ds(pl.multiple_of(j * cols, cols), cols)]
        if dj:
            arrives(theirs, sg_r.at[j])
        else:
            @pl.when(jnp.logical_not(is_root))
            def _():
                arrives(theirs, sg_r.at[j])

    starts = [ST[0], None]
    ends = [None, ST[1]]
    starts[1] = mm_nt(starts[0], t0) + MAPS[0, 1]
    ends[0] = mm(ends[1], t1) + MAPS[1, 2]
    for b in range(2):
        q, k = QK[0, blk[b], :], QK[1, blk[b], :]
        beta, d_out = XB[b, 3], XB[b, 1]
        wq = mm_nt(WQ[b], starts[b])
        fresh = UO[b, 0] - wq[:D]
        OB[b] = UO[b, 1] + wq[D:]
        zeta = ZK[b, 0] + mm_nt(ZK[b, 1], ends[b])
        pair = mm_nt(jnp.concatenate([d_out, zeta], axis=0), fresh)
        d_sc = jnp.where(incl, pair[:D], 0.0)
        d_p = beta * jnp.where(strict, -pair[D:], 0.0)
        dz_s = mm(jnp.concatenate([d_out, zeta], axis=0), starts[b])
        f_g = mm(fresh, ends[b])
        by_kb = mm(jnp.concatenate([d_sc, d_p], axis=0), FB[b, 2 * D : 3 * D, :])
        d_kb = mm_tn(jnp.concatenate([d_p, d_sc], axis=0), FB[b, 0 : 2 * D, :])
        dq = EX[b, 2] * dz_s[:D] + EX[b, 0] * by_kb[:D]
        dk = EX[b, 3] * f_g - beta * EX[b, 2] * dz_s[D:] + EX[b, 0] * by_kb[D:] + EX[b, 1] * d_kb
        for j, (unit, grad) in enumerate(((q, dq), (k, dk))):
            along = jnp.sum(unit * grad, axis=1, keepdims=True)
            DM[j, 8 + D * b : 8 + D * (b + 1), :] = (grad - unit * along) * DS[j, blk[b], :]
        DM[2, 8 + D * b : 8 + D * (b + 1), :] = beta * zeta * DS[2, blk[b], :]
    go(OB.at[1 - core], OR, one_s.at[1], one_r.at[1], sec, partner)

    d_norm = jnp.zeros((2 * D + 8, D), F32)
    for j in range(3):
        for i in range(4):
            d_norm = d_norm + taps[j][i] * DM[j, 3 - i : 3 - i + 2 * D + 8, :]
    GB[0] = d_norm[8 : 8 + D]
    GB[1] = d_norm[8 + D :]
    GRIM[2] = d_norm[:8]
    TB[2] = row_sums(jnp.concatenate([jnp.zeros((D - 8, D), F32), d_norm[:8] * RIMR[...]], axis=0))
    TB[0] = row_sums(d_norm[8 : 8 + D] * XB[0, 0])
    TB[1] = row_sums(d_norm[8 + D :] * XB[1, 0])

    for ds, dc in peers:
        back = ((sections - ds) % sections) * 2 + dc
        go(TB.at[1 - core if dc else core], R2.at[back], row2_s.at[ds * 2 + dc], row2_r.at[back],
           side(ds), partner if dc else ctx)

    def rim_back_copies():
        made = [copy_to(GRIM.at[2], GRIM.at[core], rim2_s.at[sections], rim2_r.at[2 * sections + core], sec, before_tail)]
        for ds in range(sections):
            slot = 2 * ((sections - ds) % sections) + core
            made.append(copy_to(TB.at[2], RIM2.at[slot], rim2_s.at[ds], rim2_r.at[slot], side(ds), before_tail))
        return made

    @pl.when(has_before)
    def _():
        for copy in rim_back_copies():
            copy.start()

    go(GB.at[1 - core], GR, one_s.at[2], one_r.at[2], sec, partner)

    def joined(own, oth):
        return jnp.concatenate([jnp.where(first, own, oth), jnp.where(first, oth, own)], axis=1)

    arrives(OR, one_r.at[1])
    x_wide = x_ref[...].astype(F32)
    out_ref[...] = (x_wide + joined(OB[core], OR[...])).astype(BF16)
    arrives(GR, one_r.at[2])
    scale = SC[core]
    wide_scale = jnp.concatenate([scale, scale], axis=1)
    FIN[...] = do_ref[...].astype(F32) + joined(GB[core], GR[...]) * wide_scale

    for ds, dc in peers:
        slot = ds * 2 + dc
        arrives(R2.at[slot], row2_r.at[slot])
    inner = TB[core]
    for slot in range(1, 2 * sections):
        inner = inner + R2[slot]
    RT2[0] = inner

    @pl.when(feeds)
    def _():
        for slot in range(2 * sections):
            arrives(RIM2.at[slot], rim2_r.at[slot])
        for n in range(2):
            arrives(GRIM.at[n], rim2_r.at[2 * sections + n])
        total = RT2[0]
        for slot in range(2 * sections):
            total = total + RIM2[slot]
        RT2[0] = total
        late = jnp.concatenate([GRIM[0], GRIM[1]], axis=1)
        FIN[D - 8 :, :] = FIN[D - 8 :, :] + late * jnp.concatenate([SC[core, D - 8 :, :]] * 2, axis=1)

    coef = as_columns(scale_same * scale_same * scale_same * RT2[0] / width_all)
    dx_ref[...] = (FIN[...] - x_wide * jnp.concatenate([coef, coef], axis=1)).astype(BF16)

    for copy in sent:
        copy.wait_send()

    @pl.when(feeds)
    def _():
        for copy in rim_copies():
            copy.wait_send()

    @pl.when(has_before)
    def _():
        for copy in rim_back_copies():
            copy.wait_send()

    all_roots(map_send, lambda copy: copy.wait_send())
    all_roots(part_send, lambda copy: copy.wait_send())

    @pl.when(is_root)
    def _():
        for dy in range(1, n_y):
            ends_send(dy).wait_send()
        for dz in range(1, n_z):
            slice_send(dz).wait_send()
        for yy in range(1, n_y - 1):
            @pl.when(y == yy)
            def _():
                for dy in range(1, n_y):
                    total_send(yy, dy).wait_send()


def solution(mesh):
    sections, n_ctx = mesh.shape["section"], mesh.shape["ctx"]
    n_y, n_z = (4, 8) if n_ctx == 64 else (2, n_ctx // 4)
    roots = n_z // 2
    cols = D // roots
    dma = lambda n: pltpu.SemaphoreType.DMA((n,))

    def shards(inputs, out_grads, conv_weight, log_decay, beta):
        width_all = float(inputs.shape[1] * sections)
        v = lambda *s: pltpu.VMEM(s, F32)
        scratch = [
            pltpu.VMEM((D, 2 * D), BF16), pltpu.VMEM((D, 2 * D), BF16), v(D, 2 * D), v(2, D), v(3, 4, 2 * D),
            v(4, D, D), v(2, 4, D, D), v(2 * sections, 8, D), v(2 * sections, 8, D), v(3, 8, D),
            v(2 * D + 8, D), v(sections, 8, D), v(8, D), v(2, D, D), v(3, 8, D), v(2 * sections, 8, D), v(2, 8, D),
            v(3, 2 * D, D), v(3, 2 * D, D), v(2, 4, D, D), v(2, 3 * D, D), v(2, 2 * D, D), v(2, 2, D, D),
            v(2, 2, D, D), v(2, 3, D, D), v(n_z, D, D), v(roots, 2, cols, D), v(n_z, 2, cols, D),
            v(n_z, cols + D, D), v(n_z, cols + D, D), v(n_y, 2, cols, D),
            v(max(n_y - 2, 1), D, D), v(n_z, 2, cols, D), v(2, D, D), v(3, 2 * D + 16, D),
            v(2, D, D), v(D, D), v(2, D, D), v(D, D), v(D, 2 * D), v(1, 8, D),
            dma(5), dma(2 * sections), dma(2 * sections), dma(2 * sections + 2), dma(sections + 1),
            dma(2 * sections), dma(2 * sections), dma(sections + 1), dma(2 * sections + 2), dma(3), dma(3),
            dma(roots), dma(n_z), dma(roots), dma(n_z), dma(n_z), dma(roots),
            dma(n_y), dma(n_y), dma(n_y), dma(n_y),
        ]
        vm = pl.BlockSpec(memory_space=pltpu.VMEM)
        hbm = pl.BlockSpec(memory_space=pltpu.MemorySpace.HBM)
        return pl.pallas_call(
            functools.partial(kernel, (sections, n_y, n_z, width_all)),
            out_shape=(jax.ShapeDtypeStruct(inputs.shape, BF16), jax.ShapeDtypeStruct(inputs.shape, BF16)),
            in_specs=[hbm] * 5,
            out_specs=(vm, vm),
            scratch_shapes=scratch,
            compiler_params=pltpu.CompilerParams(
                collective_id=0, has_side_effects=True, vmem_limit_bytes=40 * 2**20
            ),
        )(*[pltpu.with_memory_space_constraint(a, pltpu.MemorySpace.HBM) for a in (inputs, out_grads, log_decay, beta.T, conv_weight)])

    spec = P("ctx", "section")
    return jax.shard_map(
        shards, mesh=mesh, in_specs=(spec, spec, P(None, None, "section"), spec, spec),
        out_specs=(spec, spec), check_vma=False,
    )
```

```python
import functools

import jax
import jax.numpy as jnp
from jax import lax
from jax.experimental import pallas as pl
from jax.experimental.pallas import tpu as pltpu
from jax.sharding import PartitionSpec as P

MESH = pl.DeviceIdType.MESH
D = 128
F32 = jnp.float32
BF16 = jnp.bfloat16


def split2(a):
    high = a.astype(BF16)
    low = (a - high.astype(F32)).astype(BF16)
    return high, low


def raw_dot(a, b, ca, cb):
    return lax.dot_general(a, b, (((ca,), (cb,)), ((), ())), preferred_element_type=F32)


def mm(a, b, ca=1, cb=0):
    ah, al = split2(a)
    bh, bl = split2(b)
    aa = jnp.concatenate([ah, al], axis=ca)
    bb = jnp.concatenate([jnp.concatenate([bh, bh], axis=cb), jnp.concatenate([bl, bl], axis=cb)], axis=1 - cb)
    wide = raw_dot(aa, bb, ca, cb)
    n = b.shape[1 - cb]
    return wide[:, :n] + wide[:, n:]


def mm_nt(a, b):
    return mm(a, b, 1, 1)


def mm_tn(a, b):
    return mm(a, b, 0, 0)


def iota2(shape, axis):
    return lax.broadcasted_iota(jnp.int32, shape, axis)


def row_sums(values):
    high, low = split2(values)
    ones = jnp.ones((8, values.shape[1]), BF16)
    return raw_dot(ones, high, 1, 1) + raw_dot(ones, low, 1, 1)


def as_columns(tile):
    return jnp.transpose(jnp.broadcast_to(tile[0:1], (D, D)))


def unit_lower_inverse(strict_parts):
    r, c = iota2((D, D), 0), iota2((D, D), 1)
    eye = jnp.where(r == c, 1.0, 0.0).astype(F32)
    inverse = None
    for k in range(7):
        mask = ((r >> (k + 1)) == (c >> (k + 1))) & (((r >> k) & 1) == 1) & (((c >> k) & 1) == 0)
        off = [jnp.where(mask, a, 0.0) for a in strict_parts]
        if k == 0:
            inverse = [eye - o for o in off]
        else:
            half = [mm(m, o) for m, o in zip(inverse, off)]
            if k == 6:
                return inverse, half
            inverse = [m - mm(h, m) for h, m in zip(half, inverse)]


def kernel(geom, x_hbm, do_hbm, g_hbm, beta_hbm, w_hbm, out_ref, dx_ref, *scratch):
    sections, n_y, n_z, width_all = geom
    (
        x_ref, do_ref, g_ref, beta_ref, w_ref,
        SB, XB, R, R2, TB, NP, RIM, RIMR, SC, GRIM, RIM2, RT,
        QK, DS, EX, FB, WQ, UO, ZK, MAPS, TS, VS, VR, UP, DN, XY, PY, SS, ST, DM, OB, OR, GB, GR, FIN, RT2,
        in_s, row_s, row_r, rim_s, rim_r, row2_s, row2_r, rim2_s, rim2_r, one_s, one_r,
        ring_s, ring_r, vec_s, vec_r, sg_s, sg_r, ya_s, ya_r, yb_s, yb_r,
    ) = scratch
    n_ctx = n_y * n_z * 2
    n_chip = n_y * n_z
    roots = n_z // 2
    cols = D // roots
    sec = lax.axis_index("section")
    ctx = lax.axis_index("ctx")
    core = lax.rem(ctx, 2)
    chip = ctx // 2
    y = chip // n_z
    z = lax.rem(chip, n_z)
    partner = ctx + 1 - 2 * core
    first = core == 0
    rank = z // 2
    is_root = lax.rem(z, 2) == core
    has_before = chip > 0
    has_after = chip < n_chip - 1
    feeds = jnp.logical_and(core == 1, has_after)
    after_chip = 2 * lax.rem(chip + 1, n_chip)
    before_tail = 2 * lax.rem(chip + n_chip - 1, n_chip) + 1

    def at_z(zz):
        return y * (2 * n_z) + zz * 2 + core

    def at_y(yy):
        return yy * (2 * n_z) + z * 2 + core

    def side(ds):
        return lax.rem(sec + ds, sections)

    def copy_to(src, dst, ss, rs, to_sec, to_ctx):
        return pltpu.make_async_remote_copy(
            src_ref=src, dst_ref=dst, send_sem=ss, recv_sem=rs,
            device_id=(to_sec, to_ctx), device_id_type=MESH,
        )

    def arrives(dst, rs):
        copy_to(dst, dst, one_s.at[0], rs, sec, partner).wait_recv()

    sent = []

    def go(*args):
        copy = copy_to(*args)
        copy.start()
        sent.append(copy)

    peers = [(ds, dc) for ds in range(sections) for dc in range(2) if ds or dc]
    peers.sort(key=lambda p: abs(p[0] - sections // 2))

    barrier = pltpu.get_barrier_semaphore()

    def greet(to_sec, to_ctx):
        pl.semaphore_signal(barrier, inc=1, device_id=(to_sec, to_ctx), device_id_type=MESH)

    @pl.when(has_before)
    def _():
        for ds in range(sections):
            greet(side(ds), before_tail)

    @pl.when(feeds)
    def _():
        for ds in range(sections):
            for dc in range(2):
                greet(side(ds), after_chip + dc)

    for ds, dc in peers:
        greet(side(ds), partner if dc else ctx)
    for dz in range(1, n_z):
        greet(sec, at_z(lax.rem(z + dz, n_z)))
    for dy in range(1, n_y):
        greet(sec, at_y(lax.rem(y + dy, n_y)))

    greeted = (
        len(peers) + n_z - 1 + n_y - 1
        + sections * has_before.astype(jnp.int32) + 2 * sections * feeds.astype(jnp.int32)
    )

    loads = [
        pltpu.make_async_copy(src, dst, in_s.at[n])
        for n, (src, dst) in enumerate(
            ((x_hbm, x_ref), (do_hbm, do_ref), (g_hbm, g_ref), (beta_hbm, beta_ref), (w_hbm, w_ref))
        )
    ]
    for load in loads:
        load.start()

    for load in loads:
        load.wait()

    def halves(ref):
        whole = ref[...].astype(F32)
        low, high = whole[:, :D], whole[:, D:]
        return jnp.where(first, low, high), jnp.where(first, high, low), whole

    x_own, x_oth, x_all = halves(x_ref)
    R[0] = row_sums(x_all * x_all)[0:1]
    d_own, d_oth, _ = halves(do_ref)
    g_own, g_oth, _ = halves(g_ref)
    b0, b1 = as_columns(beta_ref[0:1, :]), as_columns(beta_ref[1:2, :])
    SB[0] = x_oth
    SB[1] = d_oth
    SB[2] = g_oth
    SB[3] = jnp.where(first, b1, b0)
    XB[core, 0] = x_own
    XB[core, 1] = d_own
    XB[core, 2] = g_own
    XB[core, 3] = jnp.where(first, b0, b1)
    RT[0] = x_all[D - 8 :, :D]
    RT[1] = x_all[D - 8 :, D:]
    pl.semaphore_wait(barrier, greeted)

    for ds, dc in peers:
        back = ((sections - ds) % sections) * 2 + dc
        go(R.at[0], R.at[back], row_s.at[ds * 2 + dc], row_r.at[back], side(ds), partner if dc else ctx)
    go(SB, XB.at[core], one_s.at[0], one_r.at[0], sec, partner)

    def rim_copies():
        made = []
        for dc in range(2):
            made.append(copy_to(RT.at[dc], RIMR, rim_s.at[2 * sections + dc], rim_r.at[sections], sec, after_chip + dc))
            for ds in range(sections):
                made.append(copy_to(R.at[0], RIM.at[(sections - ds) % sections], rim_s.at[2 * ds + dc],
                                    rim_r.at[(sections - ds) % sections], side(ds), after_chip + dc))
        return made

    @pl.when(feeds)
    def _():
        for copy in rim_copies():
            copy.start()

    arrives(XB.at[1 - core], one_r.at[0])
    r, c = iota2((D, D), 0), iota2((D, D), 1)
    incl = r >= c
    strict = r > c
    lower = jnp.where(incl, 1.0, 0.0).astype(BF16)
    fins = []
    for b in range(2):
        g = XB[b, 2]
        gh = g.astype(BF16)
        rest = g - gh.astype(F32)
        gm = rest.astype(BF16)
        gl = (rest - gm.astype(F32)).astype(BF16)
        cum = raw_dot(lower, gh, 1, 0) + (raw_dot(lower, gm, 1, 0) + raw_dot(lower, gl, 1, 0))
        mid = cum[D // 2 : D // 2 + 1]
        fin = cum[D - 1 : D]
        EX[b, 0] = jnp.exp(cum - mid)
        EX[b, 1] = jnp.exp(mid - cum)
        EX[b, 2] = jnp.exp(cum)
        EX[b, 3] = jnp.exp(fin - cum)
        fins.append(fin)

    for ds, dc in peers:
        slot = ds * 2 + dc
        arrives(R.at[slot], row_r.at[slot])
    same = R[0]
    other = R[1]
    for ds in range(1, sections):
        same = same + R[2 * ds]
        other = other + R[2 * ds + 1]

    def scale_of(total):
        return 1.0 / jnp.sqrt(total / width_all + 1e-5)

    scale_same = scale_of(same)
    SC[core] = as_columns(scale_same)
    SC[1 - core] = as_columns(scale_of(other))
    for b in range(2):
        NP[8 + D * b : 8 + D * (b + 1), :] = XB[b, 0] * SC[b]

    @pl.when(has_before)
    def _():
        for ds in range(sections):
            arrives(RIM.at[ds], rim_r.at[ds])
        arrives(RIMR, rim_r.at[sections])
        rim_total = RIM[0]
        for ds in range(1, sections):
            rim_total = rim_total + RIM[ds]
        NP[0:8, :] = RIMR[...] * as_columns(scale_of(rim_total))[D - 8 :]

    @pl.when(jnp.logical_not(has_before))
    def _():
        NP[0:8, :] = jnp.zeros((8, D), F32)
        RIMR[...] = jnp.zeros((8, D), F32)

    def tap(j, i):
        both = w_ref[j, i : i + 1, :]
        return jnp.where(first, both[:, :D], both[:, D:])

    taps = [[tap(j, i) for i in range(4)] for j in range(3)]
    shifted = [NP[5 + i : 5 + i + 2 * D, :] for i in range(4)]
    for j in range(3):
        mix = taps[j][0] * shifted[0]
        for i in range(1, 4):
            mix = mix + taps[j][i] * shifted[i]
        gate = 1.0 / (1.0 + jnp.exp(-mix))
        act = mix * gate
        slope = gate * (1.0 + mix * (1.0 - gate))
        if j < 2:
            norm = 1.0 / jnp.sqrt(jnp.sum(act * act, axis=1, keepdims=True) + 1e-6)
            QK[j] = act * norm
            DS[j] = slope * norm
        else:
            QK[j] = act
            DS[j] = slope

    blk = [slice(D * b, D * (b + 1)) for b in range(2)]
    systems, scores = [], []
    for b in range(2):
        q, k = QK[0, blk[b], :], QK[1, blk[b], :]
        kf, kb, qf = k * EX[b, 0], k * EX[b, 1], q * EX[b, 0]
        FB[b, 0:D, :] = kf
        FB[b, D : 2 * D, :] = qf
        FB[b, 2 * D : 3 * D, :] = kb
        both = mm_nt(jnp.concatenate([kf, qf], axis=0), kb)
        systems.append(jnp.where(strict, XB[b, 3] * both[:D], 0.0))
        scores.append(jnp.where(incl, both[D:], 0.0))
    inverses, halved = unit_lower_inverse(systems)
    wus, kes = [], []
    for b in range(2):
        k, v, beta = QK[1, blk[b], :], QK[2, blk[b], :], XB[b, 3]
        ke = k * EX[b, 3]
        wu = mm(inverses[b], jnp.concatenate([beta * k * EX[b, 2], beta * v], axis=1))
        wu = wu - mm(halved[b], wu)
        MAPS[b, 0] = jnp.where(r == c, jnp.exp(fins[b]), 0.0) - mm_tn(ke, wu[:, :D])
        wus.append(wu)
        kes.append(ke)
    t0, t1 = MAPS[0, 0], MAPS[1, 0]
    TS[z] = mm(t1, t0)

    def root_at(j):
        return at_z(2 * j + core)

    def map_send(dj):
        j = lax.rem(rank + dj, roots)
        return copy_to(TS.at[z], TS.at[z], ring_s.at[dj], ring_r.at[z], sec, root_at(j))

    def part_send(dj):
        j = lax.rem(rank + dj, roots)
        return copy_to(VS.at[j], VR.at[z], vec_s.at[dj], vec_r.at[z], sec, root_at(j))

    def all_roots(send, act):
        for dj in sorted(range(1, roots), key=lambda dj: abs(2 * dj - roots)):
            act(send(dj))

        @pl.when(jnp.logical_not(is_root))
        def _():
            act(send(0))

    all_roots(map_send, lambda copy: copy.start())

    for b in range(2):
        q, d_out, sc = QK[0, blk[b], :], XB[b, 1], scores[b]
        w, u = wus[b][:, :D], wus[b][:, D:]
        swu = mm(sc, wus[b])
        qeff = q * EX[b, 2] - swu[:, :D]
        WQ[b, 0:D, :] = w
        WQ[b, D : 2 * D, :] = qeff
        UO[b, 0] = u
        UO[b, 1] = swu[:, D:]
        MAPS[b, 1] = mm_tn(u, kes[b])
        MAPS[b, 2] = mm_tn(d_out, qeff)
    i_pair = mm_nt(MAPS[0, 1], t1) + MAPS[1, 1]
    s_pair = MAPS[0, 2] + mm(MAPS[1, 2], t0)
    for j in range(roots):
        VS[j, 0] = i_pair[j * cols : (j + 1) * cols]
        VS[j, 1] = s_pair[j * cols : (j + 1) * cols]
    all_roots(part_send, lambda copy: copy.start())

    for b in range(2):
        h = mm_tn(scores[b], XB[b, 1])
        zk = mm_tn(inverses[b] - mm(halved[b], inverses[b]), jnp.concatenate([h, kes[b]], axis=1))
        ZK[b, 0] = zk[:, :D]
        ZK[b, 1] = zk[:, D:]
    WS = WQ[1]
    by_start = mm_nt(WS, MAPS[0, 1])
    UO[1, 0] = UO[1, 0] - by_start[:D]
    UO[1, 1] = UO[1, 1] + by_start[D:]
    WQ[1] = mm(WS, t0)
    KS = ZK[0, 1]
    ZK[0, 0] = ZK[0, 0] + mm_nt(KS, MAPS[1, 2])
    ZK[0, 1] = mm_nt(KS, t1)
    DM[:, 0:8, :] = jnp.zeros((3, 8, D), F32)
    DM[:, 8 + 2 * D :, :] = jnp.zeros((3, 8, D), F32)
    eye = jnp.where(r == c, 1.0, 0.0).astype(F32)
    mine = pl.ds(pl.multiple_of(rank * cols, cols), cols)

    def ends_send(dy):
        return copy_to(XY.at[y], XY.at[y], ya_s.at[dy], ya_r.at[n_y - dy], sec, at_y(lax.rem(y + dy, n_y)))

    def total_send(yy, dy):
        slot = PY.at[yy - 1]
        return copy_to(slot, slot, yb_s.at[dy], yb_r.at[yy], sec, at_y(lax.rem(y + dy, n_y)))

    def slice_send(dz):
        to = lax.rem(z + dz, n_z)
        return copy_to(SS.at[to], ST.at[:, mine], sg_s.at[dz], sg_r.at[rank], sec, at_z(to))

    @pl.when(is_root)
    def _():
        VR[z] = VS[rank]
        for dz in range(1, n_z):
            zz = lax.rem(z + dz, n_z)
            arrives(TS.at[zz], ring_r.at[zz])
            arrives(VR.at[zz], vec_r.at[zz])
        none = jnp.zeros((D, D), F32)
        UP[0] = jnp.concatenate([jnp.zeros((cols, D), F32), eye], axis=0)
        DN[n_z - 1] = UP[0]
        up = jnp.concatenate([VR[0, 0], jnp.transpose(TS[0])], axis=0)
        down = jnp.concatenate([VR[n_z - 1, 1], TS[n_z - 1]], axis=0)
        for step in range(1, n_z):
            zu, zd = step, n_z - 1 - step
            UP[zu] = up
            DN[zd] = down
            up = mm_nt(up, TS[zu]) + jnp.concatenate([VR[zu, 0], none], axis=0)
            down = mm(down, TS[zd]) + jnp.concatenate([VR[zd, 1], none], axis=0)
        for yy in range(1, n_y - 1):
            @pl.when(y == yy)
            def _():
                PY[yy - 1] = up[cols:]
                for dy in sorted(range(1, n_y), key=lambda dy: abs(2 * dy - n_y)):
                    total_send(yy, dy).start()
        XY[y, 0] = up[:cols]
        XY[y, 1] = down[:cols]
        for dy in sorted(range(1, n_y), key=lambda dy: abs(2 * dy - n_y)):
            ends_send(dy).start()

        for dy in range(1, n_y):
            arrives(XY.at[lax.rem(y + dy, n_y)], ya_r.at[dy])
        for yy in range(1, n_y - 1):
            @pl.when(y != yy)
            def _():
                arrives(PY.at[yy - 1], yb_r.at[yy])
        enter = jnp.where(y > 0, XY[0, 0], 0.0)
        leave = jnp.where(y < n_y - 1, XY[n_y - 1, 1], 0.0)
        for step in range(1, n_y - 1):
            yu, yd = step, n_y - 1 - step
            enter = jnp.where(y > yu, mm(enter, PY[yu - 1]) + XY[yu, 0], enter)
            leave = jnp.where(y < yd, mm_nt(leave, PY[yd - 1]) + XY[yd, 1], leave)

        for dz in sorted(range(n_z), key=lambda dz: (dz == 0, abs(2 * dz - n_z))):
            zz = lax.rem(z + dz, n_z)
            SS[zz, 0] = UP[zz, :cols, :] + mm(enter, UP[zz, cols:, :])
            SS[zz, 1] = DN[zz, :cols, :] + mm(leave, DN[zz, cols:, :])
            if dz:
                slice_send(dz).start()
        ST[:, mine, :] = SS[z]

    for dj in range(roots):
        j = lax.rem(rank + dj, roots)
        theirs = ST.at[:, pl.ds(pl.multiple_of(j * cols, cols), cols)]
        if dj:
            arrives(theirs, sg_r.at[j])
        else:
            @pl.when(jnp.logical_not(is_root))
            def _():
                arrives(theirs, sg_r.at[j])

    starts = [ST[0], None]
    ends = [None, ST[1]]
    starts[1] = mm_nt(starts[0], t0) + MAPS[0, 1]
    ends[0] = mm(ends[1], t1) + MAPS[1, 2]
    for b in range(2):
        q, k = QK[0, blk[b], :], QK[1, blk[b], :]
        beta, d_out = XB[b, 3], XB[b, 1]
        wq = mm_nt(WQ[b], starts[0])
        fresh = UO[b, 0] - wq[:D]
        OB[b] = UO[b, 1] + wq[D:]
        zeta = ZK[b, 0] + mm_nt(ZK[b, 1], ends[1])
        pair = mm_nt(jnp.concatenate([d_out, zeta], axis=0), fresh)
        d_sc = jnp.where(incl, pair[:D], 0.0)
        d_p = beta * jnp.where(strict, -pair[D:], 0.0)
        dz_s = mm(jnp.concatenate([d_out, zeta], axis=0), starts[b])
        f_g = mm(fresh, ends[b])
        by_kb = mm(jnp.concatenate([d_sc, d_p], axis=0), FB[b, 2 * D : 3 * D, :])
        d_kb = mm_tn(jnp.concatenate([d_p, d_sc], axis=0), FB[b, 0 : 2 * D, :])
        dq = EX[b, 2] * dz_s[:D] + EX[b, 0] * by_kb[:D]
        dk = EX[b, 3] * f_g - beta * EX[b, 2] * dz_s[D:] + EX[b, 0] * by_kb[D:] + EX[b, 1] * d_kb
        for j, (unit, grad) in enumerate(((q, dq), (k, dk))):
            along = jnp.sum(unit * grad, axis=1, keepdims=True)
            DM[j, 8 + D * b : 8 + D * (b + 1), :] = (grad - unit * along) * DS[j, blk[b], :]
        DM[2, 8 + D * b : 8 + D * (b + 1), :] = beta * zeta * DS[2, blk[b], :]
    go(OB.at[1 - core], OR, one_s.at[1], one_r.at[1], sec, partner)

    d_norm = jnp.zeros((2 * D + 8, D), F32)
    for j in range(3):
        for i in range(4):
            d_norm = d_norm + taps[j][i] * DM[j, 3 - i : 3 - i + 2 * D + 8, :]
    GB[0] = d_norm[8 : 8 + D]
    GB[1] = d_norm[8 + D :]
    GRIM[2] = d_norm[:8]
    TB[2] = row_sums(jnp.concatenate([jnp.zeros((D - 8, D), F32), d_norm[:8] * RIMR[...]], axis=0))[0:1]
    TB[0] = row_sums(d_norm[8 : 8 + D] * XB[0, 0])[0:1]
    TB[1] = row_sums(d_norm[8 + D :] * XB[1, 0])[0:1]

    for ds, dc in peers:
        back = ((sections - ds) % sections) * 2 + dc
        go(TB.at[1 - core if dc else core], R2.at[back], row2_s.at[ds * 2 + dc], row2_r.at[back],
           side(ds), partner if dc else ctx)

    def rim_back_copies():
        made = [copy_to(GRIM.at[2], GRIM.at[core], rim2_s.at[sections], rim2_r.at[2 * sections + core], sec, before_tail)]
        for ds in range(sections):
            slot = 2 * ((sections - ds) % sections) + core
            made.append(copy_to(TB.at[2], RIM2.at[slot], rim2_s.at[ds], rim2_r.at[slot], side(ds), before_tail))
        return made

    @pl.when(has_before)
    def _():
        for copy in rim_back_copies():
            copy.start()

    go(GB.at[1 - core], GR, one_s.at[2], one_r.at[2], sec, partner)

    def joined(own, oth):
        return jnp.concatenate([jnp.where(first, own, oth), jnp.where(first, oth, own)], axis=1)

    arrives(OR, one_r.at[1])
    x_wide = x_ref[...].astype(F32)
    out_ref[...] = (x_wide + joined(OB[core], OR[...])).astype(BF16)
    arrives(GR, one_r.at[2])
    scale = SC[core]
    wide_scale = jnp.concatenate([scale, scale], axis=1)
    FIN[...] = do_ref[...].astype(F32) + joined(GB[core], GR[...]) * wide_scale

    for ds, dc in peers:
        slot = ds * 2 + dc
        arrives(R2.at[slot], row2_r.at[slot])
    inner = TB[core]
    for slot in range(1, 2 * sections):
        inner = inner + R2[slot]
    RT2[0] = inner

    @pl.when(feeds)
    def _():
        for slot in range(2 * sections):
            arrives(RIM2.at[slot], rim2_r.at[slot])
        for n in range(2):
            arrives(GRIM.at[n], rim2_r.at[2 * sections + n])
        total = RT2[0]
        for slot in range(2 * sections):
            total = total + RIM2[slot]
        RT2[0] = total
        late = jnp.concatenate([GRIM[0], GRIM[1]], axis=1)
        FIN[D - 8 :, :] = FIN[D - 8 :, :] + late * jnp.concatenate([SC[core, D - 8 :, :]] * 2, axis=1)

    coef = as_columns(scale_same * scale_same * scale_same * RT2[0] / width_all)
    dx_ref[...] = (FIN[...] - x_wide * jnp.concatenate([coef, coef], axis=1)).astype(BF16)

    for copy in sent:
        copy.wait_send()

    @pl.when(feeds)
    def _():
        for copy in rim_copies():
            copy.wait_send()

    @pl.when(has_before)
    def _():
        for copy in rim_back_copies():
            copy.wait_send()

    all_roots(map_send, lambda copy: copy.wait_send())
    all_roots(part_send, lambda copy: copy.wait_send())

    @pl.when(is_root)
    def _():
        for dy in range(1, n_y):
            ends_send(dy).wait_send()
        for dz in range(1, n_z):
            slice_send(dz).wait_send()
        for yy in range(1, n_y - 1):
            @pl.when(y == yy)
            def _():
                for dy in range(1, n_y):
                    total_send(yy, dy).wait_send()


def solution(mesh):
    sections, n_ctx = mesh.shape["section"], mesh.shape["ctx"]
    n_y, n_z = (4, 8) if n_ctx == 64 else (2, n_ctx // 4)
    roots = n_z // 2
    cols = D // roots
    dma = lambda n: pltpu.SemaphoreType.DMA((n,))

    def shards(inputs, out_grads, conv_weight, log_decay, beta):
        width_all = float(inputs.shape[1] * sections)
        v = lambda *s: pltpu.VMEM(s, F32)
        scratch = [
            pltpu.VMEM((D, 2 * D), BF16), pltpu.VMEM((D, 2 * D), BF16), v(D, 2 * D), v(2, D), v(3, 4, 2 * D),
            v(4, D, D), v(2, 4, D, D), v(2 * sections, 1, D), v(2 * sections, 1, D), v(3, 1, D),
            v(2 * D + 8, D), v(sections, 1, D), v(8, D), v(2, D, D), v(3, 8, D), v(2 * sections, 1, D), v(2, 8, D),
            v(3, 2 * D, D), v(3, 2 * D, D), v(2, 4, D, D), v(2, 3 * D, D), v(2, 2 * D, D), v(2, 2, D, D),
            v(2, 2, D, D), v(2, 3, D, D), v(n_z, D, D), v(roots, 2, cols, D), v(n_z, 2, cols, D),
            v(n_z, cols + D, D), v(n_z, cols + D, D), v(n_y, 2, cols, D),
            v(max(n_y - 2, 1), D, D), v(n_z, 2, cols, D), v(2, D, D), v(3, 2 * D + 16, D),
            v(2, D, D), v(D, D), v(2, D, D), v(D, D), v(D, 2 * D), v(1, 1, D),
            dma(5), dma(2 * sections), dma(2 * sections), dma(2 * sections + 2), dma(sections + 1),
            dma(2 * sections), dma(2 * sections), dma(sections + 1), dma(2 * sections + 2), dma(3), dma(3),
            dma(roots), dma(n_z), dma(roots), dma(n_z), dma(n_z), dma(roots),
            dma(n_y), dma(n_y), dma(n_y), dma(n_y),
        ]
        vm = pl.BlockSpec(memory_space=pltpu.VMEM)
        hbm = pl.BlockSpec(memory_space=pltpu.MemorySpace.HBM)
        return pl.pallas_call(
            functools.partial(kernel, (sections, n_y, n_z, width_all)),
            out_shape=(jax.ShapeDtypeStruct(inputs.shape, BF16), jax.ShapeDtypeStruct(inputs.shape, BF16)),
            in_specs=[hbm] * 5,
            out_specs=(vm, vm),
            scratch_shapes=scratch,
            compiler_params=pltpu.CompilerParams(
                collective_id=0, has_side_effects=True, vmem_limit_bytes=40 * 2**20
            ),
        )(*[pltpu.with_memory_space_constraint(a, pltpu.MemorySpace.HBM) for a in (inputs, out_grads, log_decay, beta.T, conv_weight)])

    spec = P("ctx", "section")
    return jax.shard_map(
        shards, mesh=mesh, in_specs=(spec, spec, P(None, None, "section"), spec, spec),
        out_specs=(spec, spec), check_vma=False,
    )
```

```python
import functools

import jax
import jax.numpy as jnp
from jax import lax
from jax.experimental import pallas as pl
from jax.experimental.pallas import tpu as pltpu
from jax.sharding import PartitionSpec as P

MESH = pl.DeviceIdType.MESH
D = 128
F32 = jnp.float32
BF16 = jnp.bfloat16


def split2(a):
    high = a.astype(BF16)
    low = (a - high.astype(F32)).astype(BF16)
    return high, low


def raw_dot(a, b, ca, cb):
    return lax.dot_general(a, b, (((ca,), (cb,)), ((), ())), preferred_element_type=F32)


def mm(a, b, ca=1, cb=0):
    ah, al = split2(a)
    bh, bl = split2(b)
    aa = jnp.concatenate([ah, al], axis=ca)
    bb = jnp.concatenate([jnp.concatenate([bh, bh], axis=cb), jnp.concatenate([bl, bl], axis=cb)], axis=1 - cb)
    wide = raw_dot(aa, bb, ca, cb)
    n = b.shape[1 - cb]
    return wide[:, :n] + wide[:, n:]


def mm_nt(a, b):
    return mm(a, b, 1, 1)


def mm_tn(a, b):
    return mm(a, b, 0, 0)


def iota2(shape, axis):
    return lax.broadcasted_iota(jnp.int32, shape, axis)


def row_sums(values):
    high, low = split2(values)
    ones = jnp.ones((8, values.shape[1]), BF16)
    return raw_dot(ones, high, 1, 1) + raw_dot(ones, low, 1, 1)


def as_columns(tile):
    return jnp.transpose(jnp.broadcast_to(tile[0:1], (D, D)))


def unit_lower_inverse(strict_parts):
    r, c = iota2((D, D), 0), iota2((D, D), 1)
    eye = jnp.where(r == c, 1.0, 0.0).astype(F32)
    inverse = None
    for k in range(7):
        mask = ((r >> (k + 1)) == (c >> (k + 1))) & (((r >> k) & 1) == 1) & (((c >> k) & 1) == 0)
        off = [jnp.where(mask, a, 0.0) for a in strict_parts]
        if k == 0:
            inverse = [eye - o for o in off]
        else:
            half = [mm(m, o) for m, o in zip(inverse, off)]
            if k == 6:
                return inverse, half
            inverse = [m - mm(h, m) for h, m in zip(half, inverse)]


def kernel(geom, x_hbm, do_hbm, g_hbm, beta_hbm, w_hbm, out_ref, dx_ref, *scratch):
    sections, n_y, n_z, width_all = geom
    (
        x_ref, do_ref, g_ref, beta_ref, w_ref,
        SB, XB, R, R2, TB, NP, RIM, RIMR, SC, GRIM, RIM2, RT,
        QK, DS, EX, FB, WQ, UO, ZK, MAPS, TS, VS, VR, PU, PD, XU, XD, XY, PY, SS, ST, DM, OB, OR, GB, GR, FIN, RT2,
        in_s, row_s, row_r, rim_s, rim_r, row2_s, row2_r, rim2_s, rim2_r, one_s, one_r,
        ring_s, ring_r, vec_s, vec_r, sg_s, sg_r, ya_s, ya_r, yb_s, yb_r,
    ) = scratch
    n_ctx = n_y * n_z * 2
    n_chip = n_y * n_z
    roots = n_z // 2
    cols = D // roots
    sec = lax.axis_index("section")
    ctx = lax.axis_index("ctx")
    core = lax.rem(ctx, 2)
    chip = ctx // 2
    y = chip // n_z
    z = lax.rem(chip, n_z)
    partner = ctx + 1 - 2 * core
    first = core == 0
    rank = z // 2
    is_root = lax.rem(z, 2) == core
    has_before = chip > 0
    has_after = chip < n_chip - 1
    feeds = jnp.logical_and(core == 1, has_after)
    after_chip = 2 * lax.rem(chip + 1, n_chip)
    before_tail = 2 * lax.rem(chip + n_chip - 1, n_chip) + 1

    def at_z(zz):
        return y * (2 * n_z) + zz * 2 + core

    def at_y(yy):
        return yy * (2 * n_z) + z * 2 + core

    def side(ds):
        return lax.rem(sec + ds, sections)

    def copy_to(src, dst, ss, rs, to_sec, to_ctx):
        return pltpu.make_async_remote_copy(
            src_ref=src, dst_ref=dst, send_sem=ss, recv_sem=rs,
            device_id=(to_sec, to_ctx), device_id_type=MESH,
        )

    def arrives(dst, rs):
        copy_to(dst, dst, one_s.at[0], rs, sec, partner).wait_recv()

    sent = []

    def go(*args):
        copy = copy_to(*args)
        copy.start()
        sent.append(copy)

    peers = [(ds, dc) for ds in range(sections) for dc in range(2) if ds or dc]
    peers.sort(key=lambda p: abs(p[0] - sections // 2))

    barrier = pltpu.get_barrier_semaphore()

    def greet(to_sec, to_ctx):
        pl.semaphore_signal(barrier, inc=1, device_id=(to_sec, to_ctx), device_id_type=MESH)

    @pl.when(has_before)
    def _():
        for ds in range(sections):
            greet(side(ds), before_tail)

    @pl.when(feeds)
    def _():
        for ds in range(sections):
            for dc in range(2):
                greet(side(ds), after_chip + dc)

    for ds, dc in peers:
        greet(side(ds), partner if dc else ctx)
    for dz in range(1, n_z):
        greet(sec, at_z(lax.rem(z + dz, n_z)))
    for dy in range(1, n_y):
        greet(sec, at_y(lax.rem(y + dy, n_y)))

    greeted = (
        len(peers) + n_z - 1 + n_y - 1
        + sections * has_before.astype(jnp.int32) + 2 * sections * feeds.astype(jnp.int32)
    )

    loads = [
        pltpu.make_async_copy(src, dst, in_s.at[n])
        for n, (src, dst) in enumerate(
            ((x_hbm, x_ref), (do_hbm, do_ref), (g_hbm, g_ref), (beta_hbm, beta_ref), (w_hbm, w_ref))
        )
    ]
    for load in loads:
        load.start()

    for load in loads:
        load.wait()

    def halves(ref):
        whole = ref[...].astype(F32)
        low, high = whole[:, :D], whole[:, D:]
        return jnp.where(first, low, high), jnp.where(first, high, low), whole

    x_own, x_oth, x_all = halves(x_ref)
    R[0] = row_sums(x_all * x_all)[0:1]
    d_own, d_oth, _ = halves(do_ref)
    g_own, g_oth, _ = halves(g_ref)
    b0, b1 = as_columns(beta_ref[0:1, :]), as_columns(beta_ref[1:2, :])
    SB[0] = x_oth
    SB[1] = d_oth
    SB[2] = g_oth
    SB[3] = jnp.where(first, b1, b0)
    XB[core, 0] = x_own
    XB[core, 1] = d_own
    XB[core, 2] = g_own
    XB[core, 3] = jnp.where(first, b0, b1)
    RT[0] = x_all[D - 8 :, :D]
    RT[1] = x_all[D - 8 :, D:]
    pl.semaphore_wait(barrier, greeted)

    for ds, dc in peers:
        back = ((sections - ds) % sections) * 2 + dc
        go(R.at[0], R.at[back], row_s.at[ds * 2 + dc], row_r.at[back], side(ds), partner if dc else ctx)
    go(SB, XB.at[core], one_s.at[0], one_r.at[0], sec, partner)

    def rim_copies():
        made = []
        for dc in range(2):
            made.append(copy_to(RT.at[dc], RIMR, rim_s.at[2 * sections + dc], rim_r.at[sections], sec, after_chip + dc))
            for ds in range(sections):
                made.append(copy_to(R.at[0], RIM.at[(sections - ds) % sections], rim_s.at[2 * ds + dc],
                                    rim_r.at[(sections - ds) % sections], side(ds), after_chip + dc))
        return made

    @pl.when(feeds)
    def _():
        for copy in rim_copies():
            copy.start()

    arrives(XB.at[1 - core], one_r.at[0])
    r, c = iota2((D, D), 0), iota2((D, D), 1)
    incl = r >= c
    strict = r > c
    lower = jnp.where(incl, 1.0, 0.0).astype(BF16)
    fins = []
    for b in range(2):
        g = XB[b, 2]
        gh = g.astype(BF16)
        rest = g - gh.astype(F32)
        gm = rest.astype(BF16)
        gl = (rest - gm.astype(F32)).astype(BF16)
        cum = raw_dot(lower, gh, 1, 0) + (raw_dot(lower, gm, 1, 0) + raw_dot(lower, gl, 1, 0))
        mid = cum[D // 2 : D // 2 + 1]
        fin = cum[D - 1 : D]
        EX[b, 0] = jnp.exp(cum - mid)
        EX[b, 1] = jnp.exp(mid - cum)
        EX[b, 2] = jnp.exp(cum)
        EX[b, 3] = jnp.exp(fin - cum)
        fins.append(fin)

    for ds, dc in peers:
        slot = ds * 2 + dc
        arrives(R.at[slot], row_r.at[slot])
    same = R[0]
    other = R[1]
    for ds in range(1, sections):
        same = same + R[2 * ds]
        other = other + R[2 * ds + 1]

    def scale_of(total):
        return 1.0 / jnp.sqrt(total / width_all + 1e-5)

    scale_same = scale_of(same)
    SC[core] = as_columns(scale_same)
    SC[1 - core] = as_columns(scale_of(other))
    for b in range(2):
        NP[8 + D * b : 8 + D * (b + 1), :] = XB[b, 0] * SC[b]

    @pl.when(has_before)
    def _():
        for ds in range(sections):
            arrives(RIM.at[ds], rim_r.at[ds])
        arrives(RIMR, rim_r.at[sections])
        rim_total = RIM[0]
        for ds in range(1, sections):
            rim_total = rim_total + RIM[ds]
        NP[0:8, :] = RIMR[...] * as_columns(scale_of(rim_total))[D - 8 :]

    @pl.when(jnp.logical_not(has_before))
    def _():
        NP[0:8, :] = jnp.zeros((8, D), F32)
        RIMR[...] = jnp.zeros((8, D), F32)

    def tap(j, i):
        both = w_ref[j, i : i + 1, :]
        return jnp.where(first, both[:, :D], both[:, D:])

    taps = [[tap(j, i) for i in range(4)] for j in range(3)]
    shifted = [NP[5 + i : 5 + i + 2 * D, :] for i in range(4)]
    for j in range(3):
        mix = taps[j][0] * shifted[0]
        for i in range(1, 4):
            mix = mix + taps[j][i] * shifted[i]
        gate = 1.0 / (1.0 + jnp.exp(-mix))
        act = mix * gate
        slope = gate * (1.0 + mix * (1.0 - gate))
        if j < 2:
            norm = 1.0 / jnp.sqrt(jnp.sum(act * act, axis=1, keepdims=True) + 1e-6)
            QK[j] = act * norm
            DS[j] = slope * norm
        else:
            QK[j] = act
            DS[j] = slope

    blk = [slice(D * b, D * (b + 1)) for b in range(2)]
    systems, scores = [], []
    for b in range(2):
        q, k = QK[0, blk[b], :], QK[1, blk[b], :]
        kf, kb, qf = k * EX[b, 0], k * EX[b, 1], q * EX[b, 0]
        FB[b, 0:D, :] = kf
        FB[b, D : 2 * D, :] = qf
        FB[b, 2 * D : 3 * D, :] = kb
        both = mm_nt(jnp.concatenate([kf, qf], axis=0), kb)
        systems.append(jnp.where(strict, XB[b, 3] * both[:D], 0.0))
        scores.append(jnp.where(incl, both[D:], 0.0))
    inverses, halved = unit_lower_inverse(systems)
    wus, kes = [], []
    for b in range(2):
        k, v, beta = QK[1, blk[b], :], QK[2, blk[b], :], XB[b, 3]
        ke = k * EX[b, 3]
        wu = mm(inverses[b], jnp.concatenate([beta * k * EX[b, 2], beta * v], axis=1))
        wu = wu - mm(halved[b], wu)
        MAPS[b, 0] = jnp.where(r == c, jnp.exp(fins[b]), 0.0) - mm_tn(ke, wu[:, :D])
        wus.append(wu)
        kes.append(ke)
    t0, t1 = MAPS[0, 0], MAPS[1, 0]
    TS[z] = mm(t1, t0)

    def root_at(j):
        return at_z(2 * j + core)

    def map_send(dj):
        j = lax.rem(rank + dj, roots)
        return copy_to(TS.at[z], TS.at[z], ring_s.at[dj], ring_r.at[z], sec, root_at(j))

    def part_send(dj):
        j = lax.rem(rank + dj, roots)
        return copy_to(VS.at[j], VR.at[z], vec_s.at[dj], vec_r.at[z], sec, root_at(j))

    def all_roots(send, act):
        for dj in sorted(range(1, roots), key=lambda dj: abs(2 * dj - roots)):
            act(send(dj))

        @pl.when(jnp.logical_not(is_root))
        def _():
            act(send(0))

    all_roots(map_send, lambda copy: copy.start())

    for b in range(2):
        q, d_out, sc = QK[0, blk[b], :], XB[b, 1], scores[b]
        w, u = wus[b][:, :D], wus[b][:, D:]
        swu = mm(sc, wus[b])
        qeff = q * EX[b, 2] - swu[:, :D]
        WQ[b, 0:D, :] = w
        WQ[b, D : 2 * D, :] = qeff
        UO[b, 0] = u
        UO[b, 1] = swu[:, D:]
        MAPS[b, 1] = mm_tn(u, kes[b])
        MAPS[b, 2] = mm_tn(d_out, qeff)
    i_pair = mm_nt(MAPS[0, 1], t1) + MAPS[1, 1]
    s_pair = MAPS[0, 2] + mm(MAPS[1, 2], t0)
    for j in range(roots):
        VS[j, 0] = i_pair[j * cols : (j + 1) * cols]
        VS[j, 1] = s_pair[j * cols : (j + 1) * cols]
    all_roots(part_send, lambda copy: copy.start())

    for b in range(2):
        h = mm_tn(scores[b], XB[b, 1])
        zk = mm_tn(inverses[b] - mm(halved[b], inverses[b]), jnp.concatenate([h, kes[b]], axis=1))
        ZK[b, 0] = zk[:, :D]
        ZK[b, 1] = zk[:, D:]
    WS = WQ[1]
    by_start = mm_nt(WS, MAPS[0, 1])
    UO[1, 0] = UO[1, 0] - by_start[:D]
    UO[1, 1] = UO[1, 1] + by_start[D:]
    WQ[1] = mm(WS, t0)
    KS = ZK[0, 1]
    ZK[0, 0] = ZK[0, 0] + mm_nt(KS, MAPS[1, 2])
    ZK[0, 1] = mm_nt(KS, t1)
    DM[:, 0:8, :] = jnp.zeros((3, 8, D), F32)
    DM[:, 8 + 2 * D :, :] = jnp.zeros((3, 8, D), F32)
    eye = jnp.where(r == c, 1.0, 0.0).astype(F32)
    mine = pl.ds(pl.multiple_of(rank * cols, cols), cols)

    def ends_send(dy):
        return copy_to(XY.at[y], XY.at[y], ya_s.at[dy], ya_r.at[n_y - dy], sec, at_y(lax.rem(y + dy, n_y)))

    def total_send(yy, dy):
        slot = PY.at[yy - 1]
        return copy_to(slot, slot, yb_s.at[dy], yb_r.at[yy], sec, at_y(lax.rem(y + dy, n_y)))

    def slice_send(dz):
        to = lax.rem(z + dz, n_z)
        return copy_to(SS.at[to], ST.at[:, mine], sg_s.at[dz], sg_r.at[rank], sec, at_z(to))

    @pl.when(is_root)
    def _():
        VR[z] = VS[rank]
        for dz in range(1, n_z):
            zz = lax.rem(z + dz, n_z)
            arrives(TS.at[zz], ring_r.at[zz])
        PU[0] = eye
        PD[n_z - 1] = eye
        up, down = jnp.transpose(TS[0]), TS[n_z - 1]
        for step in range(1, n_z):
            zu, zd = step, n_z - 1 - step
            PU[zu] = up
            PD[zd] = down
            up = mm_nt(up, TS[zu])
            down = mm(down, TS[zd])
        for yy in range(1, n_y - 1):
            @pl.when(y == yy)
            def _():
                PY[yy - 1] = up
                for dy in sorted(range(1, n_y), key=lambda dy: abs(2 * dy - n_y)):
                    total_send(yy, dy).start()

        for dz in range(1, n_z):
            zz = lax.rem(z + dz, n_z)
            arrives(VR.at[zz], vec_r.at[zz])
        all_up, all_down = VR[n_z - 1, 0], VR[0, 1]
        for step in range(1, n_z):
            zu, zd = n_z - 1 - step, step
            all_up = all_up + mm_nt(VR[zu, 0], PD[zu])
            all_down = all_down + mm_nt(VR[zd, 1], PU[zd])
        XY[y, 0] = all_up
        XY[y, 1] = all_down
        for dy in sorted(range(1, n_y), key=lambda dy: abs(2 * dy - n_y)):
            ends_send(dy).start()

        up, down = VR[0, 0], VR[n_z - 1, 1]
        XU[0] = jnp.zeros((cols, D), F32)
        XD[n_z - 1] = jnp.zeros((cols, D), F32)
        for step in range(1, n_z):
            zu, zd = step, n_z - 1 - step
            XU[zu] = up
            XD[zd] = down
            if step < n_z - 1:
                up = mm_nt(up, TS[zu]) + VR[zu, 0]
                down = mm(down, TS[zd]) + VR[zd, 1]

        for dy in range(1, n_y):
            arrives(XY.at[lax.rem(y + dy, n_y)], ya_r.at[dy])
        for yy in range(1, n_y - 1):
            @pl.when(y != yy)
            def _():
                arrives(PY.at[yy - 1], yb_r.at[yy])
        enter = jnp.where(y > 0, XY[0, 0], 0.0)
        leave = jnp.where(y < n_y - 1, XY[n_y - 1, 1], 0.0)
        for step in range(1, n_y - 1):
            yu, yd = step, n_y - 1 - step
            enter = jnp.where(y > yu, mm(enter, PY[yu - 1]) + XY[yu, 0], enter)
            leave = jnp.where(y < yd, mm_nt(leave, PY[yd - 1]) + XY[yd, 1], leave)

        for dz in sorted(range(n_z), key=lambda dz: (dz == 0, abs(2 * dz - n_z))):
            zz = lax.rem(z + dz, n_z)
            SS[zz, 0] = XU[zz] + mm(enter, PU[zz])
            SS[zz, 1] = XD[zz] + mm(leave, PD[zz])
            if dz:
                slice_send(dz).start()
        ST[:, mine, :] = SS[z]

    for dj in range(roots):
        j = lax.rem(rank + dj, roots)
        theirs = ST.at[:, pl.ds(pl.multiple_of(j * cols, cols), cols)]
        if dj:
            arrives(theirs, sg_r.at[j])
        else:
            @pl.when(jnp.logical_not(is_root))
            def _():
                arrives(theirs, sg_r.at[j])

    starts = [ST[0], None]
    ends = [None, ST[1]]
    starts[1] = mm_nt(starts[0], t0) + MAPS[0, 1]
    ends[0] = mm(ends[1], t1) + MAPS[1, 2]
    for b in range(2):
        q, k = QK[0, blk[b], :], QK[1, blk[b], :]
        beta, d_out = XB[b, 3], XB[b, 1]
        wq = mm_nt(WQ[b], starts[0])
        fresh = UO[b, 0] - wq[:D]
        OB[b] = UO[b, 1] + wq[D:]
        zeta = ZK[b, 0] + mm_nt(ZK[b, 1], ends[1])
        pair = mm_nt(jnp.concatenate([d_out, zeta], axis=0), fresh)
        d_sc = jnp.where(incl, pair[:D], 0.0)
        d_p = beta * jnp.where(strict, -pair[D:], 0.0)
        dz_s = mm(jnp.concatenate([d_out, zeta], axis=0), starts[b])
        f_g = mm(fresh, ends[b])
        by_kb = mm(jnp.concatenate([d_sc, d_p], axis=0), FB[b, 2 * D : 3 * D, :])
        d_kb = mm_tn(jnp.concatenate([d_p, d_sc], axis=0), FB[b, 0 : 2 * D, :])
        dq = EX[b, 2] * dz_s[:D] + EX[b, 0] * by_kb[:D]
        dk = EX[b, 3] * f_g - beta * EX[b, 2] * dz_s[D:] + EX[b, 0] * by_kb[D:] + EX[b, 1] * d_kb
        for j, (unit, grad) in enumerate(((q, dq), (k, dk))):
            along = jnp.sum(unit * grad, axis=1, keepdims=True)
            DM[j, 8 + D * b : 8 + D * (b + 1), :] = (grad - unit * along) * DS[j, blk[b], :]
        DM[2, 8 + D * b : 8 + D * (b + 1), :] = beta * zeta * DS[2, blk[b], :]
    go(OB.at[1 - core], OR, one_s.at[1], one_r.at[1], sec, partner)

    d_norm = jnp.zeros((2 * D + 8, D), F32)
    for j in range(3):
        for i in range(4):
            d_norm = d_norm + taps[j][i] * DM[j, 3 - i : 3 - i + 2 * D + 8, :]
    GB[0] = d_norm[8 : 8 + D]
    GB[1] = d_norm[8 + D :]
    GRIM[2] = d_norm[:8]
    TB[2] = row_sums(jnp.concatenate([jnp.zeros((D - 8, D), F32), d_norm[:8] * RIMR[...]], axis=0))[0:1]
    TB[0] = row_sums(d_norm[8 : 8 + D] * XB[0, 0])[0:1]
    TB[1] = row_sums(d_norm[8 + D :] * XB[1, 0])[0:1]

    for ds, dc in peers:
        back = ((sections - ds) % sections) * 2 + dc
        go(TB.at[1 - core if dc else core], R2.at[back], row2_s.at[ds * 2 + dc], row2_r.at[back],
           side(ds), partner if dc else ctx)

    def rim_back_copies():
        made = [copy_to(GRIM.at[2], GRIM.at[core], rim2_s.at[sections], rim2_r.at[2 * sections + core], sec, before_tail)]
        for ds in range(sections):
            slot = 2 * ((sections - ds) % sections) + core
            made.append(copy_to(TB.at[2], RIM2.at[slot], rim2_s.at[ds], rim2_r.at[slot], side(ds), before_tail))
        return made

    @pl.when(has_before)
    def _():
        for copy in rim_back_copies():
            copy.start()

    go(GB.at[1 - core], GR, one_s.at[2], one_r.at[2], sec, partner)

    def joined(own, oth):
        return jnp.concatenate([jnp.where(first, own, oth), jnp.where(first, oth, own)], axis=1)

    arrives(OR, one_r.at[1])
    x_wide = x_ref[...].astype(F32)
    out_ref[...] = (x_wide + joined(OB[core], OR[...])).astype(BF16)
    arrives(GR, one_r.at[2])
    scale = SC[core]
    wide_scale = jnp.concatenate([scale, scale], axis=1)
    FIN[...] = do_ref[...].astype(F32) + joined(GB[core], GR[...]) * wide_scale

    for ds, dc in peers:
        slot = ds * 2 + dc
        arrives(R2.at[slot], row2_r.at[slot])
    inner = TB[core]
    for slot in range(1, 2 * sections):
        inner = inner + R2[slot]
    RT2[0] = inner

    @pl.when(feeds)
    def _():
        for slot in range(2 * sections):
            arrives(RIM2.at[slot], rim2_r.at[slot])
        for n in range(2):
            arrives(GRIM.at[n], rim2_r.at[2 * sections + n])
        total = RT2[0]
        for slot in range(2 * sections):
            total = total + RIM2[slot]
        RT2[0] = total
        late = jnp.concatenate([GRIM[0], GRIM[1]], axis=1)
        FIN[D - 8 :, :] = FIN[D - 8 :, :] + late * jnp.concatenate([SC[core, D - 8 :, :]] * 2, axis=1)

    coef = as_columns(scale_same * scale_same * scale_same * RT2[0] / width_all)
    dx_ref[...] = (FIN[...] - x_wide * jnp.concatenate([coef, coef], axis=1)).astype(BF16)

    for copy in sent:
        copy.wait_send()

    @pl.when(feeds)
    def _():
        for copy in rim_copies():
            copy.wait_send()

    @pl.when(has_before)
    def _():
        for copy in rim_back_copies():
            copy.wait_send()

    all_roots(map_send, lambda copy: copy.wait_send())
    all_roots(part_send, lambda copy: copy.wait_send())

    @pl.when(is_root)
    def _():
        for dy in range(1, n_y):
            ends_send(dy).wait_send()
        for dz in range(1, n_z):
            slice_send(dz).wait_send()
        for yy in range(1, n_y - 1):
            @pl.when(y == yy)
            def _():
                for dy in range(1, n_y):
                    total_send(yy, dy).wait_send()


def solution(mesh):
    sections, n_ctx = mesh.shape["section"], mesh.shape["ctx"]
    n_y, n_z = (4, 8) if n_ctx == 64 else (2, n_ctx // 4)
    roots = n_z // 2
    cols = D // roots
    dma = lambda n: pltpu.SemaphoreType.DMA((n,))

    def shards(inputs, out_grads, conv_weight, log_decay, beta):
        width_all = float(inputs.shape[1] * sections)
        v = lambda *s: pltpu.VMEM(s, F32)
        scratch = [
            pltpu.VMEM((D, 2 * D), BF16), pltpu.VMEM((D, 2 * D), BF16), v(D, 2 * D), v(2, D), v(3, 4, 2 * D),
            v(4, D, D), v(2, 4, D, D), v(2 * sections, 1, D), v(2 * sections, 1, D), v(3, 1, D),
            v(2 * D + 8, D), v(sections, 1, D), v(8, D), v(2, D, D), v(3, 8, D), v(2 * sections, 1, D), v(2, 8, D),
            v(3, 2 * D, D), v(3, 2 * D, D), v(2, 4, D, D), v(2, 3 * D, D), v(2, 2 * D, D), v(2, 2, D, D),
            v(2, 2, D, D), v(2, 3, D, D), v(n_z, D, D), v(roots, 2, cols, D), v(n_z, 2, cols, D),
            v(n_z, D, D), v(n_z, D, D), v(n_z, cols, D), v(n_z, cols, D), v(n_y, 2, cols, D),
            v(max(n_y - 2, 1), D, D), v(n_z, 2, cols, D), v(2, D, D), v(3, 2 * D + 16, D),
            v(2, D, D), v(D, D), v(2, D, D), v(D, D), v(D, 2 * D), v(1, 1, D),
            dma(5), dma(2 * sections), dma(2 * sections), dma(2 * sections + 2), dma(sections + 1),
            dma(2 * sections), dma(2 * sections), dma(sections + 1), dma(2 * sections + 2), dma(3), dma(3),
            dma(roots), dma(n_z), dma(roots), dma(n_z), dma(n_z), dma(roots),
            dma(n_y), dma(n_y), dma(n_y), dma(n_y),
        ]
        vm = pl.BlockSpec(memory_space=pltpu.VMEM)
        hbm = pl.BlockSpec(memory_space=pltpu.MemorySpace.HBM)
        return pl.pallas_call(
            functools.partial(kernel, (sections, n_y, n_z, width_all)),
            out_shape=(jax.ShapeDtypeStruct(inputs.shape, BF16), jax.ShapeDtypeStruct(inputs.shape, BF16)),
            in_specs=[hbm] * 5,
            out_specs=(vm, vm),
            scratch_shapes=scratch,
            compiler_params=pltpu.CompilerParams(
                collective_id=0, has_side_effects=True, vmem_limit_bytes=40 * 2**20
            ),
        )(*[pltpu.with_memory_space_constraint(a, pltpu.MemorySpace.HBM) for a in (inputs, out_grads, log_decay, beta.T, conv_weight)])

    spec = P("ctx", "section")
    return jax.shard_map(
        shards, mesh=mesh, in_specs=(spec, spec, P(None, None, "section"), spec, spec),
        out_specs=(spec, spec), check_vma=False,
    )
```

```python
import functools

import jax
import jax.numpy as jnp
from jax import lax
from jax.experimental import pallas as pl
from jax.experimental.pallas import tpu as pltpu
from jax.sharding import PartitionSpec as P

MESH = pl.DeviceIdType.MESH
D = 128
F32 = jnp.float32
BF16 = jnp.bfloat16


def split2(a):
    high = a.astype(BF16)
    low = (a - high.astype(F32)).astype(BF16)
    return high, low


def raw_dot(a, b, ca, cb):
    return lax.dot_general(a, b, (((ca,), (cb,)), ((), ())), preferred_element_type=F32)


def mm(a, b, ca=1, cb=0):
    ah, al = split2(a)
    bh, bl = split2(b)
    aa = jnp.concatenate([ah, al], axis=ca)
    bb = jnp.concatenate([jnp.concatenate([bh, bh], axis=cb), jnp.concatenate([bl, bl], axis=cb)], axis=1 - cb)
    wide = raw_dot(aa, bb, ca, cb)
    n = b.shape[1 - cb]
    return wide[:, :n] + wide[:, n:]


def mm_nt(a, b):
    return mm(a, b, 1, 1)


def mm_tn(a, b):
    return mm(a, b, 0, 0)


def iota2(shape, axis):
    return lax.broadcasted_iota(jnp.int32, shape, axis)


def row_sums(values):
    high, low = split2(values)
    ones = jnp.ones((8, values.shape[1]), BF16)
    return raw_dot(ones, high, 1, 1) + raw_dot(ones, low, 1, 1)


def as_columns(tile):
    return jnp.transpose(jnp.broadcast_to(tile[0:1], (D, D)))


def unit_lower_inverse(strict_parts):
    r, c = iota2((D, D), 0), iota2((D, D), 1)
    eye = jnp.where(r == c, 1.0, 0.0).astype(F32)
    inverse = None
    for k in range(7):
        mask = ((r >> (k + 1)) == (c >> (k + 1))) & (((r >> k) & 1) == 1) & (((c >> k) & 1) == 0)
        off = [jnp.where(mask, a, 0.0) for a in strict_parts]
        if k == 0:
            inverse = [eye - o for o in off]
        else:
            half = [mm(m, o) for m, o in zip(inverse, off)]
            if k == 6:
                return inverse, half
            inverse = [m - mm(h, m) for h, m in zip(half, inverse)]


def kernel(geom, x_hbm, do_hbm, g_hbm, beta_hbm, w_hbm, both_ref, *scratch):
    sections, n_y, n_z, width_all = geom
    (
        x_ref, do_ref, g_ref, beta_ref, w_ref,
        SB, XB, R, R2, TB, NP, RIM, RIMR, SC, GRIM, RIM2, RT,
        QK, DS, EX, FB, WQ, UO, ZK, MAPS, TS, VS, VR, PU, PD, XU, XD, XY, PY, SS, ST, DM, OB, OR, GB, GR, FIN, RT2,
        in_s, row_s, row_r, rim_s, rim_r, row2_s, row2_r, rim2_s, rim2_r, one_s, one_r,
        ring_s, ring_r, vec_s, vec_r, sg_s, sg_r, ya_s, ya_r, yb_s, yb_r,
    ) = scratch
    n_ctx = n_y * n_z * 2
    n_chip = n_y * n_z
    roots = n_z // 2
    cols = D // roots
    sec = lax.axis_index("section")
    ctx = lax.axis_index("ctx")
    core = lax.rem(ctx, 2)
    chip = ctx // 2
    y = chip // n_z
    z = lax.rem(chip, n_z)
    partner = ctx + 1 - 2 * core
    first = core == 0
    rank = z // 2
    is_root = lax.rem(z, 2) == core
    has_before = chip > 0
    has_after = chip < n_chip - 1
    feeds = jnp.logical_and(core == 1, has_after)
    after_chip = 2 * lax.rem(chip + 1, n_chip)
    before_tail = 2 * lax.rem(chip + n_chip - 1, n_chip) + 1

    def at_z(zz):
        return y * (2 * n_z) + zz * 2 + core

    def at_y(yy):
        return yy * (2 * n_z) + z * 2 + core

    def side(ds):
        return lax.rem(sec + ds, sections)

    def copy_to(src, dst, ss, rs, to_sec, to_ctx):
        return pltpu.make_async_remote_copy(
            src_ref=src, dst_ref=dst, send_sem=ss, recv_sem=rs,
            device_id=(to_sec, to_ctx), device_id_type=MESH,
        )

    def arrives(dst, rs):
        copy_to(dst, dst, one_s.at[0], rs, sec, partner).wait_recv()

    sent = []

    def go(*args):
        copy = copy_to(*args)
        copy.start()
        sent.append(copy)

    peers = [(ds, dc) for ds in range(sections) for dc in range(2) if ds or dc]
    peers.sort(key=lambda p: abs(p[0] - sections // 2))

    barrier = pltpu.get_barrier_semaphore()

    def greet(to_sec, to_ctx):
        pl.semaphore_signal(barrier, inc=1, device_id=(to_sec, to_ctx), device_id_type=MESH)

    @pl.when(has_before)
    def _():
        for ds in range(sections):
            greet(side(ds), before_tail)

    @pl.when(feeds)
    def _():
        for ds in range(sections):
            for dc in range(2):
                greet(side(ds), after_chip + dc)

    for ds, dc in peers:
        greet(side(ds), partner if dc else ctx)
    for dz in range(1, n_z):
        greet(sec, at_z(lax.rem(z + dz, n_z)))
    for dy in range(1, n_y):
        greet(sec, at_y(lax.rem(y + dy, n_y)))

    greeted = (
        len(peers) + n_z - 1 + n_y - 1
        + sections * has_before.astype(jnp.int32) + 2 * sections * feeds.astype(jnp.int32)
    )

    loads = [
        pltpu.make_async_copy(src, dst, in_s.at[n])
        for n, (src, dst) in enumerate(
            ((x_hbm, x_ref), (do_hbm, do_ref), (g_hbm, g_ref), (beta_hbm, beta_ref), (w_hbm, w_ref))
        )
    ]
    for load in loads:
        load.start()

    for load in loads:
        load.wait()

    def halves(ref):
        whole = ref[...].astype(F32)
        low, high = whole[:, :D], whole[:, D:]
        return jnp.where(first, low, high), jnp.where(first, high, low), whole

    x_own, x_oth, x_all = halves(x_ref)
    R[0] = row_sums(x_all * x_all)[0:1]
    d_own, d_oth, _ = halves(do_ref)
    g_own, g_oth, _ = halves(g_ref)
    b0, b1 = as_columns(beta_ref[0:1, :]), as_columns(beta_ref[1:2, :])
    SB[0] = x_oth
    SB[1] = d_oth
    SB[2] = g_oth
    SB[3] = jnp.where(first, b1, b0)
    XB[core, 0] = x_own
    XB[core, 1] = d_own
    XB[core, 2] = g_own
    XB[core, 3] = jnp.where(first, b0, b1)
    RT[0] = x_all[D - 8 :, :D]
    RT[1] = x_all[D - 8 :, D:]
    pl.semaphore_wait(barrier, greeted)

    for ds, dc in peers:
        back = ((sections - ds) % sections) * 2 + dc
        go(R.at[0], R.at[back], row_s.at[ds * 2 + dc], row_r.at[back], side(ds), partner if dc else ctx)
    go(SB, XB.at[core], one_s.at[0], one_r.at[0], sec, partner)

    def rim_copies():
        made = []
        for dc in range(2):
            made.append(copy_to(RT.at[dc], RIMR, rim_s.at[2 * sections + dc], rim_r.at[sections], sec, after_chip + dc))
            for ds in range(sections):
                made.append(copy_to(R.at[0], RIM.at[(sections - ds) % sections], rim_s.at[2 * ds + dc],
                                    rim_r.at[(sections - ds) % sections], side(ds), after_chip + dc))
        return made

    @pl.when(feeds)
    def _():
        for copy in rim_copies():
            copy.start()

    arrives(XB.at[1 - core], one_r.at[0])
    r, c = iota2((D, D), 0), iota2((D, D), 1)
    incl = r >= c
    strict = r > c
    lower = jnp.where(incl, 1.0, 0.0).astype(BF16)
    fins = []
    for b in range(2):
        g = XB[b, 2]
        gh = g.astype(BF16)
        rest = g - gh.astype(F32)
        gm = rest.astype(BF16)
        gl = (rest - gm.astype(F32)).astype(BF16)
        cum = raw_dot(lower, gh, 1, 0) + (raw_dot(lower, gm, 1, 0) + raw_dot(lower, gl, 1, 0))
        mid = cum[D // 2 : D // 2 + 1]
        fin = cum[D - 1 : D]
        EX[b, 0] = jnp.exp(cum - mid)
        EX[b, 1] = jnp.exp(mid - cum)
        EX[b, 2] = jnp.exp(cum)
        EX[b, 3] = jnp.exp(fin - cum)
        fins.append(fin)

    for ds, dc in peers:
        slot = ds * 2 + dc
        arrives(R.at[slot], row_r.at[slot])
    same = R[0]
    other = R[1]
    for ds in range(1, sections):
        same = same + R[2 * ds]
        other = other + R[2 * ds + 1]

    def scale_of(total):
        return 1.0 / jnp.sqrt(total / width_all + 1e-5)

    scale_same = scale_of(same)
    SC[core] = as_columns(scale_same)
    SC[1 - core] = as_columns(scale_of(other))
    for b in range(2):
        NP[8 + D * b : 8 + D * (b + 1), :] = XB[b, 0] * SC[b]

    @pl.when(has_before)
    def _():
        for ds in range(sections):
            arrives(RIM.at[ds], rim_r.at[ds])
        arrives(RIMR, rim_r.at[sections])
        rim_total = RIM[0]
        for ds in range(1, sections):
            rim_total = rim_total + RIM[ds]
        NP[0:8, :] = RIMR[...] * as_columns(scale_of(rim_total))[D - 8 :]

    @pl.when(jnp.logical_not(has_before))
    def _():
        NP[0:8, :] = jnp.zeros((8, D), F32)
        RIMR[...] = jnp.zeros((8, D), F32)

    def tap(j, i):
        both = w_ref[j, i : i + 1, :]
        return jnp.where(first, both[:, :D], both[:, D:])

    taps = [[tap(j, i) for i in range(4)] for j in range(3)]
    shifted = [NP[5 + i : 5 + i + 2 * D, :] for i in range(4)]
    for j in range(3):
        mix = taps[j][0] * shifted[0]
        for i in range(1, 4):
            mix = mix + taps[j][i] * shifted[i]
        gate = 1.0 / (1.0 + jnp.exp(-mix))
        act = mix * gate
        slope = gate * (1.0 + mix * (1.0 - gate))
        if j < 2:
            norm = 1.0 / jnp.sqrt(jnp.sum(act * act, axis=1, keepdims=True) + 1e-6)
            QK[j] = act * norm
            DS[j] = slope * norm
        else:
            QK[j] = act
            DS[j] = slope

    blk = [slice(D * b, D * (b + 1)) for b in range(2)]
    systems, scores = [], []
    for b in range(2):
        q, k = QK[0, blk[b], :], QK[1, blk[b], :]
        kf, kb, qf = k * EX[b, 0], k * EX[b, 1], q * EX[b, 0]
        FB[b, 0:D, :] = kf
        FB[b, D : 2 * D, :] = qf
        FB[b, 2 * D : 3 * D, :] = kb
        both = mm_nt(jnp.concatenate([kf, qf], axis=0), kb)
        systems.append(jnp.where(strict, XB[b, 3] * both[:D], 0.0))
        scores.append(jnp.where(incl, both[D:], 0.0))
    inverses, halved = unit_lower_inverse(systems)
    wus, kes = [], []
    for b in range(2):
        k, v, beta = QK[1, blk[b], :], QK[2, blk[b], :], XB[b, 3]
        ke = k * EX[b, 3]
        wu = mm(inverses[b], jnp.concatenate([beta * k * EX[b, 2], beta * v], axis=1))
        wu = wu - mm(halved[b], wu)
        MAPS[b, 0] = jnp.where(r == c, jnp.exp(fins[b]), 0.0) - mm_tn(ke, wu[:, :D])
        wus.append(wu)
        kes.append(ke)
    t0, t1 = MAPS[0, 0], MAPS[1, 0]
    TS[z] = mm(t1, t0)

    def root_at(j):
        return at_z(2 * j + core)

    def map_send(dj):
        j = lax.rem(rank + dj, roots)
        return copy_to(TS.at[z], TS.at[z], ring_s.at[dj], ring_r.at[z], sec, root_at(j))

    def part_send(dj):
        j = lax.rem(rank + dj, roots)
        return copy_to(VS.at[j], VR.at[z], vec_s.at[dj], vec_r.at[z], sec, root_at(j))

    def all_roots(send, act):
        for dj in sorted(range(1, roots), key=lambda dj: abs(2 * dj - roots)):
            act(send(dj))

        @pl.when(jnp.logical_not(is_root))
        def _():
            act(send(0))

    all_roots(map_send, lambda copy: copy.start())

    for b in range(2):
        q, d_out, sc = QK[0, blk[b], :], XB[b, 1], scores[b]
        w, u = wus[b][:, :D], wus[b][:, D:]
        swu = mm(sc, wus[b])
        qeff = q * EX[b, 2] - swu[:, :D]
        WQ[b, 0:D, :] = w
        WQ[b, D : 2 * D, :] = qeff
        UO[b, 0] = u
        UO[b, 1] = swu[:, D:]
        MAPS[b, 1] = mm_tn(u, kes[b])
        MAPS[b, 2] = mm_tn(d_out, qeff)
    i_pair = mm_nt(MAPS[0, 1], t1) + MAPS[1, 1]
    s_pair = MAPS[0, 2] + mm(MAPS[1, 2], t0)
    for j in range(roots):
        VS[j, 0] = i_pair[j * cols : (j + 1) * cols]
        VS[j, 1] = s_pair[j * cols : (j + 1) * cols]
    all_roots(part_send, lambda copy: copy.start())

    for b in range(2):
        h = mm_tn(scores[b], XB[b, 1])
        zk = mm_tn(inverses[b] - mm(halved[b], inverses[b]), jnp.concatenate([h, kes[b]], axis=1))
        ZK[b, 0] = zk[:, :D]
        ZK[b, 1] = zk[:, D:]
    WS = WQ[1]
    by_start = mm_nt(WS, MAPS[0, 1])
    UO[1, 0] = UO[1, 0] - by_start[:D]
    UO[1, 1] = UO[1, 1] + by_start[D:]
    WQ[1] = mm(WS, t0)
    KS = ZK[0, 1]
    ZK[0, 0] = ZK[0, 0] + mm_nt(KS, MAPS[1, 2])
    ZK[0, 1] = mm_nt(KS, t1)
    DM[:, 0:8, :] = jnp.zeros((3, 8, D), F32)
    DM[:, 8 + 2 * D :, :] = jnp.zeros((3, 8, D), F32)
    eye = jnp.where(r == c, 1.0, 0.0).astype(F32)
    mine = pl.ds(pl.multiple_of(rank * cols, cols), cols)

    def ends_send(dy):
        return copy_to(XY.at[y], XY.at[y], ya_s.at[dy], ya_r.at[n_y - dy], sec, at_y(lax.rem(y + dy, n_y)))

    def total_send(yy, dy):
        slot = PY.at[yy - 1]
        return copy_to(slot, slot, yb_s.at[dy], yb_r.at[yy], sec, at_y(lax.rem(y + dy, n_y)))

    def slice_send(dz):
        to = lax.rem(z + dz, n_z)
        return copy_to(SS.at[to], ST.at[:, mine], sg_s.at[dz], sg_r.at[rank], sec, at_z(to))

    @pl.when(is_root)
    def _():
        VR[z] = VS[rank]
        for dz in range(1, n_z):
            zz = lax.rem(z + dz, n_z)
            arrives(TS.at[zz], ring_r.at[zz])
        PU[0] = eye
        PD[n_z - 1] = eye
        up, down = jnp.transpose(TS[0]), TS[n_z - 1]
        for step in range(1, n_z):
            zu, zd = step, n_z - 1 - step
            PU[zu] = up
            PD[zd] = down
            up = mm_nt(up, TS[zu])
            down = mm(down, TS[zd])
        for yy in range(1, n_y - 1):
            @pl.when(y == yy)
            def _():
                PY[yy - 1] = up
                for dy in sorted(range(1, n_y), key=lambda dy: abs(2 * dy - n_y)):
                    total_send(yy, dy).start()

        for dz in range(1, n_z):
            zz = lax.rem(z + dz, n_z)
            arrives(VR.at[zz], vec_r.at[zz])
        all_up, all_down = VR[n_z - 1, 0], VR[0, 1]
        for step in range(1, n_z):
            zu, zd = n_z - 1 - step, step
            all_up = all_up + mm_nt(VR[zu, 0], PD[zu])
            all_down = all_down + mm_nt(VR[zd, 1], PU[zd])
        XY[y, 0] = all_up
        XY[y, 1] = all_down
        for dy in sorted(range(1, n_y), key=lambda dy: abs(2 * dy - n_y)):
            ends_send(dy).start()

        up, down = VR[0, 0], VR[n_z - 1, 1]
        XU[0] = jnp.zeros((cols, D), F32)
        XD[n_z - 1] = jnp.zeros((cols, D), F32)
        for step in range(1, n_z):
            zu, zd = step, n_z - 1 - step
            XU[zu] = up
            XD[zd] = down
            if step < n_z - 1:
                up = mm_nt(up, TS[zu]) + VR[zu, 0]
                down = mm(down, TS[zd]) + VR[zd, 1]

        for dy in range(1, n_y):
            arrives(XY.at[lax.rem(y + dy, n_y)], ya_r.at[dy])
        for yy in range(1, n_y - 1):
            @pl.when(y != yy)
            def _():
                arrives(PY.at[yy - 1], yb_r.at[yy])
        enter = jnp.where(y > 0, XY[0, 0], 0.0)
        leave = jnp.where(y < n_y - 1, XY[n_y - 1, 1], 0.0)
        for step in range(1, n_y - 1):
            yu, yd = step, n_y - 1 - step
            enter = jnp.where(y > yu, mm(enter, PY[yu - 1]) + XY[yu, 0], enter)
            leave = jnp.where(y < yd, mm_nt(leave, PY[yd - 1]) + XY[yd, 1], leave)

        for dz in sorted(range(n_z), key=lambda dz: (dz == 0, abs(2 * dz - n_z))):
            zz = lax.rem(z + dz, n_z)
            SS[zz, 0] = XU[zz] + mm(enter, PU[zz])
            SS[zz, 1] = XD[zz] + mm(leave, PD[zz])
            if dz:
                slice_send(dz).start()
        ST[:, mine, :] = SS[z]

    for dj in range(roots):
        j = lax.rem(rank + dj, roots)
        theirs = ST.at[:, pl.ds(pl.multiple_of(j * cols, cols), cols)]
        if dj:
            arrives(theirs, sg_r.at[j])
        else:
            @pl.when(jnp.logical_not(is_root))
            def _():
                arrives(theirs, sg_r.at[j])

    starts = [ST[0], None]
    ends = [None, ST[1]]
    starts[1] = mm_nt(starts[0], t0) + MAPS[0, 1]
    ends[0] = mm(ends[1], t1) + MAPS[1, 2]
    for b in range(2):
        q, k = QK[0, blk[b], :], QK[1, blk[b], :]
        beta, d_out = XB[b, 3], XB[b, 1]
        wq = mm_nt(WQ[b], starts[0])
        fresh = UO[b, 0] - wq[:D]
        OB[b] = UO[b, 1] + wq[D:]
        zeta = ZK[b, 0] + mm_nt(ZK[b, 1], ends[1])
        pair = mm_nt(jnp.concatenate([d_out, zeta], axis=0), fresh)
        d_sc = jnp.where(incl, pair[:D], 0.0)
        d_p = beta * jnp.where(strict, -pair[D:], 0.0)
        dz_s = mm(jnp.concatenate([d_out, zeta], axis=0), starts[b])
        f_g = mm(fresh, ends[b])
        by_kb = mm(jnp.concatenate([d_sc, d_p], axis=0), FB[b, 2 * D : 3 * D, :])
        d_kb = mm_tn(jnp.concatenate([d_p, d_sc], axis=0), FB[b, 0 : 2 * D, :])
        dq = EX[b, 2] * dz_s[:D] + EX[b, 0] * by_kb[:D]
        dk = EX[b, 3] * f_g - beta * EX[b, 2] * dz_s[D:] + EX[b, 0] * by_kb[D:] + EX[b, 1] * d_kb
        for j, (unit, grad) in enumerate(((q, dq), (k, dk))):
            along = jnp.sum(unit * grad, axis=1, keepdims=True)
            DM[j, 8 + D * b : 8 + D * (b + 1), :] = (grad - unit * along) * DS[j, blk[b], :]
        DM[2, 8 + D * b : 8 + D * (b + 1), :] = beta * zeta * DS[2, blk[b], :]
    go(OB.at[1 - core], OR, one_s.at[1], one_r.at[1], sec, partner)

    d_norm = jnp.zeros((2 * D + 8, D), F32)
    for j in range(3):
        for i in range(4):
            d_norm = d_norm + taps[j][i] * DM[j, 3 - i : 3 - i + 2 * D + 8, :]
    GB[0] = d_norm[8 : 8 + D]
    GB[1] = d_norm[8 + D :]
    GRIM[2] = d_norm[:8]
    TB[2] = row_sums(jnp.concatenate([jnp.zeros((D - 8, D), F32), d_norm[:8] * RIMR[...]], axis=0))[0:1]
    TB[0] = row_sums(d_norm[8 : 8 + D] * XB[0, 0])[0:1]
    TB[1] = row_sums(d_norm[8 + D :] * XB[1, 0])[0:1]

    for ds, dc in peers:
        back = ((sections - ds) % sections) * 2 + dc
        go(TB.at[1 - core if dc else core], R2.at[back], row2_s.at[ds * 2 + dc], row2_r.at[back],
           side(ds), partner if dc else ctx)

    def rim_back_copies():
        made = [copy_to(GRIM.at[2], GRIM.at[core], rim2_s.at[sections], rim2_r.at[2 * sections + core], sec, before_tail)]
        for ds in range(sections):
            slot = 2 * ((sections - ds) % sections) + core
            made.append(copy_to(TB.at[2], RIM2.at[slot], rim2_s.at[ds], rim2_r.at[slot], side(ds), before_tail))
        return made

    @pl.when(has_before)
    def _():
        for copy in rim_back_copies():
            copy.start()

    go(GB.at[1 - core], GR, one_s.at[2], one_r.at[2], sec, partner)

    def joined(own, oth):
        return jnp.concatenate([jnp.where(first, own, oth), jnp.where(first, oth, own)], axis=1)

    arrives(OR, one_r.at[1])
    x_wide = x_ref[...].astype(F32)
    both_ref[0] = (x_wide + joined(OB[core], OR[...])).astype(BF16)
    arrives(GR, one_r.at[2])
    scale = SC[core]
    wide_scale = jnp.concatenate([scale, scale], axis=1)
    FIN[...] = do_ref[...].astype(F32) + joined(GB[core], GR[...]) * wide_scale

    for ds, dc in peers:
        slot = ds * 2 + dc
        arrives(R2.at[slot], row2_r.at[slot])
    inner = TB[core]
    for slot in range(1, 2 * sections):
        inner = inner + R2[slot]
    RT2[0] = inner

    @pl.when(feeds)
    def _():
        for slot in range(2 * sections):
            arrives(RIM2.at[slot], rim2_r.at[slot])
        for n in range(2):
            arrives(GRIM.at[n], rim2_r.at[2 * sections + n])
        total = RT2[0]
        for slot in range(2 * sections):
            total = total + RIM2[slot]
        RT2[0] = total
        late = jnp.concatenate([GRIM[0], GRIM[1]], axis=1)
        FIN[D - 8 :, :] = FIN[D - 8 :, :] + late * jnp.concatenate([SC[core, D - 8 :, :]] * 2, axis=1)

    coef = as_columns(scale_same * scale_same * scale_same * RT2[0] / width_all)
    both_ref[1] = (FIN[...] - x_wide * jnp.concatenate([coef, coef], axis=1)).astype(BF16)

    for copy in sent:
        copy.wait_send()

    @pl.when(feeds)
    def _():
        for copy in rim_copies():
            copy.wait_send()

    @pl.when(has_before)
    def _():
        for copy in rim_back_copies():
            copy.wait_send()

    all_roots(map_send, lambda copy: copy.wait_send())
    all_roots(part_send, lambda copy: copy.wait_send())

    @pl.when(is_root)
    def _():
        for dy in range(1, n_y):
            ends_send(dy).wait_send()
        for dz in range(1, n_z):
            slice_send(dz).wait_send()
        for yy in range(1, n_y - 1):
            @pl.when(y == yy)
            def _():
                for dy in range(1, n_y):
                    total_send(yy, dy).wait_send()


def solution(mesh):
    sections, n_ctx = mesh.shape["section"], mesh.shape["ctx"]
    n_y, n_z = (4, 8) if n_ctx == 64 else (2, n_ctx // 4)
    roots = n_z // 2
    cols = D // roots
    dma = lambda n: pltpu.SemaphoreType.DMA((n,))

    def shards(inputs, out_grads, conv_weight, log_decay, beta):
        width_all = float(inputs.shape[1] * sections)
        v = lambda *s: pltpu.VMEM(s, F32)
        scratch = [
            pltpu.VMEM((D, 2 * D), BF16), pltpu.VMEM((D, 2 * D), BF16), v(D, 2 * D), v(2, D), v(3, 4, 2 * D),
            v(4, D, D), v(2, 4, D, D), v(2 * sections, 1, D), v(2 * sections, 1, D), v(3, 1, D),
            v(2 * D + 8, D), v(sections, 1, D), v(8, D), v(2, D, D), v(3, 8, D), v(2 * sections, 1, D), v(2, 8, D),
            v(3, 2 * D, D), v(3, 2 * D, D), v(2, 4, D, D), v(2, 3 * D, D), v(2, 2 * D, D), v(2, 2, D, D),
            v(2, 2, D, D), v(2, 3, D, D), v(n_z, D, D), v(roots, 2, cols, D), v(n_z, 2, cols, D),
            v(n_z, D, D), v(n_z, D, D), v(n_z, cols, D), v(n_z, cols, D), v(n_y, 2, cols, D),
            v(max(n_y - 2, 1), D, D), v(n_z, 2, cols, D), v(2, D, D), v(3, 2 * D + 16, D),
            v(2, D, D), v(D, D), v(2, D, D), v(D, D), v(D, 2 * D), v(1, 1, D),
            dma(5), dma(2 * sections), dma(2 * sections), dma(2 * sections + 2), dma(sections + 1),
            dma(2 * sections), dma(2 * sections), dma(sections + 1), dma(2 * sections + 2), dma(3), dma(3),
            dma(roots), dma(n_z), dma(roots), dma(n_z), dma(n_z), dma(roots),
            dma(n_y), dma(n_y), dma(n_y), dma(n_y),
        ]
        vm = pl.BlockSpec(memory_space=pltpu.VMEM)
        hbm = pl.BlockSpec(memory_space=pltpu.MemorySpace.HBM)
        both = pl.pallas_call(
            functools.partial(kernel, (sections, n_y, n_z, width_all)),
            out_shape=jax.ShapeDtypeStruct((2,) + inputs.shape, BF16),
            in_specs=[hbm] * 5,
            out_specs=vm,
            scratch_shapes=scratch,
            compiler_params=pltpu.CompilerParams(
                collective_id=0, has_side_effects=True, vmem_limit_bytes=40 * 2**20
            ),
        )(*[pltpu.with_memory_space_constraint(a, pltpu.MemorySpace.HBM) for a in (inputs, out_grads, log_decay, beta.T, conv_weight)])
        return both[0], both[1]

    spec = P("ctx", "section")
    return jax.shard_map(
        shards, mesh=mesh, in_specs=(spec, spec, P(None, None, "section"), spec, spec),
        out_specs=(spec, spec), check_vma=False,
    )
```

```python
import functools

import jax
import jax.numpy as jnp
from jax import lax
from jax.experimental import pallas as pl
from jax.experimental.pallas import tpu as pltpu
from jax.sharding import PartitionSpec as P

MESH = pl.DeviceIdType.MESH
D = 128
F32 = jnp.float32
BF16 = jnp.bfloat16


def split2(a):
    high = a.astype(BF16)
    low = (a - high.astype(F32)).astype(BF16)
    return high, low


def raw_dot(a, b, ca, cb):
    return lax.dot_general(a, b, (((ca,), (cb,)), ((), ())), preferred_element_type=F32)


def mm(a, b, ca=1, cb=0):
    ah, al = split2(a)
    bh, bl = split2(b)
    aa = jnp.concatenate([ah, al], axis=ca)
    bb = jnp.concatenate([jnp.concatenate([bh, bh], axis=cb), jnp.concatenate([bl, bl], axis=cb)], axis=1 - cb)
    wide = raw_dot(aa, bb, ca, cb)
    n = b.shape[1 - cb]
    return wide[:, :n] + wide[:, n:]


def mm_nt(a, b):
    return mm(a, b, 1, 1)


def mm_tn(a, b):
    return mm(a, b, 0, 0)


def iota2(shape, axis):
    return lax.broadcasted_iota(jnp.int32, shape, axis)


def row_sums(values):
    high, low = split2(values)
    ones = jnp.ones((8, values.shape[1]), BF16)
    return raw_dot(ones, high, 1, 1) + raw_dot(ones, low, 1, 1)


def as_columns(tile):
    return jnp.transpose(jnp.broadcast_to(tile[0:1], (D, D)))


def unit_lower_inverse(strict_parts):
    r, c = iota2((D, D), 0), iota2((D, D), 1)
    eye = jnp.where(r == c, 1.0, 0.0).astype(F32)
    inverse = None
    for k in range(7):
        mask = ((r >> (k + 1)) == (c >> (k + 1))) & (((r >> k) & 1) == 1) & (((c >> k) & 1) == 0)
        off = [jnp.where(mask, a, 0.0) for a in strict_parts]
        if k == 0:
            inverse = [eye - o for o in off]
        else:
            half = [mm(m, o) for m, o in zip(inverse, off)]
            if k == 6:
                return inverse, half
            inverse = [m - mm(h, m) for h, m in zip(half, inverse)]


def kernel(geom, x_hbm, do_hbm, g_hbm, beta_hbm, w_hbm, both_ref, *scratch):
    sections, n_y, n_z, width_all = geom
    (
        x_ref, do_ref, g_ref, beta_ref, w_ref,
        SB, XB, R, R2, TB, NP, RIM, RIMR, SC, GRIM, RIM2, RT,
        QK, DS, EX, FB, WQ, UO, ZK, MAPS, TS, VS, VR, PU, PD, XU, XD, XY, PY, SS, ST, DM, OB, OR, GB, GR, FIN, RT2,
        in_s, row_s, row_r, rim_s, rim_r, row2_s, row2_r, rim2_s, rim2_r, one_s, one_r,
        ring_s, ring_r, vec_s, vec_r, sg_s, sg_r, ya_s, ya_r, yb_s, yb_r,
    ) = scratch
    n_ctx = n_y * n_z * 2
    n_chip = n_y * n_z
    roots = n_z // 2
    cols = D // roots
    sec = lax.axis_index("section")
    ctx = lax.axis_index("ctx")
    core = lax.rem(ctx, 2)
    chip = ctx // 2
    y = chip // n_z
    z = lax.rem(chip, n_z)
    partner = ctx + 1 - 2 * core
    first = core == 0
    rank = z // 2
    is_root = lax.rem(z, 2) == core
    has_before = chip > 0
    has_after = chip < n_chip - 1
    feeds = jnp.logical_and(core == 1, has_after)
    after_chip = 2 * lax.rem(chip + 1, n_chip)
    before_tail = 2 * lax.rem(chip + n_chip - 1, n_chip) + 1

    def at_z(zz):
        return y * (2 * n_z) + zz * 2 + core

    def at_y(yy):
        return yy * (2 * n_z) + z * 2 + core

    def side(ds):
        return lax.rem(sec + ds, sections)

    def copy_to(src, dst, ss, rs, to_sec, to_ctx):
        return pltpu.make_async_remote_copy(
            src_ref=src, dst_ref=dst, send_sem=ss, recv_sem=rs,
            device_id=(to_sec, to_ctx), device_id_type=MESH,
        )

    def arrives(dst, rs):
        copy_to(dst, dst, one_s.at[0], rs, sec, partner).wait_recv()

    sent = []

    def go(*args):
        copy = copy_to(*args)
        copy.start()
        sent.append(copy)

    peers = [(ds, dc) for ds in range(sections) for dc in range(2) if ds or dc]
    peers.sort(key=lambda p: abs(p[0] - sections // 2))

    barrier = pltpu.get_barrier_semaphore()

    def greet(to_sec, to_ctx):
        pl.semaphore_signal(barrier, inc=1, device_id=(to_sec, to_ctx), device_id_type=MESH)

    @pl.when(has_before)
    def _():
        for ds in range(sections):
            greet(side(ds), before_tail)

    @pl.when(feeds)
    def _():
        for ds in range(sections):
            for dc in range(2):
                greet(side(ds), after_chip + dc)

    for ds, dc in peers:
        greet(side(ds), partner if dc else ctx)
    for dz in range(1, n_z):
        greet(sec, at_z(lax.rem(z + dz, n_z)))
    for dy in range(1, n_y):
        greet(sec, at_y(lax.rem(y + dy, n_y)))

    greeted = (
        len(peers) + n_z - 1 + n_y - 1
        + sections * has_before.astype(jnp.int32) + 2 * sections * feeds.astype(jnp.int32)
    )

    loads = [
        pltpu.make_async_copy(src, dst, in_s.at[n])
        for n, (src, dst) in enumerate(
            ((x_hbm, x_ref), (do_hbm, do_ref), (g_hbm, g_ref), (beta_hbm, beta_ref), (w_hbm, w_ref))
        )
    ]
    for load in loads:
        load.start()

    for load in loads:
        load.wait()

    def halves(ref):
        whole = ref[...].astype(F32)
        low, high = whole[:, :D], whole[:, D:]
        return jnp.where(first, low, high), jnp.where(first, high, low), whole

    x_own, x_oth, x_all = halves(x_ref)
    R[0] = row_sums(x_all * x_all)[0:1]
    d_own, d_oth, _ = halves(do_ref)
    g_own, g_oth, _ = halves(g_ref)
    b0, b1 = as_columns(beta_ref[0:1, :]), as_columns(beta_ref[1:2, :])
    SB[0] = x_oth
    SB[1] = d_oth
    SB[2] = g_oth
    SB[3] = jnp.where(first, b1, b0)
    XB[core, 0] = x_own
    XB[core, 1] = d_own
    XB[core, 2] = g_own
    XB[core, 3] = jnp.where(first, b0, b1)
    RT[0] = x_all[D - 8 :, :D]
    RT[1] = x_all[D - 8 :, D:]
    pl.semaphore_wait(barrier, greeted)

    def rim_copies():
        made = []
        for dc in range(2):
            made.append(copy_to(RT.at[dc], RIMR, rim_s.at[2 * sections + dc], rim_r.at[sections], sec, after_chip + dc))
            for ds in range(sections):
                made.append(copy_to(R.at[0], RIM.at[(sections - ds) % sections], rim_s.at[2 * ds + dc],
                                    rim_r.at[(sections - ds) % sections], side(ds), after_chip + dc))
        return made

    @pl.when(feeds)
    def _():
        for copy in rim_copies():
            copy.start()

    for ds, dc in peers:
        back = ((sections - ds) % sections) * 2 + dc
        go(R.at[0], R.at[back], row_s.at[ds * 2 + dc], row_r.at[back], side(ds), partner if dc else ctx)
    go(SB, XB.at[core], one_s.at[0], one_r.at[0], sec, partner)

    arrives(XB.at[1 - core], one_r.at[0])
    r, c = iota2((D, D), 0), iota2((D, D), 1)
    incl = r >= c
    strict = r > c
    lower = jnp.where(incl, 1.0, 0.0).astype(BF16)
    fins = []
    for b in range(2):
        g = XB[b, 2]
        gh = g.astype(BF16)
        rest = g - gh.astype(F32)
        gm = rest.astype(BF16)
        gl = (rest - gm.astype(F32)).astype(BF16)
        cum = raw_dot(lower, gh, 1, 0) + (raw_dot(lower, gm, 1, 0) + raw_dot(lower, gl, 1, 0))
        mid = cum[D // 2 : D // 2 + 1]
        fin = cum[D - 1 : D]
        EX[b, 0] = jnp.exp(cum - mid)
        EX[b, 1] = jnp.exp(mid - cum)
        EX[b, 2] = jnp.exp(cum)
        EX[b, 3] = jnp.exp(fin - cum)
        fins.append(fin)

    for ds, dc in peers:
        slot = ds * 2 + dc
        arrives(R.at[slot], row_r.at[slot])
    same = R[0]
    other = R[1]
    for ds in range(1, sections):
        same = same + R[2 * ds]
        other = other + R[2 * ds + 1]

    def scale_of(total):
        return 1.0 / jnp.sqrt(total / width_all + 1e-5)

    scale_same = scale_of(same)
    SC[core] = as_columns(scale_same)
    SC[1 - core] = as_columns(scale_of(other))
    for b in range(2):
        NP[8 + D * b : 8 + D * (b + 1), :] = XB[b, 0] * SC[b]

    @pl.when(has_before)
    def _():
        for ds in range(sections):
            arrives(RIM.at[ds], rim_r.at[ds])
        arrives(RIMR, rim_r.at[sections])
        rim_total = RIM[0]
        for ds in range(1, sections):
            rim_total = rim_total + RIM[ds]
        NP[0:8, :] = RIMR[...] * as_columns(scale_of(rim_total))[D - 8 :]

    @pl.when(jnp.logical_not(has_before))
    def _():
        NP[0:8, :] = jnp.zeros((8, D), F32)
        RIMR[...] = jnp.zeros((8, D), F32)

    def tap(j, i):
        both = w_ref[j, i : i + 1, :]
        return jnp.where(first, both[:, :D], both[:, D:])

    taps = [[tap(j, i) for i in range(4)] for j in range(3)]
    shifted = [NP[5 + i : 5 + i + 2 * D, :] for i in range(4)]
    for j in range(3):
        mix = taps[j][0] * shifted[0]
        for i in range(1, 4):
            mix = mix + taps[j][i] * shifted[i]
        gate = 1.0 / (1.0 + jnp.exp(-mix))
        act = mix * gate
        slope = gate * (1.0 + mix * (1.0 - gate))
        if j < 2:
            norm = 1.0 / jnp.sqrt(jnp.sum(act * act, axis=1, keepdims=True) + 1e-6)
            QK[j] = act * norm
            DS[j] = slope * norm
        else:
            QK[j] = act
            DS[j] = slope

    blk = [slice(D * b, D * (b + 1)) for b in range(2)]
    systems, scores = [], []
    for b in range(2):
        q, k = QK[0, blk[b], :], QK[1, blk[b], :]
        kf, kb, qf = k * EX[b, 0], k * EX[b, 1], q * EX[b, 0]
        FB[b, 0:D, :] = kf
        FB[b, D : 2 * D, :] = qf
        FB[b, 2 * D : 3 * D, :] = kb
        both = mm_nt(jnp.concatenate([kf, qf], axis=0), kb)
        systems.append(jnp.where(strict, XB[b, 3] * both[:D], 0.0))
        scores.append(jnp.where(incl, both[D:], 0.0))
    inverses, halved = unit_lower_inverse(systems)
    wus, kes = [], []
    for b in range(2):
        k, v, beta = QK[1, blk[b], :], QK[2, blk[b], :], XB[b, 3]
        ke = k * EX[b, 3]
        wu = mm(inverses[b], jnp.concatenate([beta * k * EX[b, 2], beta * v], axis=1))
        wu = wu - mm(halved[b], wu)
        MAPS[b, 0] = jnp.where(r == c, jnp.exp(fins[b]), 0.0) - mm_tn(ke, wu[:, :D])
        wus.append(wu)
        kes.append(ke)
    t0, t1 = MAPS[0, 0], MAPS[1, 0]
    TS[z] = mm(t1, t0)

    def root_at(j):
        return at_z(2 * j + core)

    def map_send(dj):
        j = lax.rem(rank + dj, roots)
        return copy_to(TS.at[z], TS.at[z], ring_s.at[dj], ring_r.at[z], sec, root_at(j))

    def part_send(dj):
        j = lax.rem(rank + dj, roots)
        return copy_to(VS.at[j], VR.at[z], vec_s.at[dj], vec_r.at[z], sec, root_at(j))

    def all_roots(send, act):
        for dj in sorted(range(1, roots), key=lambda dj: abs(2 * dj - roots)):
            act(send(dj))

        @pl.when(jnp.logical_not(is_root))
        def _():
            act(send(0))

    all_roots(map_send, lambda copy: copy.start())

    for b in range(2):
        q, d_out, sc = QK[0, blk[b], :], XB[b, 1], scores[b]
        w, u = wus[b][:, :D], wus[b][:, D:]
        swu = mm(sc, wus[b])
        qeff = q * EX[b, 2] - swu[:, :D]
        WQ[b, 0:D, :] = w
        WQ[b, D : 2 * D, :] = qeff
        UO[b, 0] = u
        UO[b, 1] = swu[:, D:]
        MAPS[b, 1] = mm_tn(u, kes[b])
        MAPS[b, 2] = mm_tn(d_out, qeff)
    i_pair = mm_nt(MAPS[0, 1], t1) + MAPS[1, 1]
    s_pair = MAPS[0, 2] + mm(MAPS[1, 2], t0)
    for j in range(roots):
        VS[j, 0] = i_pair[j * cols : (j + 1) * cols]
        VS[j, 1] = s_pair[j * cols : (j + 1) * cols]
    all_roots(part_send, lambda copy: copy.start())

    for b in range(2):
        h = mm_tn(scores[b], XB[b, 1])
        zk = mm_tn(inverses[b] - mm(halved[b], inverses[b]), jnp.concatenate([h, kes[b]], axis=1))
        ZK[b, 0] = zk[:, :D]
        ZK[b, 1] = zk[:, D:]
    WS = WQ[1]
    by_start = mm_nt(WS, MAPS[0, 1])
    UO[1, 0] = UO[1, 0] - by_start[:D]
    UO[1, 1] = UO[1, 1] + by_start[D:]
    WQ[1] = mm(WS, t0)
    KS = ZK[0, 1]
    ZK[0, 0] = ZK[0, 0] + mm_nt(KS, MAPS[1, 2])
    ZK[0, 1] = mm_nt(KS, t1)
    DM[:, 0:8, :] = jnp.zeros((3, 8, D), F32)
    DM[:, 8 + 2 * D :, :] = jnp.zeros((3, 8, D), F32)
    eye = jnp.where(r == c, 1.0, 0.0).astype(F32)
    mine = pl.ds(pl.multiple_of(rank * cols, cols), cols)

    def ends_send(dy):
        return copy_to(XY.at[y], XY.at[y], ya_s.at[dy], ya_r.at[n_y - dy], sec, at_y(lax.rem(y + dy, n_y)))

    def total_send(yy, dy):
        slot = PY.at[yy - 1]
        return copy_to(slot, slot, yb_s.at[dy], yb_r.at[yy], sec, at_y(lax.rem(y + dy, n_y)))

    def slice_send(dz):
        to = lax.rem(z + dz, n_z)
        return copy_to(SS.at[to], ST.at[:, mine], sg_s.at[dz], sg_r.at[rank], sec, at_z(to))

    @pl.when(is_root)
    def _():
        VR[z] = VS[rank]
        for dz in range(1, n_z):
            zz = lax.rem(z + dz, n_z)
            arrives(TS.at[zz], ring_r.at[zz])
        PU[0] = eye
        PD[n_z - 1] = eye
        up, down = jnp.transpose(TS[0]), TS[n_z - 1]
        for step in range(1, n_z):
            zu, zd = step, n_z - 1 - step
            PU[zu] = up
            PD[zd] = down
            up = mm_nt(up, TS[zu])
            down = mm(down, TS[zd])
        for yy in range(1, n_y - 1):
            @pl.when(y == yy)
            def _():
                PY[yy - 1] = up
                for dy in sorted(range(1, n_y), key=lambda dy: abs(2 * dy - n_y)):
                    total_send(yy, dy).start()

        for dz in range(1, n_z):
            zz = lax.rem(z + dz, n_z)
            arrives(VR.at[zz], vec_r.at[zz])
        all_up, all_down = VR[n_z - 1, 0], VR[0, 1]
        for step in range(1, n_z):
            zu, zd = n_z - 1 - step, step
            all_up = all_up + mm_nt(VR[zu, 0], PD[zu])
            all_down = all_down + mm_nt(VR[zd, 1], PU[zd])
        XY[y, 0] = all_up
        XY[y, 1] = all_down
        for dy in sorted(range(1, n_y), key=lambda dy: abs(2 * dy - n_y)):
            ends_send(dy).start()

        up, down = VR[0, 0], VR[n_z - 1, 1]
        XU[0] = jnp.zeros((cols, D), F32)
        XD[n_z - 1] = jnp.zeros((cols, D), F32)
        for step in range(1, n_z):
            zu, zd = step, n_z - 1 - step
            XU[zu] = up
            XD[zd] = down
            if step < n_z - 1:
                up = mm_nt(up, TS[zu]) + VR[zu, 0]
                down = mm(down, TS[zd]) + VR[zd, 1]

        for dy in range(1, n_y):
            arrives(XY.at[lax.rem(y + dy, n_y)], ya_r.at[dy])
        for yy in range(1, n_y - 1):
            @pl.when(y != yy)
            def _():
                arrives(PY.at[yy - 1], yb_r.at[yy])
        enter = jnp.where(y > 0, XY[0, 0], 0.0)
        leave = jnp.where(y < n_y - 1, XY[n_y - 1, 1], 0.0)
        for step in range(1, n_y - 1):
            yu, yd = step, n_y - 1 - step
            enter = jnp.where(y > yu, mm(enter, PY[yu - 1]) + XY[yu, 0], enter)
            leave = jnp.where(y < yd, mm_nt(leave, PY[yd - 1]) + XY[yd, 1], leave)

        for dz in sorted(range(n_z), key=lambda dz: (dz == 0, abs(2 * dz - n_z))):
            zz = lax.rem(z + dz, n_z)
            SS[zz, 0] = XU[zz] + mm(enter, PU[zz])
            SS[zz, 1] = XD[zz] + mm(leave, PD[zz])
            if dz:
                slice_send(dz).start()
        ST[:, mine, :] = SS[z]

    for dj in range(roots):
        j = lax.rem(rank + dj, roots)
        theirs = ST.at[:, pl.ds(pl.multiple_of(j * cols, cols), cols)]
        if dj:
            arrives(theirs, sg_r.at[j])
        else:
            @pl.when(jnp.logical_not(is_root))
            def _():
                arrives(theirs, sg_r.at[j])

    starts = [ST[0], None]
    ends = [None, ST[1]]
    starts[1] = mm_nt(starts[0], t0) + MAPS[0, 1]
    ends[0] = mm(ends[1], t1) + MAPS[1, 2]
    for b in range(2):
        q, k = QK[0, blk[b], :], QK[1, blk[b], :]
        beta, d_out = XB[b, 3], XB[b, 1]
        wq = mm_nt(WQ[b], starts[0])
        fresh = UO[b, 0] - wq[:D]
        OB[b] = UO[b, 1] + wq[D:]
        zeta = ZK[b, 0] + mm_nt(ZK[b, 1], ends[1])
        pair = mm_nt(jnp.concatenate([d_out, zeta], axis=0), fresh)
        d_sc = jnp.where(incl, pair[:D], 0.0)
        d_p = beta * jnp.where(strict, -pair[D:], 0.0)
        dz_s = mm(jnp.concatenate([d_out, zeta], axis=0), starts[b])
        f_g = mm(fresh, ends[b])
        by_kb = mm(jnp.concatenate([d_sc, d_p], axis=0), FB[b, 2 * D : 3 * D, :])
        d_kb = mm_tn(jnp.concatenate([d_p, d_sc], axis=0), FB[b, 0 : 2 * D, :])
        dq = EX[b, 2] * dz_s[:D] + EX[b, 0] * by_kb[:D]
        dk = EX[b, 3] * f_g - beta * EX[b, 2] * dz_s[D:] + EX[b, 0] * by_kb[D:] + EX[b, 1] * d_kb
        for j, (unit, grad) in enumerate(((q, dq), (k, dk))):
            along = jnp.sum(unit * grad, axis=1, keepdims=True)
            DM[j, 8 + D * b : 8 + D * (b + 1), :] = (grad - unit * along) * DS[j, blk[b], :]
        DM[2, 8 + D * b : 8 + D * (b + 1), :] = beta * zeta * DS[2, blk[b], :]
    go(OB.at[1 - core], OR, one_s.at[1], one_r.at[1], sec, partner)

    d_norm = jnp.zeros((2 * D + 8, D), F32)
    for j in range(3):
        for i in range(4):
            d_norm = d_norm + taps[j][i] * DM[j, 3 - i : 3 - i + 2 * D + 8, :]
    GB[0] = d_norm[8 : 8 + D]
    GB[1] = d_norm[8 + D :]
    GRIM[2] = d_norm[:8]
    TB[2] = row_sums(jnp.concatenate([jnp.zeros((D - 8, D), F32), d_norm[:8] * RIMR[...]], axis=0))[0:1]
    TB[0] = row_sums(d_norm[8 : 8 + D] * XB[0, 0])[0:1]
    TB[1] = row_sums(d_norm[8 + D :] * XB[1, 0])[0:1]

    go(GB.at[1 - core], GR, one_s.at[2], one_r.at[2], sec, partner)

    def rim_back_copies():
        made = [copy_to(GRIM.at[2], GRIM.at[core], rim2_s.at[sections], rim2_r.at[2 * sections + core], sec, before_tail)]
        for ds in range(sections):
            slot = 2 * ((sections - ds) % sections) + core
            made.append(copy_to(TB.at[2], RIM2.at[slot], rim2_s.at[ds], rim2_r.at[slot], side(ds), before_tail))
        return made

    @pl.when(has_before)
    def _():
        for copy in rim_back_copies():
            copy.start()

    for ds, dc in peers:
        back = ((sections - ds) % sections) * 2 + dc
        go(TB.at[1 - core if dc else core], R2.at[back], row2_s.at[ds * 2 + dc], row2_r.at[back],
           side(ds), partner if dc else ctx)


    def joined(own, oth):
        return jnp.concatenate([jnp.where(first, own, oth), jnp.where(first, oth, own)], axis=1)

    arrives(OR, one_r.at[1])
    x_wide = x_ref[...].astype(F32)
    both_ref[0] = (x_wide + joined(OB[core], OR[...])).astype(BF16)
    arrives(GR, one_r.at[2])
    scale = SC[core]
    wide_scale = jnp.concatenate([scale, scale], axis=1)
    FIN[...] = do_ref[...].astype(F32) + joined(GB[core], GR[...]) * wide_scale

    for ds, dc in peers:
        slot = ds * 2 + dc
        arrives(R2.at[slot], row2_r.at[slot])
    inner = TB[core]
    for slot in range(1, 2 * sections):
        inner = inner + R2[slot]
    RT2[0] = inner

    @pl.when(feeds)
    def _():
        for slot in range(2 * sections):
            arrives(RIM2.at[slot], rim2_r.at[slot])
        for n in range(2):
            arrives(GRIM.at[n], rim2_r.at[2 * sections + n])
        total = RT2[0]
        for slot in range(2 * sections):
            total = total + RIM2[slot]
        RT2[0] = total
        late = jnp.concatenate([GRIM[0], GRIM[1]], axis=1)
        FIN[D - 8 :, :] = FIN[D - 8 :, :] + late * jnp.concatenate([SC[core, D - 8 :, :]] * 2, axis=1)

    coef = as_columns(scale_same * scale_same * scale_same * RT2[0] / width_all)
    both_ref[1] = (FIN[...] - x_wide * jnp.concatenate([coef, coef], axis=1)).astype(BF16)

    for copy in sent:
        copy.wait_send()

    @pl.when(feeds)
    def _():
        for copy in rim_copies():
            copy.wait_send()

    @pl.when(has_before)
    def _():
        for copy in rim_back_copies():
            copy.wait_send()

    all_roots(map_send, lambda copy: copy.wait_send())
    all_roots(part_send, lambda copy: copy.wait_send())

    @pl.when(is_root)
    def _():
        for dy in range(1, n_y):
            ends_send(dy).wait_send()
        for dz in range(1, n_z):
            slice_send(dz).wait_send()
        for yy in range(1, n_y - 1):
            @pl.when(y == yy)
            def _():
                for dy in range(1, n_y):
                    total_send(yy, dy).wait_send()


def solution(mesh):
    sections, n_ctx = mesh.shape["section"], mesh.shape["ctx"]
    n_y, n_z = (4, 8) if n_ctx == 64 else (2, n_ctx // 4)
    roots = n_z // 2
    cols = D // roots
    dma = lambda n: pltpu.SemaphoreType.DMA((n,))

    def shards(inputs, out_grads, conv_weight, log_decay, beta):
        width_all = float(inputs.shape[1] * sections)
        v = lambda *s: pltpu.VMEM(s, F32)
        scratch = [
            pltpu.VMEM((D, 2 * D), BF16), pltpu.VMEM((D, 2 * D), BF16), v(D, 2 * D), v(2, D), v(3, 4, 2 * D),
            v(4, D, D), v(2, 4, D, D), v(2 * sections, 1, D), v(2 * sections, 1, D), v(3, 1, D),
            v(2 * D + 8, D), v(sections, 1, D), v(8, D), v(2, D, D), v(3, 8, D), v(2 * sections, 1, D), v(2, 8, D),
            v(3, 2 * D, D), v(3, 2 * D, D), v(2, 4, D, D), v(2, 3 * D, D), v(2, 2 * D, D), v(2, 2, D, D),
            v(2, 2, D, D), v(2, 3, D, D), v(n_z, D, D), v(roots, 2, cols, D), v(n_z, 2, cols, D),
            v(n_z, D, D), v(n_z, D, D), v(n_z, cols, D), v(n_z, cols, D), v(n_y, 2, cols, D),
            v(max(n_y - 2, 1), D, D), v(n_z, 2, cols, D), v(2, D, D), v(3, 2 * D + 16, D),
            v(2, D, D), v(D, D), v(2, D, D), v(D, D), v(D, 2 * D), v(1, 1, D),
            dma(5), dma(2 * sections), dma(2 * sections), dma(2 * sections + 2), dma(sections + 1),
            dma(2 * sections), dma(2 * sections), dma(sections + 1), dma(2 * sections + 2), dma(3), dma(3),
            dma(roots), dma(n_z), dma(roots), dma(n_z), dma(n_z), dma(roots),
            dma(n_y), dma(n_y), dma(n_y), dma(n_y),
        ]
        vm = pl.BlockSpec(memory_space=pltpu.VMEM)
        hbm = pl.BlockSpec(memory_space=pltpu.MemorySpace.HBM)
        both = pl.pallas_call(
            functools.partial(kernel, (sections, n_y, n_z, width_all)),
            out_shape=jax.ShapeDtypeStruct((2,) + inputs.shape, BF16),
            in_specs=[hbm] * 5,
            out_specs=vm,
            scratch_shapes=scratch,
            compiler_params=pltpu.CompilerParams(
                collective_id=0, has_side_effects=True, vmem_limit_bytes=40 * 2**20
            ),
        )(*[pltpu.with_memory_space_constraint(a, pltpu.MemorySpace.HBM) for a in (inputs, out_grads, log_decay, beta.T, conv_weight)])
        return both[0], both[1]

    spec = P("ctx", "section")
    return jax.shard_map(
        shards, mesh=mesh, in_specs=(spec, spec, P(None, None, "section"), spec, spec),
        out_specs=(spec, spec), check_vma=False,
    )
```
